128 devices in a mesh: gx: 8 (over y, core), gy: 4 (over z), gz: 4 (over x).
Axes of the slice: x: 4, y: 4, z: 4, core: 2. Of those that a mesh axis runs over, the one named last changes fastest.
Arguments:
- displacement: float32 [3, 64, 512, 512], P(None, 'gx', 'gy', 'gz'), may hold values from -0.9 to 0.9
- density: float32 [64, 512, 512], P('gx', 'gy', 'gz'), may hold values from 0.05 to 1
- element_stiffness: float32 [24, 24], replicated, may hold values from -0.3 to 8.3, as said below
Outputs:
- design_sensitivity: float32 [64, 512, 512], P('gx', 'gy', 'gz')
The draws below stay inside these ranges and needn't reach their ends.
Inputs may be any that keep to these rules, and one draw needn't show every extreme that they name: `element_stiffness`: symmetric.
All inputs are finite; a program needn't handle non-finite values.
Results may differ from the reference program's by a relative error of at most 0.00027.
Values sent between devices are 32-bit elements; how exact they have to be, the bound alone decides.
No kernel may reach another device: no remote copies, remote signals or barrier semaphores. Data moves between devices by JAX's collectives and lax.ppermute only.
A program may use at most 128 MiB of HBM per device.

```python
import jax
import jax.numpy as jnp
from jax import lax

LEVELS = 3
CYCLES = 2
PRE_SWEEPS = 2
POST_SWEEPS = 2
COARSE_SWEEPS = 8
FILTER_COEF = 36
NX = 64
NY = 512
NZ = 512


def draw_element_stiffness(key, part):
    random_part = jax.random.uniform(key, (24, 24), jnp.float32, -0.3, 0.3)
    symmetric = 0.5 * (random_part + random_part.T)
    return symmetric + 8.0 * jnp.eye(24, dtype=jnp.float32)


def levels(key, extent, pieces, low, high):
    def one(dim, blocks):
        draws = jax.random.uniform(jax.random.fold_in(jax.random.fold_in(key, 6), dim), (blocks,), jnp.float32, low / len(pieces), high / len(pieces))
        return jnp.repeat(jnp.exp(draws), extent[dim] // blocks).reshape((-1,) + (1,) * (len(extent) - dim - 1))

    gain = one(*pieces[0])
    for cut in pieces[1:]:
        gain = gain * one(*cut)
    return gain


def normal_values(own_key, dims, width, reach, cuts=(), kind=jnp.bfloat16):
    result = width * jax.random.normal(own_key, dims, jnp.float32)
    if cuts:
        result = result * levels(own_key, dims, cuts, -0.22, 0.18)
    return jnp.clip(result, -reach, reach).astype(kind)


def setup_inputs(seed: int = 0) -> dict:
    seeds = jax.random.split(jax.random.key(seed), 4)
    displacement = normal_values(seeds[0], (3, NX, NY, NZ), 0.15, 0.9, ((1, 8), (2, 4), (3, 4)), jnp.float32)
    density = jnp.clip(0.05 + 0.95 * jax.random.uniform(seeds[1], (NX, NY, NZ), jnp.float32) ** levels(seeds[1], (NX, NY, NZ), ((0, 8), (1, 4), (2, 4)), -0.2, 0.2), 0.05, 1.0)
    element_stiffness = draw_element_stiffness(jax.random.fold_in(seeds[3], 71), 0)
    return dict(displacement=displacement, density=density, element_stiffness=element_stiffness)


DAMPING = 0.95


def beside_sum(padded):
    total = padded[2:, 1:-1, 1:-1] + padded[:-2, 1:-1, 1:-1]
    total = total + padded[1:-1, 2:, 1:-1] + padded[1:-1, :-2, 1:-1]
    total = total + padded[1:-1, 1:-1, 2:] + padded[1:-1, 1:-1, :-2]
    return total


def neighbour_counts(grid_shape):
    counts = jnp.zeros(grid_shape, jnp.float32)
    for axis_pos in range(3):
        places = lax.iota(jnp.int32, grid_shape[axis_pos])
        view_shape = [1, 1, 1]
        view_shape[axis_pos] = grid_shape[axis_pos]
        places = places.reshape(view_shape)
        counts = counts + (places > 0).astype(jnp.float32) + (places < grid_shape[axis_pos] - 1).astype(jnp.float32)
    return counts


def relax_once(iterate, source, diagonal, coefficient):
    applied = diagonal * iterate - coefficient * beside_sum(jnp.pad(iterate, 1))
    return iterate + DAMPING * (source - applied) / diagonal


def restrict_mean(residual):
    size_x, size_y, size_z = residual.shape
    return residual.reshape(size_x // 2, 2, size_y // 2, 2, size_z // 2, 2).mean(axis=(1, 3, 5))


def prolong(coarse):
    size_x, size_y, size_z = coarse.shape
    spread = jnp.broadcast_to(coarse[:, None, :, None, :, None], (size_x, 2, size_y, 2, size_z, 2))
    return spread.reshape(2 * size_x, 2 * size_y, 2 * size_z)


def vee_cycle(source, iterate, level_index):
    coefficient = FILTER_COEF / 4.0 ** level_index
    diagonal = 1.0 + coefficient * neighbour_counts(source.shape)
    if level_index == LEVELS - 1:
        iterate = jnp.zeros(source.shape, jnp.float32)
        for sweep_index in range(COARSE_SWEEPS):
            iterate = relax_once(iterate, source, diagonal, coefficient)
        return iterate
    for sweep_index in range(PRE_SWEEPS):
        iterate = relax_once(iterate, source, diagonal, coefficient)
    applied = diagonal * iterate - coefficient * beside_sum(jnp.pad(iterate, 1))
    residual = source - applied
    coarse_source = restrict_mean(residual)
    correction = vee_cycle(coarse_source, jnp.zeros(coarse_source.shape, jnp.float32), level_index + 1)
    iterate = iterate + prolong(correction)
    for sweep_index in range(POST_SWEEPS):
        iterate = relax_once(iterate, source, diagonal, coefficient)
    return iterate


def element_energy(extended, element_stiffness, cells_y, cells_z, block_index):
    window = lax.dynamic_slice_in_dim(extended, block_index * 4, 5, 1)
    corners = [window[:, shift_x:shift_x + 4, shift_y:shift_y + cells_y, shift_z:shift_z + cells_z]
               for shift_z in (0, 1) for shift_y in (0, 1) for shift_x in (0, 1)]
    stacked = jnp.concatenate(corners, axis=0).reshape(24, -1)
    pushed = jnp.dot(element_stiffness, stacked, precision=lax.Precision.HIGHEST)
    return jnp.sum(stacked * pushed, axis=0).reshape(4, cells_y, cells_z)


def reference(displacement, density, element_stiffness):
    cells_x, cells_y, cells_z = density.shape
    extended = jnp.pad(displacement, ((0, 0), (0, 1), (0, 1), (0, 1)))
    energy = lax.map(lambda block_index: element_energy(extended, element_stiffness, cells_y, cells_z, block_index),
                     jnp.arange(cells_x // 4, dtype=jnp.int32))
    energy = energy.reshape(density.shape)
    physical_sens = -3.0 * density * density * energy
    iterate = jnp.zeros(density.shape, jnp.float32)
    for cycle_index in range(CYCLES):
        iterate = vee_cycle(physical_sens, iterate, 0)
    return iterate
```

```python
import jax
import jax.numpy as jnp
from jax import lax
from jax.experimental import pallas as pl
from jax.experimental.pallas import tpu as pltpu
from jax.sharding import PartitionSpec as P

FILTER_COEF = 36.0
DAMPING = 0.95
S0 = FILTER_COEF
S1 = FILTER_COEF / 4.0
S2 = FILTER_COEF / 16.0
KEEP = 1.0 - DAMPING
HIGH = lax.Precision.HIGHEST
F32 = jnp.float32

PL0, R0 = 24, 160
PL1, R1 = 42, 128
PL2, R2 = 18, 72


def iota(shape, dim):
    return lax.broadcasted_iota(jnp.int32, shape, dim)


def next_lane(value):
    return pltpu.roll(value, 127, 1)


def prev_lane(value):
    return pltpu.roll(value, 1, 1)


def axis_count(place, total):
    return jnp.where(place > 0, 1.0, 0.0) + jnp.where(place < total - 1, 1.0, 0.0)


def make_tables(weight, diag, rows, row_off, lane_place, lane_ok, base_y, base_z, total, scale):
    y = iota((rows, 128), 0) - row_off + base_y
    z = lane_place + base_z
    inside = lane_ok & (y >= 0) & (y < total) & (z >= 0) & (z < total)
    count = axis_count(y, total) + axis_count(z, total)
    weight[0] = jnp.zeros((rows, 128), F32)
    for i in (1, 2):
        value = 1.0 + scale * (count + float(i))
        weight[i] = jnp.where(inside, DAMPING / value, 0.0)
        if diag is not None:
            diag[i] = value


def x_index(place, total):
    edge = (place == 0) | (place == total - 1)
    out = (place < 0) | (place >= total)
    return jnp.where(out, 0, jnp.where(edge, 1, 2))


def lanes_main():
    return iota((R0, 128), 1)


def level0_tables(pos, wm, ws, dm):
    lane = lanes_main()
    yes = lane >= 0
    make_tables(wm, dm, R0, 16, lane, yes, pos[1] * 128, pos[2] * 128, 512, S0)
    side = jnp.where(lane < 64, lane + 128, lane - 128)
    ok = (lane < 8) | (lane >= 120)
    make_tables(ws, None, R0, 16, side, ok, pos[1] * 128, pos[2] * 128, 512, S0)


def level0_sweep(pos, src, dst, fm, fs, wm, ws, first, last, side):
    lane = iota((48, 128), 1)

    def body(p, carry):
        i = x_index(pos[0] * 8 + p - 8, 64)
        for r in range(8, 152, 48):
            rows = pl.ds(r, 48)
            up, dn = pl.ds(r - 1, 48), pl.ds(r + 1, 48)
            m, s = src[0][p, rows], src[1][p, rows]
            mr, sr, ml, sl = next_lane(m), next_lane(s), prev_lane(m), prev_lane(s)
            tot = src[0][p - 1, rows] + src[0][p + 1, rows] + src[0][p, up] + src[0][p, dn]
            tot = tot + jnp.where(lane == 127, sr, mr) + jnp.where(lane == 0, sl, ml)
            dst[0][p, rows] = KEEP * m + wm[i, rows] * (fm[p, rows] + S0 * tot)
            if side:
                tot = src[1][p - 1, rows] + src[1][p + 1, rows] + src[1][p, up] + src[1][p, dn]
                tot = tot + jnp.where(lane == 127, mr, sr) + jnp.where(lane == 0, ml, sl)
                dst[1][p, rows] = KEEP * s + ws[i, rows] * (fs[p, rows] + S0 * tot)
        return carry

    lax.fori_loop(first, last + 1, body, 0)


def restrict_matrix(size):
    src, dst = iota((size, 128), 0), iota((size, 128), 1)
    col = jnp.where(dst < 64, dst, dst - 64)
    ok = (dst < 86) | (dst >= 106)
    return jnp.where(ok & (src // 2 == col), 0.125, 0.0)


def level0_restrict(pos, src, fm, dm, tmp, out):
    lane = iota((64, 128), 1)
    matrix = restrict_matrix(128)

    def body(k, carry):
        for r in (0, 64):
            both = None
            for q in (0, 1):
                p = 8 + 2 * k + q
                i = x_index(pos[0] * 8 + p - 8, 64)
                rows = pl.ds(r + 16, 64)
                m, s = src[0][p, rows], src[1][p, rows]
                tot = src[0][p - 1, rows] + src[0][p + 1, rows]
                tot = tot + src[0][p, pl.ds(r + 15, 64)] + src[0][p, pl.ds(r + 17, 64)]
                tot = tot + jnp.where(lane == 127, next_lane(s), next_lane(m))
                tot = tot + jnp.where(lane == 0, prev_lane(s), prev_lane(m))
                res = fm[p, rows] + S0 * tot - dm[i, rows] * m
                both = res if both is None else both + res
            tmp[pl.ds(r, 64)] = both
        pair = tmp[pl.ds(0, 64, stride=2)] + tmp[pl.ds(1, 64, stride=2)]
        out[k] = jnp.dot(pair, matrix, precision=HIGH, preferred_element_type=F32)
        return carry

    lax.fori_loop(0, 4, body, 0)


def plane_sweep(src, dst, f, w, first, last, x_off, total, rows, scale):
    def body(p, carry):
        i = x_index(p - x_off, total)
        n = rows - 16
        mid = pl.ds(8, n)
        m = src[p, mid]
        tot = src[p - 1, mid] + src[p + 1, mid] + src[p, pl.ds(7, n)] + src[p, pl.ds(9, n)]
        tot = tot + next_lane(m) + prev_lane(m)
        dst[p, mid] = KEEP * m + w[i, mid] * (f[p, mid] + scale * tot)
        return carry

    lax.fori_loop(first, last + 1, body, 0)


def coarse_levels(pos, blocks, f1, va, vb, f2, a2, b2, w1, d1, w2, tmp):
    gx = pos[0]
    lane1 = iota((R1, 128), 1)
    z1 = jnp.where(lane1 < 96, lane1, lane1 - 128)
    ok1 = (lane1 < 86) | (lane1 >= 106)
    make_tables(w1, d1, R1, 32, z1, ok1, pos[1] * 64, pos[2] * 64, 256, S1)
    lane2 = iota((R2, 128), 1)
    z2 = jnp.where(lane2 < 64, lane2, lane2 - 128)
    ok2 = (lane2 < 43) | (lane2 >= 117)
    make_tables(w2, None, R2, 20, z2, ok2, pos[1] * 32, pos[2] * 32, 128, S2)

    zero = jnp.zeros((R1, 128), F32)
    for p in list(range(0, 5)) + list(range(37, 42)):
        f1[p] = zero
        va[p] = zero
        vb[p] = zero
    for p in range(5, 37):
        for ref in (va, vb):
            ref[p, pl.ds(0, 8)] = jnp.zeros((8, 128), F32)
            ref[p, pl.ds(120, 8)] = jnp.zeros((8, 128), F32)
    for ref in (a2, b2):
        for p in (0, 17):
            ref[p] = jnp.zeros((R2, 128), F32)
        for p in range(1, 17):
            ref[p, pl.ds(0, 8)] = jnp.zeros((8, 128), F32)
            ref[p, pl.ds(64, 8)] = jnp.zeros((8, 128), F32)

    for m in range(4):
        for q in range(2):
            block = blocks[2 * m + q]
            own = gx if q == 0 else jnp.bitwise_xor(gx, 1)
            place = jnp.bitwise_and(own + 8 - 2 * m, 7)
            for j in range(4):
                p = 5 + 4 * place + j
                i = x_index(4 * place + j, 32)
                value = block[j]
                f1[p, pl.ds(8, 112)] = value
                va[p, pl.ds(8, 112)] = w1[i, pl.ds(8, 112)] * value

    plane_sweep(va, vb, f1, w1, 5, 36, 5, 32, R1, S1)

    src, dst = iota((128, 128), 0), iota((128, 128), 1)
    zs1 = jnp.where(src < 96, src, src - 128)
    ks1 = (src < 86) | (src >= 106)
    zd2 = jnp.where(dst < 64, dst, dst - 128)
    kd2 = (dst < 43) | (dst >= 117)
    down = jnp.where(ks1 & kd2 & (lax.shift_right_arithmetic(zs1, 1) == zd2), 0.125, 0.0)
    zs2 = jnp.where(src < 64, src, src - 128)
    ks2 = (src < 43) | (src >= 117)
    zd1 = jnp.where(dst < 96, dst, dst - 128)
    kd1 = (dst < 86) | (dst >= 106)
    up = jnp.where(ks2 & kd1 & (lax.shift_right_arithmetic(zd1, 1) == zs2), 1.0, 0.0)

    def restrict(k, carry):
        both = None
        mid = pl.ds(8, 112)
        for q in (0, 1):
            p = 5 + 2 * k + q
            i = x_index(p - 5, 32)
            m = vb[p, mid]
            tot = vb[p - 1, mid] + vb[p + 1, mid] + vb[p, pl.ds(7, 112)] + vb[p, pl.ds(9, 112)]
            tot = tot + next_lane(m) + prev_lane(m)
            res = f1[p, mid] + S1 * tot - d1[i, mid] * m
            both = res if both is None else both + res
        tmp[pl.ds(0, 112)] = both
        pair = tmp[pl.ds(0, 56, stride=2)] + tmp[pl.ds(1, 56, stride=2)]
        value = jnp.dot(pair, down, precision=HIGH, preferred_element_type=F32)
        f2[1 + k, pl.ds(8, 56)] = value
        a2[1 + k, pl.ds(8, 56)] = w2[x_index(k, 16), pl.ds(8, 56)] * value
        return carry

    lax.fori_loop(0, 16, restrict, 0)

    src2, dst2 = a2, b2
    for _ in range(7):
        plane_sweep(src2, dst2, f2, w2, 1, 16, 1, 16, R2, S2)
        src2, dst2 = dst2, src2

    def prolong(k, carry):
        e = jnp.dot(src2[1 + k, pl.ds(8, 56)], up, precision=HIGH, preferred_element_type=F32)
        for q in (0, 1):
            for h in (0, 1):
                rows = pl.ds(8 + h, 56, stride=2)
                vb[5 + 2 * k + q, rows] = vb[5 + 2 * k + q, rows] + e
        return carry

    lax.fori_loop(0, 16, prolong, 0)
    plane_sweep(vb, va, f1, w1, 4 * gx + 1, 4 * gx + 12, 5, 32, R1, S1)
    plane_sweep(va, vb, f1, w1, 4 * gx + 2, 4 * gx + 11, 5, 32, R1, S1)


def level0_prolong(pos, e1, old, new, first, last):
    src, dst = iota((128, 256), 0), iota((128, 256), 1)
    zs = jnp.where(src < 96, src, src - 128)
    side = dst - 128
    zd = jnp.where(dst < 128, dst, jnp.where(side < 64, side + 128, side - 128))
    ok = (dst < 128) | (side < 8) | (side >= 120)
    up = jnp.where(ok & (lax.shift_right_arithmetic(zd, 1) == zs), 1.0, 0.0)

    def body(k, carry):
        e = e1[4 * pos[0] + 1 + k, pl.ds(28, 72)]
        e = jnp.dot(e, up, precision=HIGH, preferred_element_type=F32)
        for q in (0, 1):
            p = 2 * k + q
            for h in (0, 1):
                rows = pl.ds(8 + h, 72, stride=2)
                new[0][p, rows] = old[0][p, rows] + e[:, :128]
                new[1][p, rows] = old[1][p, rows] + e[:, 128:]
        return carry

    lax.fori_loop(first // 2, last // 2 + 1, body, 0)


def zero_pads(refs, first, last):
    zero = jnp.zeros((8, 128), F32)
    for ref in refs:
        for p in range(first, last + 1):
            ref[p, pl.ds(0, 8)] = zero
            ref[p, pl.ds(152, 8)] = zero


def rim_kernel(u, cols, rows):
    lane = iota((128, 128), 1)
    acc = jnp.zeros((128, 128), F32)
    for d in range(3):
        for x in range(8):
            k = 8 * d + x
            value = u[d, x]
            acc = jnp.where(lane == k, pltpu.roll(value, k, 1) if k else value, acc)
            rows[pl.ds(k, 1)] = u[d, x, pl.ds(0, 1)]
    cols[...] = acc


def energy_kernel(pos, stiff, u, xface, yrim, zrim, xrim, rho, f, pack, u0, u1, table):
    gx, gy, gz = pos[0], pos[1], pos[2]
    keep_x = jnp.where(gx < 7, 1.0, 0.0)
    keep_y = jnp.where(gy < 3, 1.0, 0.0)
    keep_z = jnp.where(gz < 3, 1.0, 0.0)
    n = 0
    for i in range(24):
        for j in range(i, 24):
            value = stiff[i, j] if i == j else stiff[i, j] + stiff[j, i]
            table[n] = jnp.full((8, 128), value, F32)
            n += 1
    lane = iota((128, 128), 1)
    lane8 = iota((8, 128), 1)
    for d in range(3):
        for x in range(9):
            k = 8 * d + x
            if x < 8:
                body = u[d, x]
                col = zrim[...]
                row = yrim[pl.ds(k, 1)]
                corner = yrim[pl.ds(24, 8)]
            else:
                k = 8 * d
                body = xface[d] * keep_x
                col = xrim[pl.ds(32, 128)] * keep_x
                row = xrim[pl.ds(k, 1)] * keep_x
                corner = xrim[pl.ds(24, 8)] * keep_x
            row = jnp.broadcast_to(row, (8, 128)) * keep_y
            corner = jnp.broadcast_to(corner[0:1], (8, 128)) * (keep_y * keep_z)
            q = 9 * d + x
            u0[q, pl.ds(0, 128)] = body
            u0[q, pl.ds(128, 8)] = row
            u1[q, pl.ds(0, 128)] = jnp.where(
                lane == 127, pltpu.roll(col, 127 - k, 1) * keep_z, next_lane(body))
            u1[q, pl.ds(128, 8)] = jnp.where(
                lane8 == 127, pltpu.roll(corner, 127 - k, 1), next_lane(row))

    def chunk(c, carry):
        x, y = c // 16, pl.multiple_of((c % 16) * 8, 8)
        val = []
        for c_z in (0, 1):
            for b in (0, 1):
                for a in (0, 1):
                    for d in range(3):
                        ref = u1 if c_z else u0
                        val.append(ref[9 * d + x + a, pl.ds(y + b, 8)])
        energy = None
        n = 0
        for i in range(24):
            acc = None
            for j in range(i, 24):
                term = table[n] * val[j]
                acc = term if acc is None else acc + term
                n += 1
            acc = acc * val[i]
            energy = acc if energy is None else energy + acc
        r = rho[x, pl.ds(y, 8)]
        f[x, pl.ds(y, 8)] = -3.0 * r * r * energy
        return carry

    lax.fori_loop(0, 128, chunk, 0)
    acc = jnp.zeros((128, 128), F32)
    for x in range(8):
        value = f[x]
        low = pltpu.roll(value, 8 * x, 1) if x else value
        acc = jnp.where((lane >= 8 * x) & (lane < 8 * x + 8), low, acc)
        high = pltpu.roll(value, (8 * x + 72) % 128, 1)
        acc = jnp.where((lane >= 64 + 8 * x) & (lane < 72 + 8 * x), high, acc)
    pack[...] = acc


def spread(value, x):
    lane = iota(value.shape, 1)
    low = pltpu.roll(value, (128 - 8 * x) % 128, 1) if x else value
    high = pltpu.roll(value, (56 - 8 * x) % 128, 1)
    return jnp.where(lane < 64, low, high)


def first_kernel(pos, fl, fc, fr, hl, hc, hr, fm, fs, vm, vs, out, am, as_, wm, ws, dm, tmp):
    level0_tables(pos, wm, ws, dm)
    zero_pads((fm, fs, vm, vs, am, as_), 0, 23)
    for b, (blk, halo) in enumerate(((fl, hl), (fc, hc), (fr, hr))):
        for x in range(8):
            p = 8 * b + x
            i = x_index(pos[0] * 8 + p - 8, 64)
            parts = (
                (8, 8, halo[pl.ds(8 * x, 8)], spread(halo[pl.ds(64, 8)], x)),
                (16, 128, blk[x], spread(halo[pl.ds(144, 128)], x)),
                (144, 8, halo[pl.ds(72 + 8 * x, 8)], spread(halo[pl.ds(136, 8)], x)),
            )
            for start, size, main, side in parts:
                rows = pl.ds(start, size)
                fm[p, rows] = main
                fs[p, rows] = side
                am[p, rows] = wm[i, rows] * main
                as_[p, rows] = ws[i, rows] * side
    level0_sweep(pos, (am, as_), (vm, vs), fm, fs, wm, ws, 2, 21, True)
    level0_restrict(pos, (vm, vs), fm, dm, tmp, out)


def middle_kernel(pos, *refs):
    blocks = refs[:8]
    fm, fs, vm, vs, om, os_, out = refs[8:15]
    am, as_, bm, bs, wm, ws, dm, f1, va, vb, f2, a2, b2, w1, d1, w2, tmp = refs[15:]
    coarse_levels(pos, blocks, f1, va, vb, f2, a2, b2, w1, d1, w2, tmp)
    level0_tables(pos, wm, ws, dm)
    zero_pads((am, as_, bm, bs, om, os_), 0, 23)
    level0_prolong(pos, vb, (vm, vs), (am, as_), 2, 21)
    level0_sweep(pos, (am, as_), (bm, bs), fm, fs, wm, ws, 3, 20, True)
    level0_sweep(pos, (bm, bs), (am, as_), fm, fs, wm, ws, 4, 19, True)
    level0_sweep(pos, (am, as_), (bm, bs), fm, fs, wm, ws, 5, 18, True)
    level0_sweep(pos, (bm, bs), (om, os_), fm, fs, wm, ws, 6, 17, True)
    level0_restrict(pos, (om, os_), fm, dm, tmp, out)


def last_kernel(pos, *refs):
    blocks = refs[:8]
    fm, fs, vm, vs, out = refs[8:13]
    am, as_, bm, bs, wm, ws, f1, va, vb, f2, a2, b2, w1, d1, w2, tmp = refs[13:]
    coarse_levels(pos, blocks, f1, va, vb, f2, a2, b2, w1, d1, w2, tmp)
    level0_tables(pos, wm, ws, None)
    zero_pads((am, as_, bm, bs), 0, 23)
    level0_prolong(pos, vb, (vm, vs), (am, as_), 6, 17)
    level0_sweep(pos, (am, as_), (bm, bs), fm, fs, wm, ws, 7, 16, True)
    level0_sweep(pos, (bm, bs), (am, as_), fm, fs, wm, ws, 8, 15, False)
    for x in range(8):
        out[x] = am[8 + x, pl.ds(16, 128)]


SMEM = pl.BlockSpec(memory_space=pltpu.SMEM)
VM = pl.BlockSpec(memory_space=pltpu.VMEM)


def shape(*dims):
    return jax.ShapeDtypeStruct(dims, F32)


def vmem(*dims):
    return pltpu.VMEM(dims, F32)


def call(kernel, outs, scratch, scalars, args, name):
    specs = [SMEM] * scalars + [VM] * (len(args) - scalars)
    return pl.pallas_call(
        kernel,
        out_shape=outs,
        in_specs=specs,
        out_specs=[VM] * len(outs),
        scratch_shapes=scratch,
        compiler_params=pltpu.CompilerParams(vmem_limit_bytes=48 << 20),
        name=name,
    )(*args)


def shifted(value, axis, step):
    size = lax.axis_size(axis)
    return lax.ppermute(value, axis, [(i, (i + step) % size) for i in range(size)])


def swapped(value):
    return lax.ppermute(value, "gx", [(i, i ^ 1) for i in range(lax.axis_size("gx"))])


COARSE_SCRATCH = [
    vmem(PL1, R1, 128), vmem(PL1, R1, 128), vmem(PL1, R1, 128),
    vmem(PL2, R2, 128), vmem(PL2, R2, 128), vmem(PL2, R2, 128),
    vmem(3, R1, 128), vmem(3, R1, 128), vmem(3, R2, 128), vmem(128, 128),
]
TABLE = vmem(3, R0, 128)
WIDE = vmem(PL0, R0, 128)


def gather_level1(own):
    lane = lax.broadcasted_iota(jnp.int32, own.shape, 2)
    right, left = shifted(own, "gz", -1), shifted(own, "gz", 1)
    own = jnp.where(lane < 64, own, jnp.where(lane < 96, right, left))
    low, high = shifted(own[:, 40:], "gy", 1), shifted(own[:, :24], "gy", -1)
    own = jnp.concatenate([low, own, high], axis=1)
    blocks = []
    for m in range(4):
        part = own if m == 0 else shifted(own, "gx", 2 * m)
        blocks += [part, swapped(part)]
    return blocks


def per_device(u, rho, stiff):
    pos = jnp.stack([lax.axis_index(a) for a in ("gx", "gy", "gz")]).astype(jnp.int32)
    cols, rows = call(rim_kernel, [shape(128, 128), shape(24, 128)], [], 0, [u], "rims")
    xface = shifted(u[:, 0], "gx", -1)
    zrim = shifted(cols, "gz", -1)
    yrim = shifted(jnp.concatenate([rows, zrim[:8]], axis=0), "gy", -1)
    xrim = shifted(jnp.concatenate([yrim, zrim], axis=0), "gx", -1)
    f, pack = call(
        energy_kernel, [shape(8, 128, 128), shape(128, 128)],
        [vmem(27, 136, 128), vmem(27, 136, 128), vmem(300, 8, 128)], 2,
        [pos, stiff, u, xface, yrim, zrim, xrim, rho], "energy")

    fl, fr = shifted(f, "gx", 1), shifted(f, "gx", -1)
    lane = lax.broadcasted_iota(jnp.int32, pack.shape, 1)
    z = jnp.where(lane < 64, shifted(pack, "gz", -1), shifted(pack, "gz", 1))
    up = jnp.concatenate([f[:, 120:].reshape(64, 128), z[120:]], axis=0)
    down = jnp.concatenate([f[:, :8].reshape(64, 128), z[:8]], axis=0)
    h = jnp.concatenate([shifted(up, "gy", 1), shifted(down, "gy", -1), z], axis=0)
    hl, hr = shifted(h, "gx", 1), shifted(h, "gx", -1)

    wide = shape(PL0, R0, 128)
    fm, fs, vm, vs, f1 = call(
        first_kernel, [wide, wide, wide, wide, shape(4, 64, 128)],
        [WIDE, WIDE, TABLE, TABLE, TABLE, vmem(128, 128)], 1,
        [pos, fl, f, fr, hl, h, hr], "first")
    vm, vs, f1 = call(
        middle_kernel, [wide, wide, shape(4, 64, 128)],
        [WIDE] * 4 + [TABLE] * 3 + COARSE_SCRATCH, 1,
        [pos, *gather_level1(f1), fm, fs, vm, vs], "middle")
    (out,) = call(
        last_kernel, [shape(8, 128, 128)],
        [WIDE] * 4 + [TABLE] * 2 + COARSE_SCRATCH, 1,
        [pos, *gather_level1(f1), fm, fs, vm, vs], "last")
    return out


def solution(mesh):
    return jax.shard_map(
        per_device,
        mesh=mesh,
        in_specs=(P(None, "gx", "gy", "gz"), P("gx", "gy", "gz"), P()),
        out_specs=P("gx", "gy", "gz"),
        check_vma=False,
    )
```

```python
import jax
import jax.numpy as jnp
from jax import lax
from jax.experimental import pallas as pl
from jax.experimental.pallas import tpu as pltpu
from jax.sharding import PartitionSpec as P

FILTER_COEF = 36.0
DAMPING = 0.95
S0 = FILTER_COEF
S1 = FILTER_COEF / 4.0
S2 = FILTER_COEF / 16.0
UN0 = 10
KEEP = 1.0 - DAMPING
HIGH = lax.Precision.HIGHEST
F32 = jnp.float32

PL0, R0 = 24, 160
PL1, R1 = 42, 128
PL2, R2 = 18, 72


def iota(shape, dim):
    return lax.broadcasted_iota(jnp.int32, shape, dim)


def next_lane(value):
    return pltpu.roll(value, 127, 1)


def prev_lane(value):
    return pltpu.roll(value, 1, 1)


def axis_count(place, total):
    return jnp.where(place > 0, 1.0, 0.0) + jnp.where(place < total - 1, 1.0, 0.0)


def planes(start, count, unroll, body):
    step = max(u for u in range(1, unroll + 1) if count % u == 0)
    if step == count:
        for j in range(count):
            body(start + j)
        return

    def block(k, carry):
        for j in range(step):
            body(start + k * step + j)
        return carry

    lax.fori_loop(0, count // step, block, 0)


def make_tables(weight, diag, rows, row_off, lane_place, lane_ok, base_y, base_z, total, scale):
    y = iota((rows, 128), 0) - row_off + base_y
    z = lane_place + base_z
    inside = lane_ok & (y >= 0) & (y < total) & (z >= 0) & (z < total)
    count = axis_count(y, total) + axis_count(z, total)
    weight[0] = jnp.zeros((rows, 128), F32)
    for i in (1, 2):
        value = 1.0 + scale * (count + float(i))
        weight[i] = jnp.where(inside, DAMPING / value, 0.0)
        if diag is not None:
            diag[i] = value


def x_index(place, total):
    edge = (place == 0) | (place == total - 1)
    out = (place < 0) | (place >= total)
    return jnp.where(out, 0, jnp.where(edge, 1, 2))


def lanes_main():
    return iota((R0, 128), 1)


def level0_tables(pos, wm, ws, dm):
    lane = lanes_main()
    yes = lane >= 0
    make_tables(wm, dm, R0, 16, lane, yes, pos[1] * 128, pos[2] * 128, 512, S0)
    side = jnp.where(lane < 64, lane + 128, lane - 128)
    ok = (lane < 8) | (lane >= 120)
    make_tables(ws, None, R0, 16, side, ok, pos[1] * 128, pos[2] * 128, 512, S0)


def level0_sweep(pos, src, dst, fm, fs, wm, ws, first, last, side):
    lane = iota((48, 128), 1)

    def body(p):
        i = x_index(pos[0] * 8 + p - 8, 64)
        for r in range(8, 152, 48):
            rows = pl.ds(r, 48)
            up, dn = pl.ds(r - 1, 48), pl.ds(r + 1, 48)
            m, s = src[0][p, rows], src[1][p, rows]
            mr, sr, ml, sl = next_lane(m), next_lane(s), prev_lane(m), prev_lane(s)
            tot = src[0][p - 1, rows] + src[0][p + 1, rows] + src[0][p, up] + src[0][p, dn]
            tot = tot + jnp.where(lane == 127, sr, mr) + jnp.where(lane == 0, sl, ml)
            dst[0][p, rows] = KEEP * m + wm[i, rows] * (fm[p, rows] + S0 * tot)
            if side:
                tot = src[1][p - 1, rows] + src[1][p + 1, rows] + src[1][p, up] + src[1][p, dn]
                tot = tot + jnp.where(lane == 127, mr, sr) + jnp.where(lane == 0, ml, sl)
                dst[1][p, rows] = KEEP * s + ws[i, rows] * (fs[p, rows] + S0 * tot)

    planes(first, last + 1 - first, UN0, body)


def restrict_matrix(size):
    src, dst = iota((size, 128), 0), iota((size, 128), 1)
    col = jnp.where(dst < 64, dst, dst - 64)
    ok = (dst < 86) | (dst >= 106)
    return jnp.where(ok & (src // 2 == col), 0.125, 0.0)


def level0_restrict(pos, src, fm, dm, tmp, out):
    lane = iota((64, 128), 1)
    matrix = restrict_matrix(128)

    def body(k):
        for r in (0, 64):
            both = None
            for q in (0, 1):
                p = 8 + 2 * k + q
                i = x_index(pos[0] * 8 + p - 8, 64)
                rows = pl.ds(r + 16, 64)
                m, s = src[0][p, rows], src[1][p, rows]
                tot = src[0][p - 1, rows] + src[0][p + 1, rows]
                tot = tot + src[0][p, pl.ds(r + 15, 64)] + src[0][p, pl.ds(r + 17, 64)]
                tot = tot + jnp.where(lane == 127, next_lane(s), next_lane(m))
                tot = tot + jnp.where(lane == 0, prev_lane(s), prev_lane(m))
                res = fm[p, rows] + S0 * tot - dm[i, rows] * m
                both = res if both is None else both + res
            tmp[k, pl.ds(r, 64)] = both
        pair = tmp[k, pl.ds(0, 64, stride=2)] + tmp[k, pl.ds(1, 64, stride=2)]
        out[k] = jnp.dot(pair, matrix, precision=HIGH, preferred_element_type=F32)

    planes(0, 4, 4, body)


def plane_sweep(src, dst, f, w, first, count, x_off, total, rows, scale):
    def body(p):
        i = x_index(p - x_off, total)
        n = rows - 16
        mid = pl.ds(8, n)
        m = src[p, mid]
        tot = src[p - 1, mid] + src[p + 1, mid] + src[p, pl.ds(7, n)] + src[p, pl.ds(9, n)]
        tot = tot + next_lane(m) + prev_lane(m)
        dst[p, mid] = KEEP * m + w[i, mid] * (f[p, mid] + scale * tot)

    planes(first, count, 16, body)


def coarse_levels(pos, blocks, f1, va, vb, f2, a2, b2, w1, d1, w2, tmp):
    gx = pos[0]
    lane1 = iota((R1, 128), 1)
    z1 = jnp.where(lane1 < 96, lane1, lane1 - 128)
    ok1 = (lane1 < 86) | (lane1 >= 106)
    make_tables(w1, d1, R1, 32, z1, ok1, pos[1] * 64, pos[2] * 64, 256, S1)
    lane2 = iota((R2, 128), 1)
    z2 = jnp.where(lane2 < 64, lane2, lane2 - 128)
    ok2 = (lane2 < 43) | (lane2 >= 117)
    make_tables(w2, None, R2, 20, z2, ok2, pos[1] * 32, pos[2] * 32, 128, S2)

    zero = jnp.zeros((R1, 128), F32)
    for p in list(range(0, 5)) + list(range(37, 42)):
        f1[p] = zero
        va[p] = zero
        vb[p] = zero
    for p in range(5, 37):
        for ref in (va, vb):
            ref[p, pl.ds(0, 8)] = jnp.zeros((8, 128), F32)
            ref[p, pl.ds(120, 8)] = jnp.zeros((8, 128), F32)
    for ref in (a2, b2):
        for p in (0, 17):
            ref[p] = jnp.zeros((R2, 128), F32)
        for p in range(1, 17):
            ref[p, pl.ds(0, 8)] = jnp.zeros((8, 128), F32)
            ref[p, pl.ds(64, 8)] = jnp.zeros((8, 128), F32)

    for m in range(4):
        for q in range(2):
            block = blocks[2 * m + q]
            own = gx if q == 0 else jnp.bitwise_xor(gx, 1)
            place = jnp.bitwise_and(own + 8 - 2 * m, 7)
            for j in range(4):
                p = 5 + 4 * place + j
                i = x_index(4 * place + j, 32)
                value = block[j]
                f1[p, pl.ds(8, 112)] = value
                va[p, pl.ds(8, 112)] = w1[i, pl.ds(8, 112)] * value

    plane_sweep(va, vb, f1, w1, 5, 32, 5, 32, R1, S1)

    src, dst = iota((128, 128), 0), iota((128, 128), 1)
    zs1 = jnp.where(src < 96, src, src - 128)
    ks1 = (src < 86) | (src >= 106)
    zd2 = jnp.where(dst < 64, dst, dst - 128)
    kd2 = (dst < 43) | (dst >= 117)
    down = jnp.where(ks1 & kd2 & (lax.shift_right_arithmetic(zs1, 1) == zd2), 0.125, 0.0)
    zs2 = jnp.where(src < 64, src, src - 128)
    ks2 = (src < 43) | (src >= 117)
    zd1 = jnp.where(dst < 96, dst, dst - 128)
    kd1 = (dst < 86) | (dst >= 106)
    up = jnp.where(ks2 & kd1 & (lax.shift_right_arithmetic(zd1, 1) == zs2), 1.0, 0.0)

    def restrict(k):
        both = None
        mid = pl.ds(8, 112)
        for q in (0, 1):
            p = 5 + 2 * k + q
            i = x_index(p - 5, 32)
            m = vb[p, mid]
            tot = vb[p - 1, mid] + vb[p + 1, mid] + vb[p, pl.ds(7, 112)] + vb[p, pl.ds(9, 112)]
            tot = tot + next_lane(m) + prev_lane(m)
            res = f1[p, mid] + S1 * tot - d1[i, mid] * m
            both = res if both is None else both + res
        tmp[k, pl.ds(0, 112)] = both
        pair = tmp[k, pl.ds(0, 56, stride=2)] + tmp[k, pl.ds(1, 56, stride=2)]
        value = jnp.dot(pair, down, precision=HIGH, preferred_element_type=F32)
        f2[1 + k, pl.ds(8, 56)] = value
        a2[1 + k, pl.ds(8, 56)] = w2[x_index(k, 16), pl.ds(8, 56)] * value

    planes(0, 16, 8, restrict)

    src2, dst2 = a2, b2
    for _ in range(7):
        plane_sweep(src2, dst2, f2, w2, 1, 16, 1, 16, R2, S2)
        src2, dst2 = dst2, src2

    def prolong(k):
        e = jnp.dot(src2[1 + k, pl.ds(8, 56)], up, precision=HIGH, preferred_element_type=F32)
        for q in (0, 1):
            for h in (0, 1):
                rows = pl.ds(8 + h, 56, stride=2)
                vb[5 + 2 * k + q, rows] = vb[5 + 2 * k + q, rows] + e

    planes(0, 16, 8, prolong)
    plane_sweep(vb, va, f1, w1, 4 * gx + 1, 12, 5, 32, R1, S1)
    plane_sweep(va, vb, f1, w1, 4 * gx + 2, 10, 5, 32, R1, S1)


def level0_prolong(pos, e1, old, new, first, last):
    src, dst = iota((128, 256), 0), iota((128, 256), 1)
    zs = jnp.where(src < 96, src, src - 128)
    side = dst - 128
    zd = jnp.where(dst < 128, dst, jnp.where(side < 64, side + 128, side - 128))
    ok = (dst < 128) | (side < 8) | (side >= 120)
    up = jnp.where(ok & (lax.shift_right_arithmetic(zd, 1) == zs), 1.0, 0.0)

    def body(k):
        e = e1[4 * pos[0] + 1 + k, pl.ds(28, 72)]
        e = jnp.dot(e, up, precision=HIGH, preferred_element_type=F32)
        for q in (0, 1):
            p = 2 * k + q
            for h in (0, 1):
                rows = pl.ds(8 + h, 72, stride=2)
                new[0][p, rows] = old[0][p, rows] + e[:, :128]
                new[1][p, rows] = old[1][p, rows] + e[:, 128:]

    planes(first // 2, last // 2 + 1 - first // 2, 10, body)


def zero_pads(refs, first, last):
    zero = jnp.zeros((8, 128), F32)
    for ref in refs:
        for p in range(first, last + 1):
            ref[p, pl.ds(0, 8)] = zero
            ref[p, pl.ds(152, 8)] = zero


def rim_kernel(u, cols, rows):
    lane = iota((128, 128), 1)
    acc = jnp.zeros((128, 128), F32)
    for d in range(3):
        for x in range(8):
            k = 8 * d + x
            value = u[d, x]
            acc = jnp.where(lane == k, pltpu.roll(value, k, 1) if k else value, acc)
            rows[pl.ds(k, 1)] = u[d, x, pl.ds(0, 1)]
    cols[...] = acc


def energy_kernel(pos, stiff, u, xface, yrim, zrim, xrim, rho, f, pack, u0, u1, table):
    gx, gy, gz = pos[0], pos[1], pos[2]
    keep_x = jnp.where(gx < 7, 1.0, 0.0)
    keep_y = jnp.where(gy < 3, 1.0, 0.0)
    keep_z = jnp.where(gz < 3, 1.0, 0.0)
    n = 0
    for i in range(24):
        for j in range(i, 24):
            value = stiff[i, j] if i == j else stiff[i, j] + stiff[j, i]
            table[n] = jnp.full((8, 128), value, F32)
            n += 1
    lane = iota((128, 128), 1)
    lane8 = iota((8, 128), 1)
    for d in range(3):
        for x in range(9):
            k = 8 * d + x
            if x < 8:
                body = u[d, x]
                col = zrim[...]
                row = yrim[pl.ds(k, 1)]
                corner = yrim[pl.ds(24, 8)]
            else:
                k = 8 * d
                body = xface[d] * keep_x
                col = xrim[pl.ds(32, 128)] * keep_x
                row = xrim[pl.ds(k, 1)] * keep_x
                corner = xrim[pl.ds(24, 8)] * keep_x
            row = jnp.broadcast_to(row, (8, 128)) * keep_y
            corner = jnp.broadcast_to(corner[0:1], (8, 128)) * (keep_y * keep_z)
            q = 9 * d + x
            u0[q, pl.ds(0, 128)] = body
            u0[q, pl.ds(128, 8)] = row
            u1[q, pl.ds(0, 128)] = jnp.where(
                lane == 127, pltpu.roll(col, 127 - k, 1) * keep_z, next_lane(body))
            u1[q, pl.ds(128, 8)] = jnp.where(
                lane8 == 127, pltpu.roll(corner, 127 - k, 1), next_lane(row))

    def chunk(c, carry):
        x, y = c // 16, pl.multiple_of((c % 16) * 8, 8)
        val = []
        for c_z in (0, 1):
            for b in (0, 1):
                for a in (0, 1):
                    for d in range(3):
                        ref = u1 if c_z else u0
                        val.append(ref[9 * d + x + a, pl.ds(y + b, 8)])
        energy = None
        n = 0
        for i in range(24):
            acc = None
            for j in range(i, 24):
                term = table[n] * val[j]
                acc = term if acc is None else acc + term
                n += 1
            acc = acc * val[i]
            energy = acc if energy is None else energy + acc
        r = rho[x, pl.ds(y, 8)]
        f[x, pl.ds(y, 8)] = -3.0 * r * r * energy
        return carry

    lax.fori_loop(0, 128, chunk, 0)
    acc = jnp.zeros((128, 128), F32)
    for x in range(8):
        value = f[x]
        low = pltpu.roll(value, 8 * x, 1) if x else value
        acc = jnp.where((lane >= 8 * x) & (lane < 8 * x + 8), low, acc)
        high = pltpu.roll(value, (8 * x + 72) % 128, 1)
        acc = jnp.where((lane >= 64 + 8 * x) & (lane < 72 + 8 * x), high, acc)
    pack[...] = acc


def spread(value, x):
    lane = iota(value.shape, 1)
    low = pltpu.roll(value, (128 - 8 * x) % 128, 1) if x else value
    high = pltpu.roll(value, (56 - 8 * x) % 128, 1)
    return jnp.where(lane < 64, low, high)


def first_kernel(pos, fl, fc, fr, hl, hc, hr, fm, fs, vm, vs, out, am, as_, wm, ws, dm, tmp):
    level0_tables(pos, wm, ws, dm)
    zero_pads((fm, fs, vm, vs, am, as_), 0, 23)
    for b, (blk, halo) in enumerate(((fl, hl), (fc, hc), (fr, hr))):
        for x in range(8):
            p = 8 * b + x
            i = x_index(pos[0] * 8 + p - 8, 64)
            parts = (
                (8, 8, halo[pl.ds(8 * x, 8)], spread(halo[pl.ds(64, 8)], x)),
                (16, 128, blk[x], spread(halo[pl.ds(144, 128)], x)),
                (144, 8, halo[pl.ds(72 + 8 * x, 8)], spread(halo[pl.ds(136, 8)], x)),
            )
            for start, size, main, side in parts:
                rows = pl.ds(start, size)
                fm[p, rows] = main
                fs[p, rows] = side
                am[p, rows] = wm[i, rows] * main
                as_[p, rows] = ws[i, rows] * side
    level0_sweep(pos, (am, as_), (vm, vs), fm, fs, wm, ws, 2, 21, True)
    level0_restrict(pos, (vm, vs), fm, dm, tmp, out)


def middle_kernel(pos, *refs):
    blocks = refs[:8]
    fm, fs, vm, vs, om, os_, out = refs[8:15]
    am, as_, bm, bs, wm, ws, dm, f1, va, vb, f2, a2, b2, w1, d1, w2, tmp = refs[15:]
    coarse_levels(pos, blocks, f1, va, vb, f2, a2, b2, w1, d1, w2, tmp)
    level0_tables(pos, wm, ws, dm)
    zero_pads((am, as_, bm, bs, om, os_), 0, 23)
    level0_prolong(pos, vb, (vm, vs), (am, as_), 2, 21)
    level0_sweep(pos, (am, as_), (bm, bs), fm, fs, wm, ws, 3, 20, True)
    level0_sweep(pos, (bm, bs), (am, as_), fm, fs, wm, ws, 4, 19, True)
    level0_sweep(pos, (am, as_), (bm, bs), fm, fs, wm, ws, 5, 18, True)
    level0_sweep(pos, (bm, bs), (om, os_), fm, fs, wm, ws, 6, 17, True)
    level0_restrict(pos, (om, os_), fm, dm, tmp, out)


def last_kernel(pos, *refs):
    blocks = refs[:8]
    fm, fs, vm, vs, out = refs[8:13]
    am, as_, bm, bs, wm, ws, f1, va, vb, f2, a2, b2, w1, d1, w2, tmp = refs[13:]
    coarse_levels(pos, blocks, f1, va, vb, f2, a2, b2, w1, d1, w2, tmp)
    level0_tables(pos, wm, ws, None)
    zero_pads((am, as_, bm, bs), 0, 23)
    level0_prolong(pos, vb, (vm, vs), (am, as_), 6, 17)
    level0_sweep(pos, (am, as_), (bm, bs), fm, fs, wm, ws, 7, 16, True)
    level0_sweep(pos, (bm, bs), (am, as_), fm, fs, wm, ws, 8, 15, False)
    for x in range(8):
        out[x] = am[8 + x, pl.ds(16, 128)]


SMEM = pl.BlockSpec(memory_space=pltpu.SMEM)
VM = pl.BlockSpec(memory_space=pltpu.VMEM)


def shape(*dims):
    return jax.ShapeDtypeStruct(dims, F32)


def vmem(*dims):
    return pltpu.VMEM(dims, F32)


def call(kernel, outs, scratch, scalars, args, name, limit=12):
    specs = [SMEM] * scalars + [VM] * (len(args) - scalars)
    return pl.pallas_call(
        kernel,
        out_shape=outs,
        in_specs=specs,
        out_specs=[VM] * len(outs),
        scratch_shapes=scratch,
        compiler_params=pltpu.CompilerParams(vmem_limit_bytes=limit << 20),
        name=name,
    )(*args)


def shifted(value, axis, step):
    size = lax.axis_size(axis)
    return lax.ppermute(value, axis, [(i, (i + step) % size) for i in range(size)])


def swapped(value):
    return lax.ppermute(value, "gx", [(i, i ^ 1) for i in range(lax.axis_size("gx"))])


COARSE_SCRATCH = [
    vmem(PL1, R1, 128), vmem(PL1, R1, 128), vmem(PL1, R1, 128),
    vmem(PL2, R2, 128), vmem(PL2, R2, 128), vmem(PL2, R2, 128),
    vmem(3, R1, 128), vmem(3, R1, 128), vmem(3, R2, 128), vmem(16, 128, 128),
]
TABLE = vmem(3, R0, 128)
WIDE = vmem(PL0, R0, 128)


def gather_level1(own):
    lane = lax.broadcasted_iota(jnp.int32, own.shape, 2)
    right, left = shifted(own, "gz", -1), shifted(own, "gz", 1)
    own = jnp.where(lane < 64, own, jnp.where(lane < 96, right, left))
    low, high = shifted(own[:, 40:], "gy", 1), shifted(own[:, :24], "gy", -1)
    own = jnp.concatenate([low, own, high], axis=1)
    blocks = []
    for m in range(4):
        part = own if m == 0 else shifted(own, "gx", 2 * m)
        blocks += [part, swapped(part)]
    return blocks


def per_device(u, rho, stiff):
    pos = jnp.stack([lax.axis_index(a) for a in ("gx", "gy", "gz")]).astype(jnp.int32)
    cols, rows = call(rim_kernel, [shape(128, 128), shape(24, 128)], [], 0, [u], "rims")
    xface = shifted(u[:, 0], "gx", -1)
    zrim = shifted(cols, "gz", -1)
    yrim = shifted(jnp.concatenate([rows, zrim[:8]], axis=0), "gy", -1)
    xrim = shifted(jnp.concatenate([yrim, zrim], axis=0), "gx", -1)
    f, pack = call(
        energy_kernel, [shape(8, 128, 128), shape(128, 128)],
        [vmem(27, 136, 128), vmem(27, 136, 128), vmem(300, 8, 128)], 2,
        [pos, stiff, u, xface, yrim, zrim, xrim, rho], "energy")

    fl, fr = shifted(f, "gx", 1), shifted(f, "gx", -1)
    lane = lax.broadcasted_iota(jnp.int32, pack.shape, 1)
    z = jnp.where(lane < 64, shifted(pack, "gz", -1), shifted(pack, "gz", 1))
    up = jnp.concatenate([f[:, 120:].reshape(64, 128), z[120:]], axis=0)
    down = jnp.concatenate([f[:, :8].reshape(64, 128), z[:8]], axis=0)
    h = jnp.concatenate([shifted(up, "gy", 1), shifted(down, "gy", -1), z], axis=0)
    hl, hr = shifted(h, "gx", 1), shifted(h, "gx", -1)

    wide = shape(PL0, R0, 128)
    fm, fs, vm, vs, f1 = call(
        first_kernel, [wide, wide, wide, wide, shape(4, 64, 128)],
        [WIDE, WIDE, TABLE, TABLE, TABLE, vmem(4, 128, 128)], 1,
        [pos, fl, f, fr, hl, h, hr], "first")
    vm, vs, f1 = call(
        middle_kernel, [wide, wide, shape(4, 64, 128)],
        [WIDE] * 4 + [TABLE] * 3 + COARSE_SCRATCH, 1,
        [pos, *gather_level1(f1), fm, fs, vm, vs], "middle", 24)
    (out,) = call(
        last_kernel, [shape(8, 128, 128)],
        [WIDE] * 4 + [TABLE] * 2 + COARSE_SCRATCH, 1,
        [pos, *gather_level1(f1), fm, fs, vm, vs], "last", 24)
    return out


def solution(mesh):
    return jax.shard_map(
        per_device,
        mesh=mesh,
        in_specs=(P(None, "gx", "gy", "gz"), P("gx", "gy", "gz"), P()),
        out_specs=P("gx", "gy", "gz"),
        check_vma=False,
    )
```

```python
import jax
import jax.numpy as jnp
from jax import lax
from jax.experimental import pallas as pl
from jax.experimental.pallas import tpu as pltpu
from jax.sharding import PartitionSpec as P

FILTER_COEF = 36.0
DAMPING = 0.95
S0 = FILTER_COEF
S1 = FILTER_COEF / 4.0
S2 = FILTER_COEF / 16.0
UN0 = 10
KEEP = 1.0 - DAMPING
HIGH = lax.Precision.HIGHEST
F32 = jnp.float32
BF16 = jnp.bfloat16

PL0, R0 = 24, 160
PL1, R1 = 42, 128
PL2, R2 = 18, 72


def iota(shape, dim):
    return lax.broadcasted_iota(jnp.int32, shape, dim)


def next_lane(value):
    return pltpu.roll(value, 127, 1)


def prev_lane(value):
    return pltpu.roll(value, 1, 1)


def axis_count(place, total):
    return jnp.where(place > 0, 1.0, 0.0) + jnp.where(place < total - 1, 1.0, 0.0)


def planes(start, count, unroll, body):
    step = max(u for u in range(1, unroll + 1) if count % u == 0)
    if step == count:
        for j in range(count):
            body(start + j)
        return

    def block(k, carry):
        for j in range(step):
            body(start + k * step + j)
        return carry

    lax.fori_loop(0, count // step, block, 0)


def make_tables(weight, diag, rows, row_off, lane_place, lane_ok, base_y, base_z, total, scale):
    y = iota((rows, 128), 0) - row_off + base_y
    z = lane_place + base_z
    inside = lane_ok & (y >= 0) & (y < total) & (z >= 0) & (z < total)
    count = axis_count(y, total) + axis_count(z, total)
    weight[0] = jnp.zeros((rows, 128), F32)
    for i in (1, 2):
        value = 1.0 + scale * (count + float(i))
        weight[i] = jnp.where(inside, DAMPING / value, 0.0)
        if diag is not None:
            diag[i] = value


def x_index(place, total):
    edge = (place == 0) | (place == total - 1)
    out = (place < 0) | (place >= total)
    return jnp.where(out, 0, jnp.where(edge, 1, 2))


def lanes_main():
    return iota((R0, 128), 1)


def level0_tables(pos, wm, ws, dm):
    lane = lanes_main()
    yes = lane >= 0
    make_tables(wm, dm, R0, 16, lane, yes, pos[1] * 128, pos[2] * 128, 512, S0)
    side = jnp.where(lane < 64, lane + 128, lane - 128)
    ok = (lane < 8) | (lane >= 120)
    make_tables(ws, None, R0, 16, side, ok, pos[1] * 128, pos[2] * 128, 512, S0)


def level0_sweep(pos, src, dst, fm, fs, wm, ws, first, last, side):
    lane = iota((48, 128), 1)

    def body(p):
        i = x_index(pos[0] * 8 + p - 8, 64)
        for r in range(8, 152, 48):
            rows = pl.ds(r, 48)
            up, dn = pl.ds(r - 1, 48), pl.ds(r + 1, 48)
            m, s = src[0][p, rows], src[1][p, rows]
            mr, sr, ml, sl = next_lane(m), next_lane(s), prev_lane(m), prev_lane(s)
            tot = src[0][p - 1, rows] + src[0][p + 1, rows] + src[0][p, up] + src[0][p, dn]
            tot = tot + jnp.where(lane == 127, sr, mr) + jnp.where(lane == 0, sl, ml)
            dst[0][p, rows] = KEEP * m + wm[i, rows] * (fm[p, rows] + S0 * tot)
            if side:
                tot = src[1][p - 1, rows] + src[1][p + 1, rows] + src[1][p, up] + src[1][p, dn]
                tot = tot + jnp.where(lane == 127, mr, sr) + jnp.where(lane == 0, ml, sl)
                dst[1][p, rows] = KEEP * s + ws[i, rows] * (fs[p, rows] + S0 * tot)

    planes(first, last + 1 - first, UN0, body)


def restrict_matrix(size):
    src, dst = iota((size, 128), 0), iota((size, 128), 1)
    col = jnp.where(dst < 64, dst, dst - 64)
    ok = (dst < 86) | (dst >= 106)
    return jnp.where(ok & (src // 2 == col), 0.125, 0.0)


def level0_restrict(pos, src, fm, dm, tmp, out):
    lane = iota((64, 128), 1)
    matrix = restrict_matrix(128)

    def body(k):
        for r in (0, 64):
            both = None
            for q in (0, 1):
                p = 8 + 2 * k + q
                i = x_index(pos[0] * 8 + p - 8, 64)
                rows = pl.ds(r + 16, 64)
                m, s = src[0][p, rows], src[1][p, rows]
                tot = src[0][p - 1, rows] + src[0][p + 1, rows]
                tot = tot + src[0][p, pl.ds(r + 15, 64)] + src[0][p, pl.ds(r + 17, 64)]
                tot = tot + jnp.where(lane == 127, next_lane(s), next_lane(m))
                tot = tot + jnp.where(lane == 0, prev_lane(s), prev_lane(m))
                res = fm[p, rows] + S0 * tot - dm[i, rows] * m
                both = res if both is None else both + res
            tmp[k, pl.ds(r, 64)] = both
        pair = tmp[k, pl.ds(0, 64, stride=2)] + tmp[k, pl.ds(1, 64, stride=2)]
        out[k] = jnp.dot(pair, matrix, precision=HIGH, preferred_element_type=F32)

    planes(0, 4, 4, body)


def plane_sweep(src, dst, f, w, first, count, x_off, total, rows, scale):
    def body(p):
        i = x_index(p - x_off, total)
        n = rows - 16
        mid = pl.ds(8, n)
        m = src[p, mid]
        tot = src[p - 1, mid] + src[p + 1, mid] + src[p, pl.ds(7, n)] + src[p, pl.ds(9, n)]
        tot = tot + next_lane(m) + prev_lane(m)
        dst[p, mid] = KEEP * m + w[i, mid] * (f[p, mid] + scale * tot)

    planes(first, count, 16, body)


def coarse_levels(pos, blocks, f1, va, vb, f2, a2, b2, w1, d1, w2, tmp):
    gx = pos[0]
    lane1 = iota((R1, 128), 1)
    z1 = jnp.where(lane1 < 96, lane1, lane1 - 128)
    ok1 = (lane1 < 86) | (lane1 >= 106)
    make_tables(w1, d1, R1, 32, z1, ok1, pos[1] * 64, pos[2] * 64, 256, S1)
    lane2 = iota((R2, 128), 1)
    z2 = jnp.where(lane2 < 64, lane2, lane2 - 128)
    ok2 = (lane2 < 43) | (lane2 >= 117)
    make_tables(w2, None, R2, 20, z2, ok2, pos[1] * 32, pos[2] * 32, 128, S2)

    zero = jnp.zeros((R1, 128), F32)
    for p in list(range(0, 5)) + list(range(37, 42)):
        f1[p] = zero
        va[p] = zero
        vb[p] = zero
    for p in range(5, 37):
        for ref in (va, vb):
            ref[p, pl.ds(0, 8)] = jnp.zeros((8, 128), F32)
            ref[p, pl.ds(120, 8)] = jnp.zeros((8, 128), F32)
    for ref in (a2, b2):
        for p in (0, 17):
            ref[p] = jnp.zeros((R2, 128), F32)
        for p in range(1, 17):
            ref[p, pl.ds(0, 8)] = jnp.zeros((8, 128), F32)
            ref[p, pl.ds(64, 8)] = jnp.zeros((8, 128), F32)

    for m in range(4):
        for q in range(2):
            block = blocks[2 * m + q]
            own = gx if q == 0 else jnp.bitwise_xor(gx, 1)
            place = jnp.bitwise_and(own + 8 - 2 * m, 7)
            for j in range(4):
                p = 5 + 4 * place + j
                i = x_index(4 * place + j, 32)
                value = block[j]
                f1[p, pl.ds(8, 112)] = value
                va[p, pl.ds(8, 112)] = w1[i, pl.ds(8, 112)] * value

    plane_sweep(va, vb, f1, w1, 5, 32, 5, 32, R1, S1)

    src, dst = iota((128, 128), 0), iota((128, 128), 1)
    zs1 = jnp.where(src < 96, src, src - 128)
    ks1 = (src < 86) | (src >= 106)
    zd2 = jnp.where(dst < 64, dst, dst - 128)
    kd2 = (dst < 43) | (dst >= 117)
    down = jnp.where(ks1 & kd2 & (lax.shift_right_arithmetic(zs1, 1) == zd2), 0.125, 0.0)
    zs2 = jnp.where(src < 64, src, src - 128)
    ks2 = (src < 43) | (src >= 117)
    zd1 = jnp.where(dst < 96, dst, dst - 128)
    kd1 = (dst < 86) | (dst >= 106)
    up = jnp.where(ks2 & kd1 & (lax.shift_right_arithmetic(zd1, 1) == zs2), 1.0, 0.0)

    def restrict(k):
        both = None
        mid = pl.ds(8, 112)
        for q in (0, 1):
            p = 5 + 2 * k + q
            i = x_index(p - 5, 32)
            m = vb[p, mid]
            tot = vb[p - 1, mid] + vb[p + 1, mid] + vb[p, pl.ds(7, 112)] + vb[p, pl.ds(9, 112)]
            tot = tot + next_lane(m) + prev_lane(m)
            res = f1[p, mid] + S1 * tot - d1[i, mid] * m
            both = res if both is None else both + res
        tmp[k, pl.ds(0, 112)] = both
        pair = tmp[k, pl.ds(0, 56, stride=2)] + tmp[k, pl.ds(1, 56, stride=2)]
        value = jnp.dot(pair, down, precision=HIGH, preferred_element_type=F32)
        f2[1 + k, pl.ds(8, 56)] = value
        a2[1 + k, pl.ds(8, 56)] = w2[x_index(k, 16), pl.ds(8, 56)] * value

    planes(0, 16, 8, restrict)

    src2, dst2 = a2, b2
    for _ in range(7):
        plane_sweep(src2, dst2, f2, w2, 1, 16, 1, 16, R2, S2)
        src2, dst2 = dst2, src2

    def prolong(k):
        e = jnp.dot(src2[1 + k, pl.ds(8, 56)], up, precision=HIGH, preferred_element_type=F32)
        for q in (0, 1):
            for h in (0, 1):
                rows = pl.ds(8 + h, 56, stride=2)
                vb[5 + 2 * k + q, rows] = vb[5 + 2 * k + q, rows] + e

    planes(0, 16, 8, prolong)
    plane_sweep(vb, va, f1, w1, 4 * gx + 1, 12, 5, 32, R1, S1)
    plane_sweep(va, vb, f1, w1, 4 * gx + 2, 10, 5, 32, R1, S1)


def level0_prolong(pos, e1, old, new, first, last):
    src, dst = iota((128, 256), 0), iota((128, 256), 1)
    zs = jnp.where(src < 96, src, src - 128)
    side = dst - 128
    zd = jnp.where(dst < 128, dst, jnp.where(side < 64, side + 128, side - 128))
    ok = (dst < 128) | (side < 8) | (side >= 120)
    up = jnp.where(ok & (lax.shift_right_arithmetic(zd, 1) == zs), 1.0, 0.0)

    def body(k):
        e = e1[4 * pos[0] + 1 + k, pl.ds(28, 72)]
        e = jnp.dot(e, up, precision=HIGH, preferred_element_type=F32)
        for q in (0, 1):
            p = 2 * k + q
            for h in (0, 1):
                rows = pl.ds(8 + h, 72, stride=2)
                new[0][p, rows] = old[0][p, rows] + e[:, :128]
                new[1][p, rows] = old[1][p, rows] + e[:, 128:]

    planes(first // 2, last // 2 + 1 - first // 2, 10, body)


def zero_pads(refs, first, last):
    zero = jnp.zeros((8, 128), F32)
    for ref in refs:
        for p in range(first, last + 1):
            ref[p, pl.ds(0, 8)] = zero
            ref[p, pl.ds(152, 8)] = zero


def rim_kernel(u, cols, rows):
    lane = iota((128, 128), 1)
    acc = jnp.zeros((128, 128), F32)
    for d in range(3):
        for x in range(8):
            k = 8 * d + x
            value = u[d, x]
            acc = jnp.where(lane == k, pltpu.roll(value, k, 1) if k else value, acc)
            rows[pl.ds(k, 1)] = u[d, x, pl.ds(0, 1)]
    cols[...] = acc


def form_matrix(stiff, high, low):
    r, c = iota((192, 24), 0), iota((192, 24), 1)
    wide = jnp.where(lax.shift_right_logical(r, 3) == c, 1.0, 0.0)
    r, c = iota((24, 192), 0), iota((24, 192), 1)
    tall = jnp.where(lax.shift_right_logical(c, 3) == r, 1.0, 0.0)
    full = jnp.dot(wide, stiff, precision=HIGH, preferred_element_type=F32)
    full = jnp.dot(full, tall, precision=HIGH, preferred_element_type=F32)
    r, c = iota((192, 192), 0), iota((192, 192), 1)
    full = jnp.where(jnp.bitwise_and(r, 7) == jnp.bitwise_and(c, 7), full, 0.0)
    top = full.astype(BF16)
    high[...] = top
    low[...] = (full - top.astype(F32)).astype(BF16)


def energy_group(u0, u1, high, low, rho, f, x, y, x_in, x_out):
    cols = []
    for q in range(4):
        val = []
        for ref in (u0, u1):
            for b in (0, 1):
                for a in (0, 1):
                    for d in range(3):
                        val.append(ref[9 * d + x + a, pl.ds(y + 8 * q + b, 8)])
        cols.append(jnp.concatenate(val, axis=0))
    u = jnp.concatenate(cols, axis=1)
    top = u.astype(BF16)
    pushed = jnp.dot(high[...], top, preferred_element_type=F32)
    pushed = pushed + jnp.dot(low[...], top, preferred_element_type=F32)
    prod = pushed * (u + (u - top.astype(F32)))
    energy = prod[0:8]
    for i in range(1, 24):
        energy = energy + prod[8 * i:8 * i + 8]
    for q in range(4):
        rows = pl.ds(y + 8 * q, 8)
        r = rho[x_in, rows]
        f[x_out, rows] = -3.0 * r * r * energy[:, 128 * q:128 * q + 128]


def energy_first(pos, stiff, u, zrim, rho, u0, u1, high, low, f):
    keep_z = jnp.where(pos[2] < 3, 1.0, 0.0)
    form_matrix(stiff[...], high, low)
    lane = iota((128, 128), 1)
    col = zrim[...] * keep_z
    for d in range(3):
        for x in range(8):
            k, q = 8 * d + x, 9 * d + x
            body = u[d, x]
            u0[q] = body
            u1[q] = jnp.where(lane == 127, pltpu.roll(col, 127 - k, 1), next_lane(body))

    def group(c):
        x = c // 3
        y = pl.multiple_of((c - 3 * x) * 32, 32)
        energy_group(u0, u1, high, low, rho, f, x, y, x, x)

    planes(0, 12, 4, group)


def energy_second(u0, u1, high, low, rho, f):
    def group(c):
        x = c // 3
        y = pl.multiple_of((c - 3 * x) * 32, 32)
        energy_group(u0, u1, high, low, rho, f, x + 4, y, x + 4, x)

    planes(0, 9, 3, group)


def energy_last(pos, u0, u1, high, low, rho, xface, yrim, zrim, xrim, fa, fb, f, pack, w0, w1):
    gx, gy, gz = pos[0], pos[1], pos[2]
    keep_x = jnp.where(gx < 7, 1.0, 0.0)
    keep_y = jnp.where(gy < 3, 1.0, 0.0)
    keep_z = jnp.where(gz < 3, 1.0, 0.0)
    lane = iota((128, 128), 1)
    lane8 = iota((8, 128), 1)
    for d in range(3):
        for x in range(9):
            k, q = 8 * d + x, 9 * d + x
            if x < 8:
                rows = pl.ds(0, 128) if x == 7 else pl.ds(96, 32)
                w0[q, rows] = u0[q, rows]
                w1[q, rows] = u1[q, rows]
                row = yrim[pl.ds(k, 1)]
                corner = yrim[pl.ds(24, 8)]
            else:
                k = 8 * d
                body = xface[d] * keep_x
                col = xrim[pl.ds(32, 128)] * (keep_x * keep_z)
                w0[q, pl.ds(0, 128)] = body
                w1[q, pl.ds(0, 128)] = jnp.where(
                    lane == 127, pltpu.roll(col, 127 - k, 1), next_lane(body))
                row = xrim[pl.ds(k, 1)] * keep_x
                corner = xrim[pl.ds(24, 8)] * keep_x
            row = jnp.broadcast_to(row, (8, 128)) * keep_y
            corner = jnp.broadcast_to(corner[0:1], (8, 128)) * (keep_y * keep_z)
            w0[q, pl.ds(128, 8)] = row
            w1[q, pl.ds(128, 8)] = jnp.where(
                lane8 == 127, pltpu.roll(corner, 127 - k, 1), next_lane(row))
    for x in range(4):
        f[x, pl.ds(0, 96)] = fa[x, pl.ds(0, 96)]
    for x in range(3):
        f[4 + x, pl.ds(0, 96)] = fb[x, pl.ds(0, 96)]
    for x in range(7):
        energy_group(w0, w1, high, low, rho, f, x, 96, x, x)
    for q in range(4):
        energy_group(w0, w1, high, low, rho, f, 7, 32 * q, 7, 7)
    acc = jnp.zeros((128, 128), F32)
    for x in range(8):
        value = f[x]
        low_z = pltpu.roll(value, 8 * x, 1) if x else value
        acc = jnp.where((lane >= 8 * x) & (lane < 8 * x + 8), low_z, acc)
        high_z = pltpu.roll(value, (8 * x + 72) % 128, 1)
        acc = jnp.where((lane >= 64 + 8 * x) & (lane < 72 + 8 * x), high_z, acc)
    pack[...] = acc


def spread(value, x):
    lane = iota(value.shape, 1)
    low = pltpu.roll(value, (128 - 8 * x) % 128, 1) if x else value
    high = pltpu.roll(value, (56 - 8 * x) % 128, 1)
    return jnp.where(lane < 64, low, high)


def first_kernel(pos, fl, fc, fr, hl, hc, hr, fm, fs, vm, vs, out, am, as_, wm, ws, dm, tmp):
    level0_tables(pos, wm, ws, dm)
    zero_pads((fm, fs, vm, vs, am, as_), 0, 23)
    for b, (blk, halo) in enumerate(((fl, hl), (fc, hc), (fr, hr))):
        for x in range(8):
            p = 8 * b + x
            i = x_index(pos[0] * 8 + p - 8, 64)
            parts = (
                (8, 8, halo[pl.ds(8 * x, 8)], spread(halo[pl.ds(64, 8)], x)),
                (16, 128, blk[x], spread(halo[pl.ds(144, 128)], x)),
                (144, 8, halo[pl.ds(72 + 8 * x, 8)], spread(halo[pl.ds(136, 8)], x)),
            )
            for start, size, main, side in parts:
                rows = pl.ds(start, size)
                fm[p, rows] = main
                fs[p, rows] = side
                am[p, rows] = wm[i, rows] * main
                as_[p, rows] = ws[i, rows] * side
    level0_sweep(pos, (am, as_), (vm, vs), fm, fs, wm, ws, 2, 21, True)
    level0_restrict(pos, (vm, vs), fm, dm, tmp, out)


def middle_kernel(pos, *refs):
    blocks = refs[:8]
    fm, fs, vm, vs, om, os_, out = refs[8:15]
    am, as_, bm, bs, wm, ws, dm, f1, va, vb, f2, a2, b2, w1, d1, w2, tmp = refs[15:]
    coarse_levels(pos, blocks, f1, va, vb, f2, a2, b2, w1, d1, w2, tmp)
    level0_tables(pos, wm, ws, dm)
    zero_pads((am, as_, bm, bs, om, os_), 0, 23)
    level0_prolong(pos, vb, (vm, vs), (am, as_), 2, 21)
    level0_sweep(pos, (am, as_), (bm, bs), fm, fs, wm, ws, 3, 20, True)
    level0_sweep(pos, (bm, bs), (am, as_), fm, fs, wm, ws, 4, 19, True)
    level0_sweep(pos, (am, as_), (bm, bs), fm, fs, wm, ws, 5, 18, True)
    level0_sweep(pos, (bm, bs), (om, os_), fm, fs, wm, ws, 6, 17, True)
    level0_restrict(pos, (om, os_), fm, dm, tmp, out)


def last_kernel(pos, *refs):
    blocks = refs[:8]
    fm, fs, vm, vs, out = refs[8:13]
    am, as_, bm, bs, wm, ws, f1, va, vb, f2, a2, b2, w1, d1, w2, tmp = refs[13:]
    coarse_levels(pos, blocks, f1, va, vb, f2, a2, b2, w1, d1, w2, tmp)
    level0_tables(pos, wm, ws, None)
    zero_pads((am, as_, bm, bs), 0, 23)
    level0_prolong(pos, vb, (vm, vs), (am, as_), 6, 17)
    level0_sweep(pos, (am, as_), (bm, bs), fm, fs, wm, ws, 7, 16, True)
    level0_sweep(pos, (bm, bs), (am, as_), fm, fs, wm, ws, 8, 15, False)
    for x in range(8):
        out[x] = am[8 + x, pl.ds(16, 128)]


SMEM = pl.BlockSpec(memory_space=pltpu.SMEM)
VM = pl.BlockSpec(memory_space=pltpu.VMEM)


def shape(*dims):
    return jax.ShapeDtypeStruct(dims, F32)


def vmem(*dims):
    return pltpu.VMEM(dims, F32)


def call(kernel, outs, scratch, scalars, args, name, limit=12):
    specs = [SMEM] * scalars + [VM] * (len(args) - scalars)
    return pl.pallas_call(
        kernel,
        out_shape=outs,
        in_specs=specs,
        out_specs=[VM] * len(outs),
        scratch_shapes=scratch,
        compiler_params=pltpu.CompilerParams(vmem_limit_bytes=limit << 20),
        name=name,
    )(*args)


def shifted(value, axis, step):
    size = lax.axis_size(axis)
    return lax.ppermute(value, axis, [(i, (i + step) % size) for i in range(size)])


def swapped(value):
    return lax.ppermute(value, "gx", [(i, i ^ 1) for i in range(lax.axis_size("gx"))])


COARSE_SCRATCH = [
    vmem(PL1, R1, 128), vmem(PL1, R1, 128), vmem(PL1, R1, 128),
    vmem(PL2, R2, 128), vmem(PL2, R2, 128), vmem(PL2, R2, 128),
    vmem(3, R1, 128), vmem(3, R1, 128), vmem(3, R2, 128), vmem(16, 128, 128),
]
TABLE = vmem(3, R0, 128)
WIDE = vmem(PL0, R0, 128)


def gather_level1(own):
    lane = lax.broadcasted_iota(jnp.int32, own.shape, 2)
    right, left = shifted(own, "gz", -1), shifted(own, "gz", 1)
    own = jnp.where(lane < 64, own, jnp.where(lane < 96, right, left))
    low, high = shifted(own[:, 40:], "gy", 1), shifted(own[:, :24], "gy", -1)
    own = jnp.concatenate([low, own, high], axis=1)
    blocks = []
    for m in range(4):
        part = own if m == 0 else shifted(own, "gx", 2 * m)
        blocks += [part, swapped(part)]
    return blocks


def per_device(u, rho, stiff):
    pos = jnp.stack([lax.axis_index(a) for a in ("gx", "gy", "gz")]).astype(jnp.int32)
    cols, rows = call(rim_kernel, [shape(128, 128), shape(24, 128)], [], 0, [u], "rims")
    xface = shifted(u[:, 0], "gx", -1)
    zrim = shifted(cols, "gz", -1)
    yrim = shifted(jnp.concatenate([rows, zrim[:8]], axis=0), "gy", -1)
    mat = jax.ShapeDtypeStruct((192, 192), BF16)
    u0, u1, high, low, fa = call(
        energy_first, [shape(27, 128, 128), shape(27, 128, 128), mat, mat, shape(4, 128, 128)],
        [], 1, [pos, stiff, u, zrim, rho], "energy_first")
    yrim, fa = lax.optimization_barrier((yrim, fa))
    xrim = shifted(jnp.concatenate([yrim, zrim], axis=0), "gx", -1)
    (fb,) = call(
        energy_second, [shape(3, 128, 128)], [], 0, [u0, u1, high, low, rho], "energy_second")
    f, pack = call(
        energy_last, [shape(8, 128, 128), shape(128, 128)],
        [vmem(27, 136, 128), vmem(27, 136, 128)], 1,
        [pos, u0, u1, high, low, rho, xface, yrim, zrim, xrim, fa, fb], "energy_last")

    fl, fr = shifted(f, "gx", 1), shifted(f, "gx", -1)
    lane = lax.broadcasted_iota(jnp.int32, pack.shape, 1)
    z = jnp.where(lane < 64, shifted(pack, "gz", -1), shifted(pack, "gz", 1))
    up = jnp.concatenate([f[:, 120:].reshape(64, 128), z[120:]], axis=0)
    down = jnp.concatenate([f[:, :8].reshape(64, 128), z[:8]], axis=0)
    h = jnp.concatenate([shifted(up, "gy", 1), shifted(down, "gy", -1), z], axis=0)
    hl, hr = shifted(h, "gx", 1), shifted(h, "gx", -1)

    wide = shape(PL0, R0, 128)
    fm, fs, vm, vs, f1 = call(
        first_kernel, [wide, wide, wide, wide, shape(4, 64, 128)],
        [WIDE, WIDE, TABLE, TABLE, TABLE, vmem(4, 128, 128)], 1,
        [pos, fl, f, fr, hl, h, hr], "first")
    vm, vs, f1 = call(
        middle_kernel, [wide, wide, shape(4, 64, 128)],
        [WIDE] * 4 + [TABLE] * 3 + COARSE_SCRATCH, 1,
        [pos, *gather_level1(f1), fm, fs, vm, vs], "middle", 24)
    (out,) = call(
        last_kernel, [shape(8, 128, 128)],
        [WIDE] * 4 + [TABLE] * 2 + COARSE_SCRATCH, 1,
        [pos, *gather_level1(f1), fm, fs, vm, vs], "last", 24)
    return out


def solution(mesh):
    return jax.shard_map(
        per_device,
        mesh=mesh,
        in_specs=(P(None, "gx", "gy", "gz"), P("gx", "gy", "gz"), P()),
        out_specs=P("gx", "gy", "gz"),
        check_vma=False,
    )
```

```python
import jax
import jax.numpy as jnp
from jax import lax
from jax.experimental import pallas as pl
from jax.experimental.pallas import tpu as pltpu
from jax.sharding import PartitionSpec as P

FILTER_COEF = 36.0
DAMPING = 0.95
S0 = FILTER_COEF
S1 = FILTER_COEF / 4.0
S2 = FILTER_COEF / 16.0
KEEP = 1.0 - DAMPING
HIGH = lax.Precision.HIGHEST
F32 = jnp.float32
BF16 = jnp.bfloat16

PL0, R0 = 24, 160
PL1, R1 = 42, 128
R2 = 72


def iota(shape, dim):
    return lax.broadcasted_iota(jnp.int32, shape, dim)


def next_lane(value):
    return pltpu.roll(value, 127, 1)


def prev_lane(value):
    return pltpu.roll(value, 1, 1)


def axis_count(place, total):
    return jnp.where(place > 0, 1.0, 0.0) + jnp.where(place < total - 1, 1.0, 0.0)


def planes(start, count, unroll, body):
    step = max(u for u in range(1, unroll + 1) if count % u == 0)
    if step == count:
        for j in range(count):
            body(start + j, j)
        return

    def block(k, carry):
        for j in range(step):
            body(start + k * step + j, j)
        return carry

    lax.fori_loop(0, count // step, block, 0)


def make_tables(weight, diag, rows, row_off, lane_place, lane_ok, base_y, base_z, total, scale):
    y = iota((rows, 128), 0) - row_off + base_y
    z = lane_place + base_z
    inside = lane_ok & (y >= 0) & (y < total) & (z >= 0) & (z < total)
    count = axis_count(y, total) + axis_count(z, total)
    weight[0] = jnp.zeros((rows, 128), F32)
    for i in (1, 2):
        value = 1.0 + scale * (count + float(i))
        weight[i] = jnp.where(inside, DAMPING / value, 0.0)
        if diag is not None:
            diag[i] = value


def x_index(place, total):
    edge = (place == 0) | (place == total - 1)
    out = (place < 0) | (place >= total)
    return jnp.where(out, 0, jnp.where(edge, 1, 2))


def side_place(lane):
    return jnp.where(lane < 64, lane + 128, lane - 128)


def level1_place(lane):
    return jnp.where(lane < 96, lane, lane - 128)


def level1_ok(place):
    return (place >= -22) & (place < 86)


def half(place):
    return lax.shift_right_arithmetic(place, 1)


def hits(cond):
    return jnp.where(cond, 1.0, 0.0)


def level0_place(index):
    side = index - 128
    ok = (index < 128) | (side < 8) | (side >= 120)
    return jnp.where(index < 128, index, side_place(side)), ok


def setup_kernel(pos, wm, ws, dm, w1, d1, w2, t0, t1, r0, tr0, dd, tdd, uu, up0):
    gy, gz = pos[1], pos[2]
    lane = iota((R0, 128), 1)
    make_tables(wm, dm, R0, 16, lane, lane >= 0, gy * 128, gz * 128, 512, S0)
    ok = (lane < 8) | (lane >= 120)
    make_tables(ws, None, R0, 16, side_place(lane), ok, gy * 128, gz * 128, 512, S0)
    z = level1_place(iota((R1, 128), 1))
    make_tables(w1, d1, R1, 32, z, level1_ok(z), gy * 64, gz * 64, 256, S1)

    lane = iota((R2, 128), 1)
    part = jnp.bitwise_and(lane, 63)
    y, z = iota((R2, 128), 0) - 20 + gy * 32, part - 11 + gz * 32
    inside = (part < 54) & (y >= 0) & (y < 128) & (z >= 0) & (z < 128)
    count = axis_count(y, 128) + axis_count(z, 128)
    for i in range(3):
        edge = {0: lane < 64, 1: lane < 0, 2: lane >= 64}[i]
        value = 1.0 + S2 * (count + jnp.where(edge, 1.0, 2.0))
        w2[i] = jnp.where(inside, DAMPING / value, 0.0)

    src, dst = iota((256, 256), 0), iota((256, 256), 1)
    step = jnp.bitwise_and(src - dst, 255)
    t0[...] = hits((step == 1) | (step == 255)).astype(BF16)
    src, dst = iota((256, 128), 0), iota((256, 128), 1)
    step = jnp.bitwise_and(src - dst, 127)
    t1[...] = hits((step == 1) | (step == 127)).astype(BF16)

    col = jnp.where(dst < 64, dst, dst - 64)
    good = (dst < 86) | (dst >= 106)
    z, ok = level0_place(src)
    total = jnp.zeros((256, 128), F32)
    for dz in (-1, 1):
        total = total + hits(ok & good & (z + dz >= 0) & (z + dz < 128) & (half(z + dz) == col))
    tr0[...] = 0.125 * total
    r0[...] = 0.125 * hits(good & (half(src) == col) & (src < 128))[0:128]

    z = level1_place(jnp.bitwise_and(src, 127))
    part = jnp.bitwise_and(dst, 63)
    good = (part < 54) & ((src < 128) == (dst < 64))
    dd[...] = 0.125 * hits(good & level1_ok(z) & (half(z) == part - 11))
    total = jnp.zeros((256, 128), F32)
    for dz in (-1, 1):
        total = total + hits(good & level1_ok(z + dz) & (half(z + dz) == part - 11))
    tdd[...] = 0.125 * total

    src, dst = iota((128, 256), 0), iota((128, 256), 1)
    z = level1_place(jnp.bitwise_and(dst, 127))
    part = jnp.bitwise_and(src, 63)
    good = (part < 54) & ((dst < 128) == (src < 64))
    uu[...] = hits(good & level1_ok(z) & (half(z) == part - 11))
    z, ok = level0_place(dst)
    up0[...] = hits(ok & (half(z) == level1_place(src)))


def two_parts(value):
    top = value.astype(BF16)
    return top, (value - top.astype(F32)).astype(BF16)


def level0_sweep(pos, src, dst, fm, fs, wm, ws, t0, first, last, side):
    lane = iota((144, 128), 1)
    rows, up, dn = pl.ds(8, 144), pl.ds(7, 144), pl.ds(9, 144)

    def body(p, j):
        i = x_index(pos[0] * 8 + p - 8, 64)
        m, s = src[0][p, rows], src[1][p, rows]
        if j % 2:
            a, b = two_parts(jnp.concatenate([m, s], axis=1))
            near = jnp.dot(a, t0[...], preferred_element_type=F32)
            near = near + jnp.dot(b, t0[...], preferred_element_type=F32)
            near_m, near_s = near[:, :128], near[:, 128:]
        else:
            mr, sr, ml, sl = next_lane(m), next_lane(s), prev_lane(m), prev_lane(s)
            near_m = jnp.where(lane == 127, sr, mr) + jnp.where(lane == 0, sl, ml)
            near_s = jnp.where(lane == 127, mr, sr) + jnp.where(lane == 0, ml, sl)
        tot = src[0][p - 1, rows] + src[0][p + 1, rows] + src[0][p, up] + src[0][p, dn]
        dst[0][p, rows] = KEEP * m + wm[i, rows] * (fm[p, rows] + S0 * (tot + near_m))
        if side:
            tot = src[1][p - 1, rows] + src[1][p + 1, rows] + src[1][p, up] + src[1][p, dn]
            dst[1][p, rows] = KEEP * s + ws[i, rows] * (fs[p, rows] + S0 * (tot + near_s))

    planes(first, last + 1 - first, 10, body)


def level0_restrict(pos, src, fm, dm, r0, tr0, tmp, out):
    rows, up, dn = pl.ds(16, 128), pl.ds(15, 128), pl.ds(17, 128)

    def body(k, j):
        sums = [None, None, None]
        for q in (0, 1):
            p = 8 + 2 * k + q
            i = x_index(pos[0] * 8 + p - 8, 64)
            m = src[0][p, rows]
            tot = src[0][p - 1, rows] + src[0][p + 1, rows] + src[0][p, up] + src[0][p, dn]
            parts = (fm[p, rows] + S0 * tot - dm[i, rows] * m, m, src[1][p, rows])
            sums = [v if t is None else t + v for t, v in zip(sums, parts)]
        pairs = []
        for n in range(3):
            tmp[3 * k + n] = sums[n]
            pairs.append(tmp[3 * k + n, pl.ds(0, 64, stride=2)] + tmp[3 * k + n, pl.ds(1, 64, stride=2)])
        value = jnp.dot(pairs[0], r0[...], precision=HIGH, preferred_element_type=F32)
        near = jnp.concatenate(pairs[1:], axis=1)
        near = jnp.dot(near, tr0[...], precision=HIGH, preferred_element_type=F32)
        out[k] = value + S0 * near

    planes(0, 4, 4, body)


def level1_sweep(src, dst, f, w, t1, first, count):
    mid, up, dn = pl.ds(8, 112), pl.ds(7, 112), pl.ds(9, 112)

    def body(p, j):
        i = x_index(p - 5, 32)
        m = src[p, mid]
        if j % 2:
            near = jnp.concatenate(two_parts(m), axis=1)
            near = jnp.dot(near, t1[...], preferred_element_type=F32)
        else:
            near = next_lane(m) + prev_lane(m)
        tot = src[p - 1, mid] + src[p + 1, mid] + src[p, up] + src[p, dn] + near
        dst[p, mid] = KEEP * m + w[i, mid] * (f[p, mid] + S1 * tot)

    planes(first, count, 16, body)


def level2_sweep(src, dst, f, w):
    lane = iota((56, 128), 1)
    mid, up, dn = pl.ds(8, 56), pl.ds(7, 56), pl.ds(9, 56)
    for p in range(1, 9):
        m = src[p, mid]
        if p == 1:
            before = jnp.where(lane >= 64, pltpu.roll(src[8, mid], 64, 1), 0.0)
        else:
            before = src[p - 1, mid]
        if p == 8:
            after = jnp.where(lane < 64, pltpu.roll(src[1, mid], 64, 1), 0.0)
        else:
            after = src[p + 1, mid]
        tot = before + after + src[p, up] + src[p, dn] + next_lane(m) + prev_lane(m)
        dst[p, mid] = KEEP * m + w[{1: 0, 8: 2}.get(p, 1), mid] * (f[p, mid] + S2 * tot)


def coarse_levels(pos, blocks, tables, f1, va, vb, f2, a2, b2, tmp):
    w1, d1, w2, t1, dd, tdd, uu = tables
    gx = pos[0]
    zero = jnp.zeros((R1, 128), F32)
    for p in list(range(0, 5)) + list(range(37, 42)):
        f1[p] = zero
        va[p] = zero
        vb[p] = zero
    for p in range(5, 37):
        for ref in (va, vb):
            ref[p, pl.ds(0, 8)] = jnp.zeros((8, 128), F32)
            ref[p, pl.ds(120, 8)] = jnp.zeros((8, 128), F32)
    for ref in (a2, b2):
        for p in range(1, 9):
            ref[p, pl.ds(0, 8)] = jnp.zeros((8, 128), F32)
            ref[p, pl.ds(64, 8)] = jnp.zeros((8, 128), F32)

    for m in range(4):
        for q in range(2):
            block = blocks[2 * m + q]
            own = gx if q == 0 else jnp.bitwise_xor(gx, 1)
            place = jnp.bitwise_and(own + 8 - 2 * m, 7)
            for j in range(4):
                p = 5 + 4 * place + j
                i = x_index(4 * place + j, 32)
                value = block[j]
                f1[p, pl.ds(8, 112)] = value
                va[p, pl.ds(8, 112)] = w1[i, pl.ds(8, 112)] * value

    level1_sweep(va, vb, f1, w1, t1, 5, 32)

    def residual(k):
        mid = pl.ds(8, 112)
        sums = [None, None]
        for q in (0, 1):
            p = 5 + 2 * k + q
            i = x_index(p - 5, 32)
            m = vb[p, mid]
            tot = vb[p - 1, mid] + vb[p + 1, mid] + vb[p, pl.ds(7, 112)] + vb[p, pl.ds(9, 112)]
            parts = (f1[p, mid] + S1 * tot - d1[i, mid] * m, m)
            sums = [v if t is None else t + v for t, v in zip(sums, parts)]
        pairs = []
        for n in range(2):
            tmp[2 * k + n, pl.ds(0, 112)] = sums[n]
            pairs.append(tmp[2 * k + n, pl.ds(0, 56, stride=2)] + tmp[2 * k + n, pl.ds(1, 56, stride=2)])
        return pairs

    def restrict(p, j):
        low, high = residual(p - 1), residual(p + 7)
        value = jnp.dot(jnp.concatenate([low[0], high[0]], axis=1), dd[...],
                        precision=HIGH, preferred_element_type=F32)
        near = jnp.dot(jnp.concatenate([low[1], high[1]], axis=1), tdd[...],
                       precision=HIGH, preferred_element_type=F32)
        value = value + S1 * near
        f2[p, pl.ds(8, 56)] = value
        i = jnp.where(p == 1, 0, jnp.where(p == 8, 2, 1))
        a2[p, pl.ds(8, 56)] = w2[i, pl.ds(8, 56)] * value

    planes(1, 8, 8, restrict)

    src2, dst2 = a2, b2
    for _ in range(7):
        level2_sweep(src2, dst2, f2, w2)
        src2, dst2 = dst2, src2

    def prolong(p, j):
        both = jnp.dot(src2[p, pl.ds(8, 56)], uu[...], precision=HIGH, preferred_element_type=F32)
        for n, k in ((0, p - 1), (1, p + 7)):
            e = both[:, 128 * n:128 * n + 128]
            for q in (0, 1):
                for h in (0, 1):
                    rows = pl.ds(8 + h, 56, stride=2)
                    vb[5 + 2 * k + q, rows] = vb[5 + 2 * k + q, rows] + e

    planes(1, 8, 8, prolong)
    level1_sweep(vb, va, f1, w1, t1, 4 * gx + 1, 12)
    level1_sweep(va, vb, f1, w1, t1, 4 * gx + 2, 10)


def level0_prolong(pos, e1, up0, old, new, first, last):
    def body(k, j):
        e = e1[4 * pos[0] + 1 + k, pl.ds(28, 72)]
        e = jnp.dot(e, up0[...], precision=HIGH, preferred_element_type=F32)
        for q in (0, 1):
            p = 2 * k + q
            for h in (0, 1):
                rows = pl.ds(8 + h, 72, stride=2)
                new[0][p, rows] = old[0][p, rows] + e[:, :128]
                new[1][p, rows] = old[1][p, rows] + e[:, 128:]

    planes(first // 2, last // 2 + 1 - first // 2, 10, body)


def zero_pads(refs, first, last):
    zero = jnp.zeros((8, 128), F32)
    for ref in refs:
        for p in range(first, last + 1):
            ref[p, pl.ds(0, 8)] = zero
            ref[p, pl.ds(152, 8)] = zero


def rim_kernel(u, cols, rows):
    lane = iota((128, 128), 1)
    acc = jnp.zeros((128, 128), F32)
    for d in range(3):
        for x in range(8):
            k = 8 * d + x
            value = u[d, x]
            acc = jnp.where(lane == k, pltpu.roll(value, k, 1) if k else value, acc)
            rows[pl.ds(k, 1)] = u[d, x, pl.ds(0, 1)]
    cols[...] = acc


def form_matrix(stiff, high, low):
    r, c = iota((192, 24), 0), iota((192, 24), 1)
    wide = jnp.where(lax.shift_right_logical(r, 3) == c, 1.0, 0.0)
    r, c = iota((24, 192), 0), iota((24, 192), 1)
    tall = jnp.where(lax.shift_right_logical(c, 3) == r, 1.0, 0.0)
    full = jnp.dot(wide, stiff, precision=HIGH, preferred_element_type=F32)
    full = jnp.dot(full, tall, precision=HIGH, preferred_element_type=F32)
    r, c = iota((192, 192), 0), iota((192, 192), 1)
    full = jnp.where(jnp.bitwise_and(r, 7) == jnp.bitwise_and(c, 7), full, 0.0)
    top = full.astype(BF16)
    high[...] = top
    low[...] = (full - top.astype(F32)).astype(BF16)


def energy_group(u0, u1, high, low, rho, f, x, y, x_in, x_out):
    cols = []
    for q in range(4):
        val = []
        for ref in (u0, u1):
            for b in (0, 1):
                for a in (0, 1):
                    for d in range(3):
                        val.append(ref[9 * d + x + a, pl.ds(y + 8 * q + b, 8)])
        cols.append(jnp.concatenate(val, axis=0))
    u = jnp.concatenate(cols, axis=1)
    top = u.astype(BF16)
    pushed = jnp.dot(high[...], top, preferred_element_type=F32)
    pushed = pushed + jnp.dot(low[...], top, preferred_element_type=F32)
    prod = pushed * (u + (u - top.astype(F32)))
    energy = prod[0:8]
    for i in range(1, 24):
        energy = energy + prod[8 * i:8 * i + 8]
    for q in range(4):
        rows = pl.ds(y + 8 * q, 8)
        r = rho[x_in, rows]
        f[x_out, rows] = -3.0 * r * r * energy[:, 128 * q:128 * q + 128]


def energy_first(pos, stiff, u, zrim, rho, u0, u1, high, low, f):
    keep_z = jnp.where(pos[2] < 3, 1.0, 0.0)
    form_matrix(stiff[...], high, low)
    lane = iota((128, 128), 1)
    col = zrim[...] * keep_z
    for d in range(3):
        for x in range(8):
            k, q = 8 * d + x, 9 * d + x
            body = u[d, x]
            u0[q] = body
            u1[q] = jnp.where(lane == 127, pltpu.roll(col, 127 - k, 1), next_lane(body))

    def group(c, j):
        x = c // 3
        y = pl.multiple_of((c - 3 * x) * 32, 32)
        energy_group(u0, u1, high, low, rho, f, x, y, x, x)

    planes(0, 12, 4, group)


def energy_second(u0, u1, high, low, rho, f):
    def group(c, j):
        x = c // 3
        y = pl.multiple_of((c - 3 * x) * 32, 32)
        energy_group(u0, u1, high, low, rho, f, x + 4, y, x + 4, x)

    planes(0, 9, 3, group)


def energy_last(pos, u0, u1, high, low, rho, xface, yrim, zrim, xrim, fa, fb, f, lead, tail, pack, w0, w1):
    gx, gy, gz = pos[0], pos[1], pos[2]
    keep_x = jnp.where(gx < 7, 1.0, 0.0)
    keep_y = jnp.where(gy < 3, 1.0, 0.0)
    keep_z = jnp.where(gz < 3, 1.0, 0.0)
    lane = iota((128, 128), 1)
    lane8 = iota((8, 128), 1)
    for d in range(3):
        for x in range(9):
            k, q = 8 * d + x, 9 * d + x
            if x < 8:
                rows = pl.ds(0, 128) if x == 7 else pl.ds(96, 32)
                w0[q, rows] = u0[q, rows]
                w1[q, rows] = u1[q, rows]
                row = yrim[pl.ds(k, 1)]
                corner = yrim[pl.ds(24, 8)]
            else:
                k = 8 * d
                body = xface[d] * keep_x
                col = xrim[pl.ds(32, 128)] * (keep_x * keep_z)
                w0[q, pl.ds(0, 128)] = body
                w1[q, pl.ds(0, 128)] = jnp.where(
                    lane == 127, pltpu.roll(col, 127 - k, 1), next_lane(body))
                row = xrim[pl.ds(k, 1)] * keep_x
                corner = xrim[pl.ds(24, 8)] * keep_x
            row = jnp.broadcast_to(row, (8, 128)) * keep_y
            corner = jnp.broadcast_to(corner[0:1], (8, 128)) * (keep_y * keep_z)
            w0[q, pl.ds(128, 8)] = row
            w1[q, pl.ds(128, 8)] = jnp.where(
                lane8 == 127, pltpu.roll(corner, 127 - k, 1), next_lane(row))
    for x in range(4):
        f[x, pl.ds(0, 96)] = fa[x, pl.ds(0, 96)]
    for x in range(3):
        f[4 + x, pl.ds(0, 96)] = fb[x, pl.ds(0, 96)]
    for x in range(7):
        energy_group(w0, w1, high, low, rho, f, x, 96, x, x)
    for q in range(4):
        energy_group(w0, w1, high, low, rho, f, 7, 32 * q, 7, 7)
    acc = jnp.zeros((128, 128), F32)
    for x in range(8):
        value = f[x]
        if x < 7:
            lead[x] = value
        if x > 0:
            tail[x - 1] = value
        low_z = pltpu.roll(value, 8 * x, 1) if x else value
        acc = jnp.where((lane >= 8 * x) & (lane < 8 * x + 8), low_z, acc)
        high_z = pltpu.roll(value, (8 * x + 72) % 128, 1)
        acc = jnp.where((lane >= 64 + 8 * x) & (lane < 72 + 8 * x), high_z, acc)
    pack[...] = acc


def spread(value, x):
    lane = iota(value.shape, 1)
    low = pltpu.roll(value, (128 - 8 * x) % 128, 1) if x else value
    high = pltpu.roll(value, (56 - 8 * x) % 128, 1)
    return jnp.where(lane < 64, low, high)


def first_kernel(pos, fl, fc, fr, hl, hc, hr, wm, ws, dm, t0, r0, tr0,
                 fm, fs, vm, vs, out, am, as_, tmp):
    zero_pads((fm, fs, vm, vs, am, as_), 1, 22)
    for b, (blk, halo) in enumerate(((fl, hl), (fc, hc), (fr, hr))):
        for x in range(1 if b == 0 else 0, 7 if b == 2 else 8):
            p = 8 * b + x
            i = x_index(pos[0] * 8 + p - 8, 64)
            parts = (
                (8, 8, halo[pl.ds(8 * x, 8)], spread(halo[pl.ds(64, 8)], x)),
                (16, 128, blk[x - 1 if b == 0 else x], spread(halo[pl.ds(144, 128)], x)),
                (144, 8, halo[pl.ds(72 + 8 * x, 8)], spread(halo[pl.ds(136, 8)], x)),
            )
            for start, size, main, side in parts:
                rows = pl.ds(start, size)
                fm[p, rows] = main
                fs[p, rows] = side
                am[p, rows] = wm[i, rows] * main
                as_[p, rows] = ws[i, rows] * side
    level0_sweep(pos, (am, as_), (vm, vs), fm, fs, wm, ws, t0, 2, 21, True)
    level0_restrict(pos, (vm, vs), fm, dm, r0, tr0, tmp, out)


def middle_kernel(pos, *refs):
    blocks, tables = refs[:8], refs[8:15]
    up0, wm, ws, dm, t0, r0, tr0, fm, fs, vm, vs, om, os_, out = refs[15:29]
    am, as_, bm, bs, f1, va, vb, f2, a2, b2, tmp = refs[29:]
    zero_pads((am, as_, bm, bs, om, os_), 2, 21)
    coarse_levels(pos, blocks, tables, f1, va, vb, f2, a2, b2, tmp)
    level0_prolong(pos, vb, up0, (vm, vs), (am, as_), 2, 21)
    level0_sweep(pos, (am, as_), (bm, bs), fm, fs, wm, ws, t0, 3, 20, True)
    level0_sweep(pos, (bm, bs), (am, as_), fm, fs, wm, ws, t0, 4, 19, True)
    level0_sweep(pos, (am, as_), (bm, bs), fm, fs, wm, ws, t0, 5, 18, True)
    level0_sweep(pos, (bm, bs), (om, os_), fm, fs, wm, ws, t0, 6, 17, True)
    level0_restrict(pos, (om, os_), fm, dm, r0, tr0, tmp, out)


def last_kernel(pos, *refs):
    blocks, tables = refs[:8], refs[8:15]
    up0, wm, ws, t0, fm, fs, vm, vs, out = refs[15:24]
    am, as_, bm, bs, f1, va, vb, f2, a2, b2, tmp = refs[24:]
    zero_pads((am, as_, bm, bs), 6, 17)
    coarse_levels(pos, blocks, tables, f1, va, vb, f2, a2, b2, tmp)
    level0_prolong(pos, vb, up0, (vm, vs), (am, as_), 6, 17)
    level0_sweep(pos, (am, as_), (bm, bs), fm, fs, wm, ws, t0, 7, 16, True)
    level0_sweep(pos, (bm, bs), (am, as_), fm, fs, wm, ws, t0, 8, 15, False)
    for x in range(8):
        out[x] = am[8 + x, pl.ds(16, 128)]


SMEM = pl.BlockSpec(memory_space=pltpu.SMEM)
VM = pl.BlockSpec(memory_space=pltpu.VMEM)


def shape(*dims):
    return jax.ShapeDtypeStruct(dims, F32)


def vmem(*dims):
    return pltpu.VMEM(dims, F32)


def call(kernel, outs, scratch, scalars, args, name, limit=12):
    specs = [SMEM] * scalars + [VM] * (len(args) - scalars)
    return pl.pallas_call(
        kernel,
        out_shape=outs,
        in_specs=specs,
        out_specs=[VM] * len(outs),
        scratch_shapes=scratch,
        compiler_params=pltpu.CompilerParams(vmem_limit_bytes=limit << 20),
        name=name,
    )(*args)


def shifted(value, axis, step):
    size = lax.axis_size(axis)
    return lax.ppermute(value, axis, [(i, (i + step) % size) for i in range(size)])


def swapped(value):
    return lax.ppermute(value, "gx", [(i, i ^ 1) for i in range(lax.axis_size("gx"))])


COARSE_SCRATCH = [
    vmem(PL1, R1, 128), vmem(PL1, R1, 128), vmem(PL1, R1, 128),
    vmem(10, R2, 128), vmem(10, R2, 128), vmem(10, R2, 128), vmem(32, 128, 128),
]
WIDE = vmem(PL0, R0, 128)


def gather_level1(own):
    lane = lax.broadcasted_iota(jnp.int32, own.shape, 2)
    right, left = shifted(own, "gz", -1), shifted(own, "gz", 1)
    own = jnp.where(lane < 64, own, jnp.where(lane < 96, right, left))
    low, high = shifted(own[:, 40:], "gy", 1), shifted(own[:, :24], "gy", -1)
    own = jnp.concatenate([low, own, high], axis=1)
    blocks = []
    for m in range(4):
        part = own if m == 0 else shifted(own, "gx", 2 * m)
        blocks += [part, swapped(part)]
    return blocks


def per_device(u, rho, stiff):
    pos = jnp.stack([lax.axis_index(a) for a in ("gx", "gy", "gz")]).astype(jnp.int32)
    t = shape(3, R0, 128)
    wm, ws, dm, w1, d1, w2, t0, t1, r0, tr0, dd, tdd, uu, up0 = call(
        setup_kernel,
        [t, t, t, shape(3, R1, 128), shape(3, R1, 128), shape(3, R2, 128),
         jax.ShapeDtypeStruct((256, 256), BF16), jax.ShapeDtypeStruct((256, 128), BF16),
         shape(128, 128), shape(256, 128), shape(256, 128), shape(256, 128),
         shape(128, 256), shape(128, 256)], [], 1, [pos], "setup")
    cols, rows = call(rim_kernel, [shape(128, 128), shape(24, 128)], [], 0, [u], "rims")
    xface = shifted(u[:, 0], "gx", -1)
    zrim = shifted(cols, "gz", -1)
    yrim = shifted(jnp.concatenate([rows, zrim[:8]], axis=0), "gy", -1)
    mat = jax.ShapeDtypeStruct((192, 192), BF16)
    u0, u1, high, low, fa = call(
        energy_first, [shape(27, 128, 128), shape(27, 128, 128), mat, mat, shape(4, 128, 128)],
        [], 1, [pos, stiff, u, zrim, rho], "energy_first")
    yrim, fa = lax.optimization_barrier((yrim, fa))
    xrim = shifted(jnp.concatenate([yrim, zrim], axis=0), "gx", -1)
    (fb,) = call(
        energy_second, [shape(3, 128, 128)], [], 0, [u0, u1, high, low, rho], "energy_second")
    f, lead, tail, pack = call(
        energy_last, [shape(8, 128, 128), shape(7, 128, 128), shape(7, 128, 128), shape(128, 128)],
        [vmem(27, 136, 128), vmem(27, 136, 128)], 1,
        [pos, u0, u1, high, low, rho, xface, yrim, zrim, xrim, fa, fb], "energy_last")

    fl, fr = shifted(tail, "gx", 1), shifted(lead, "gx", -1)
    lane = lax.broadcasted_iota(jnp.int32, pack.shape, 1)
    z = jnp.where(lane < 64, shifted(pack, "gz", -1), shifted(pack, "gz", 1))
    up = jnp.concatenate([f[:, 120:].reshape(64, 128), z[120:]], axis=0)
    down = jnp.concatenate([f[:, :8].reshape(64, 128), z[:8]], axis=0)
    h = jnp.concatenate([shifted(up, "gy", 1), shifted(down, "gy", -1), z], axis=0)
    hl, hr = shifted(h, "gx", 1), shifted(h, "gx", -1)

    wide = shape(PL0, R0, 128)
    fm, fs, vm, vs, f1 = call(
        first_kernel, [wide, wide, wide, wide, shape(4, 64, 128)],
        [WIDE, WIDE, vmem(12, 128, 128)], 1,
        [pos, fl, f, fr, hl, h, hr, wm, ws, dm, t0, r0, tr0], "first")
    tables = [w1, d1, w2, t1, dd, tdd, uu, up0]
    vm, vs, f1 = call(
        middle_kernel, [wide, wide, shape(4, 64, 128)], [WIDE] * 4 + COARSE_SCRATCH, 1,
        [pos, *gather_level1(f1), *tables, wm, ws, dm, t0, r0, tr0, fm, fs, vm, vs], "middle", 24)
    (out,) = call(
        last_kernel, [shape(8, 128, 128)], [WIDE] * 4 + COARSE_SCRATCH, 1,
        [pos, *gather_level1(f1), *tables, wm, ws, t0, fm, fs, vm, vs], "last", 24)
    return out


def solution(mesh):
    return jax.shard_map(
        per_device,
        mesh=mesh,
        in_specs=(P(None, "gx", "gy", "gz"), P("gx", "gy", "gz"), P()),
        out_specs=P("gx", "gy", "gz"),
        check_vma=False,
    )
```

```python
import jax
import jax.numpy as jnp
from jax import lax
from jax.experimental import pallas as pl
from jax.experimental.pallas import tpu as pltpu
from jax.sharding import PartitionSpec as P

FILTER_COEF = 36.0
DAMPING = 0.95
S0 = FILTER_COEF
S1 = FILTER_COEF / 4.0
S2 = FILTER_COEF / 16.0
KEEP = 1.0 - DAMPING
HIGH = lax.Precision.HIGHEST
F32 = jnp.float32
BF16 = jnp.bfloat16

PL0, R0 = 24, 160
PL1, R1 = 42, 128
R2 = 72


def iota(shape, dim):
    return lax.broadcasted_iota(jnp.int32, shape, dim)


def next_lane(value):
    return pltpu.roll(value, 127, 1)


def prev_lane(value):
    return pltpu.roll(value, 1, 1)


def axis_count(place, total):
    return jnp.where(place > 0, 1.0, 0.0) + jnp.where(place < total - 1, 1.0, 0.0)


def planes(start, count, unroll, body):
    step = max(u for u in range(1, unroll + 1) if count % u == 0)
    if step == count:
        for j in range(count):
            body(start + j, j)
        return

    def block(k, carry):
        for j in range(step):
            body(start + k * step + j, j)
        return carry

    lax.fori_loop(0, count // step, block, 0)


def make_tables(weight, diag, rows, row_off, lane_place, lane_ok, base_y, base_z, total, scale):
    y = iota((rows, 128), 0) - row_off + base_y
    z = lane_place + base_z
    inside = lane_ok & (y >= 0) & (y < total) & (z >= 0) & (z < total)
    count = axis_count(y, total) + axis_count(z, total)
    weight[0] = jnp.zeros((rows, 128), F32)
    for i in (1, 2):
        value = 1.0 + scale * (count + float(i))
        weight[i] = jnp.where(inside, DAMPING / value, 0.0)
        if diag is not None:
            diag[i] = value


def x_index(place, total):
    edge = (place == 0) | (place == total - 1)
    out = (place < 0) | (place >= total)
    return jnp.where(out, 0, jnp.where(edge, 1, 2))


def side_place(lane):
    return jnp.where(lane < 64, lane + 128, lane - 128)


def level1_place(lane):
    return jnp.where(lane < 96, lane, lane - 128)


def level1_ok(place):
    return (place >= -22) & (place < 86)


def half(place):
    return lax.shift_right_arithmetic(place, 1)


def hits(cond):
    return jnp.where(cond, 1.0, 0.0)


def level0_place(index):
    side = index - 128
    ok = (index < 128) | (side < 8) | (side >= 120)
    return jnp.where(index < 128, index, side_place(side)), ok


def setup_kernel(pos, wm, ws, dm, w1, d1, w2, t0, t1, r0, tr0, dd, tdd, uu, up0, zz):
    gy, gz = pos[1], pos[2]
    lane = iota((R0, 128), 1)
    make_tables(wm, dm, R0, 16, lane, lane >= 0, gy * 128, gz * 128, 512, S0)
    ok = (lane < 8) | (lane >= 120)
    make_tables(ws, None, R0, 16, side_place(lane), ok, gy * 128, gz * 128, 512, S0)
    z = level1_place(iota((R1, 128), 1))
    make_tables(w1, d1, R1, 32, z, level1_ok(z), gy * 64, gz * 64, 256, S1)

    lane = iota((R2, 128), 1)
    part = jnp.bitwise_and(lane, 63)
    y, z = iota((R2, 128), 0) - 20 + gy * 32, part - 11 + gz * 32
    inside = (part < 54) & (y >= 0) & (y < 128) & (z >= 0) & (z < 128)
    count = axis_count(y, 128) + axis_count(z, 128)
    for i in range(3):
        edge = {0: lane < 64, 1: lane < 0, 2: lane >= 64}[i]
        value = 1.0 + S2 * (count + jnp.where(edge, 1.0, 2.0))
        w2[i] = jnp.where(inside, DAMPING / value, 0.0)

    src, dst = iota((256, 256), 0), iota((256, 256), 1)
    step = jnp.bitwise_and(src - dst, 255)
    t0[...] = hits((step == 1) | (step == 255)).astype(BF16)
    src, dst = iota((256, 128), 0), iota((256, 128), 1)
    step = jnp.bitwise_and(src - dst, 127)
    t1[...] = hits((step == 1) | (step == 127)).astype(BF16)

    col, good = dst, dst < 64
    z, ok = level0_place(src)
    total = jnp.zeros((256, 128), F32)
    for dz in (-1, 1):
        total = total + hits(ok & good & (z + dz >= 0) & (z + dz < 128) & (half(z + dz) == col))
    tr0[...] = (0.125 * total).astype(BF16)
    r0[...] = (0.125 * hits(good & (half(src) == col) & (src < 128)))[0:128].astype(BF16)

    src5, dst5 = iota((512, 256), 0), iota((512, 256), 1)
    slot = jnp.bitwise_and(dst5, 31)
    same = lax.shift_right_logical(src5, 7) == lax.shift_right_logical(jnp.bitwise_and(dst5, 127), 5)
    edge = src5 == jnp.bitwise_and(src5, 384) + slot + jnp.where(dst5 < 128, 0, 32)
    used = (slot >= jnp.where(dst5 < 128, 0, 10)) & (slot < jnp.where(dst5 < 128, 22, 32))
    zz[...] = hits(same & edge & used).astype(BF16)

    z = level1_place(jnp.bitwise_and(src, 127))
    part = jnp.bitwise_and(dst, 63)
    good = (part < 54) & ((src < 128) == (dst < 64))
    dd[...] = (0.125 * hits(good & level1_ok(z) & (half(z) == part - 11))).astype(BF16)
    total = jnp.zeros((256, 128), F32)
    for dz in (-1, 1):
        total = total + hits(good & level1_ok(z + dz) & (half(z + dz) == part - 11))
    tdd[...] = (0.125 * total).astype(BF16)

    src, dst = iota((128, 256), 0), iota((128, 256), 1)
    z = level1_place(jnp.bitwise_and(dst, 127))
    part = jnp.bitwise_and(src, 63)
    good = (part < 54) & ((dst < 128) == (src < 64))
    uu[...] = hits(good & level1_ok(z) & (half(z) == part - 11)).astype(BF16)
    z, ok = level0_place(dst)
    up0[...] = hits(ok & (half(z) == level1_place(src))).astype(BF16)


def two_parts(value):
    top = value.astype(BF16)
    return top, (value - top.astype(F32)).astype(BF16)


def select(value, matrix):
    top, rest = two_parts(value)
    out = jnp.dot(top, matrix, preferred_element_type=F32)
    return out + jnp.dot(rest, matrix, preferred_element_type=F32)


def level0_sweep(pos, src, dst, fm, fs, wm, ws, t0, first, last, side):
    lane = iota((144, 128), 1)
    rows, up, dn = pl.ds(8, 144), pl.ds(7, 144), pl.ds(9, 144)

    def body(p, j):
        i = x_index(pos[0] * 8 + p - 8, 64)
        m, s = src[0][p, rows], src[1][p, rows]
        if j % 2:
            near = select(jnp.concatenate([m, s], axis=1), t0[...])
            near_m, near_s = near[:, :128], near[:, 128:]
        else:
            mr, sr, ml, sl = next_lane(m), next_lane(s), prev_lane(m), prev_lane(s)
            near_m = jnp.where(lane == 127, sr, mr) + jnp.where(lane == 0, sl, ml)
            near_s = jnp.where(lane == 127, mr, sr) + jnp.where(lane == 0, ml, sl)
        tot = src[0][p - 1, rows] + src[0][p + 1, rows] + src[0][p, up] + src[0][p, dn]
        dst[0][p, rows] = KEEP * m + wm[i, rows] * (fm[p, rows] + S0 * (tot + near_m))
        if side:
            tot = src[1][p - 1, rows] + src[1][p + 1, rows] + src[1][p, up] + src[1][p, dn]
            dst[1][p, rows] = KEEP * s + ws[i, rows] * (fs[p, rows] + S0 * (tot + near_s))

    planes(first, last + 1 - first, 10, body)


def level0_restrict(pos, src, fm, dm, r0, tr0, zz, tmp, out, z_low, z_high):
    rows, up, dn = pl.ds(16, 128), pl.ds(15, 128), pl.ds(17, 128)
    values = []
    for k in range(4):
        sums = [None, None, None]
        for q in (0, 1):
            p = 8 + 2 * k + q
            i = x_index(pos[0] * 8 + p - 8, 64)
            m = src[0][p, rows]
            tot = src[0][p - 1, rows] + src[0][p + 1, rows] + src[0][p, up] + src[0][p, dn]
            parts = (fm[p, rows] + S0 * tot - dm[i, rows] * m, m, src[1][p, rows])
            sums = [v if t is None else t + v for t, v in zip(sums, parts)]
        pairs = []
        for n in range(3):
            tmp[3 * k + n] = sums[n]
            pairs.append(tmp[3 * k + n, pl.ds(0, 64, stride=2)] + tmp[3 * k + n, pl.ds(1, 64, stride=2)])
        near = select(jnp.concatenate(pairs[1:], axis=1), tr0[...])
        values.append(select(pairs[0], r0[...]) + S0 * near)
        out[k] = values[k]
    edges = select(jnp.concatenate(values, axis=1), zz[...])
    z_low[...] = edges[:, :128]
    z_high[...] = edges[:, 128:]


def level1_sweep(src, dst, f, w, t1, first, count):
    mid, up, dn = pl.ds(8, 112), pl.ds(7, 112), pl.ds(9, 112)

    def body(p, j):
        i = x_index(p - 5, 32)
        m = src[p, mid]
        if j % 2:
            near = jnp.concatenate(two_parts(m), axis=1)
            near = jnp.dot(near, t1[...], preferred_element_type=F32)
        else:
            near = next_lane(m) + prev_lane(m)
        tot = src[p - 1, mid] + src[p + 1, mid] + src[p, up] + src[p, dn] + near
        dst[p, mid] = KEEP * m + w[i, mid] * (f[p, mid] + S1 * tot)

    planes(first, count, 16, body)


def level2_sweep(src, dst, f, w):
    lane = iota((56, 128), 1)
    mid, up, dn = pl.ds(8, 56), pl.ds(7, 56), pl.ds(9, 56)
    for p in range(1, 9):
        m = src[p, mid]
        if p == 1:
            before = jnp.where(lane >= 64, pltpu.roll(src[8, mid], 64, 1), 0.0)
        else:
            before = src[p - 1, mid]
        if p == 8:
            after = jnp.where(lane < 64, pltpu.roll(src[1, mid], 64, 1), 0.0)
        else:
            after = src[p + 1, mid]
        tot = before + after + src[p, up] + src[p, dn] + next_lane(m) + prev_lane(m)
        dst[p, mid] = KEEP * m + w[{1: 0, 8: 2}.get(p, 1), mid] * (f[p, mid] + S2 * tot)


def coarse_levels(pos, blocks, tables, f1, va, vb, f2, a2, b2, tmp):
    w1, d1, w2, t1, dd, tdd, uu = tables
    gx = pos[0]
    zero = jnp.zeros((R1, 128), F32)
    for p in list(range(0, 5)) + list(range(37, 42)):
        f1[p] = zero
        va[p] = zero
        vb[p] = zero
    for p in range(5, 37):
        for ref in (va, vb):
            ref[p, pl.ds(0, 8)] = jnp.zeros((8, 128), F32)
            ref[p, pl.ds(120, 8)] = jnp.zeros((8, 128), F32)
    for ref in (a2, b2):
        for p in range(1, 9):
            ref[p, pl.ds(0, 8)] = jnp.zeros((8, 128), F32)
            ref[p, pl.ds(64, 8)] = jnp.zeros((8, 128), F32)

    for m in range(4):
        for q in range(2):
            block = blocks[2 * m + q]
            own = gx if q == 0 else jnp.bitwise_xor(gx, 1)
            place = jnp.bitwise_and(own + 8 - 2 * m, 7)
            for j in range(4):
                p = 5 + 4 * place + j
                i = x_index(4 * place + j, 32)
                value = block[j]
                f1[p, pl.ds(8, 112)] = value
                va[p, pl.ds(8, 112)] = w1[i, pl.ds(8, 112)] * value

    level1_sweep(va, vb, f1, w1, t1, 5, 32)

    def residual(k):
        mid = pl.ds(8, 112)
        sums = [None, None]
        for q in (0, 1):
            p = 5 + 2 * k + q
            i = x_index(p - 5, 32)
            m = vb[p, mid]
            tot = vb[p - 1, mid] + vb[p + 1, mid] + vb[p, pl.ds(7, 112)] + vb[p, pl.ds(9, 112)]
            parts = (f1[p, mid] + S1 * tot - d1[i, mid] * m, m)
            sums = [v if t is None else t + v for t, v in zip(sums, parts)]
        pairs = []
        for n in range(2):
            tmp[2 * k + n, pl.ds(0, 112)] = sums[n]
            pairs.append(tmp[2 * k + n, pl.ds(0, 56, stride=2)] + tmp[2 * k + n, pl.ds(1, 56, stride=2)])
        return pairs

    def restrict(p, j):
        low, high = residual(p - 1), residual(p + 7)
        value = select(jnp.concatenate([low[0], high[0]], axis=1), dd[...])
        value = value + S1 * select(jnp.concatenate([low[1], high[1]], axis=1), tdd[...])
        f2[p, pl.ds(8, 56)] = value
        i = jnp.where(p == 1, 0, jnp.where(p == 8, 2, 1))
        a2[p, pl.ds(8, 56)] = w2[i, pl.ds(8, 56)] * value

    planes(1, 8, 8, restrict)

    src2, dst2 = a2, b2
    for _ in range(7):
        level2_sweep(src2, dst2, f2, w2)
        src2, dst2 = dst2, src2

    def prolong(p, j):
        both = select(src2[p, pl.ds(8, 56)], uu[...])
        for n, k in ((0, p - 1), (1, p + 7)):
            e = both[:, 128 * n:128 * n + 128]
            for q in (0, 1):
                for h in (0, 1):
                    rows = pl.ds(8 + h, 56, stride=2)
                    vb[5 + 2 * k + q, rows] = vb[5 + 2 * k + q, rows] + e

    planes(1, 8, 8, prolong)
    level1_sweep(vb, va, f1, w1, t1, 4 * gx + 1, 12)
    level1_sweep(va, vb, f1, w1, t1, 4 * gx + 2, 10)


def level0_prolong(pos, e1, up0, old, new, first, last):
    def body(k, j):
        e = e1[4 * pos[0] + 1 + k, pl.ds(28, 72)]
        e = select(e, up0[...])
        for q in (0, 1):
            p = 2 * k + q
            for h in (0, 1):
                rows = pl.ds(8 + h, 72, stride=2)
                new[0][p, rows] = old[0][p, rows] + e[:, :128]
                new[1][p, rows] = old[1][p, rows] + e[:, 128:]

    planes(first // 2, last // 2 + 1 - first // 2, 10, body)


def zero_pads(refs, first, last):
    zero = jnp.zeros((8, 128), F32)
    for ref in refs:
        for p in range(first, last + 1):
            ref[p, pl.ds(0, 8)] = zero
            ref[p, pl.ds(152, 8)] = zero


def rim_kernel(u, u0, cols, rows):
    lane = iota((128, 128), 1)
    acc = jnp.zeros((128, 128), F32)
    for d in range(3):
        for x in range(8):
            k = 8 * d + x
            value = u[d, x]
            u0[9 * d + x] = value
            acc = jnp.where(lane == k, pltpu.roll(value, k, 1) if k else value, acc)
            rows[pl.ds(k, 1)] = u[d, x, pl.ds(0, 1)]
    cols[...] = acc


def form_matrix(stiff, high, low):
    r, c = iota((192, 24), 0), iota((192, 24), 1)
    wide = jnp.where(lax.shift_right_logical(r, 3) == c, 1.0, 0.0)
    r, c = iota((24, 192), 0), iota((24, 192), 1)
    tall = jnp.where(lax.shift_right_logical(c, 3) == r, 1.0, 0.0)
    full = jnp.dot(wide, stiff, precision=HIGH, preferred_element_type=F32)
    full = jnp.dot(full, tall, precision=HIGH, preferred_element_type=F32)
    r, c = iota((192, 192), 0), iota((192, 192), 1)
    full = jnp.where(jnp.bitwise_and(r, 7) == jnp.bitwise_and(c, 7), full, 0.0)
    top = full.astype(BF16)
    high[...] = top
    low[...] = (full - top.astype(F32)).astype(BF16)


def energy_group(u0, u1, high, low, rho, f, x, y, x_in, x_out):
    cols = []
    for q in range(4):
        val = []
        for ref in (u0, u1):
            for b in (0, 1):
                for a in (0, 1):
                    for d in range(3):
                        val.append(ref[9 * d + x + a, pl.ds(y + 8 * q + b, 8)])
        cols.append(jnp.concatenate(val, axis=0))
    u = jnp.concatenate(cols, axis=1)
    top = u.astype(BF16)
    pushed = jnp.dot(high[...], top, preferred_element_type=F32)
    pushed = pushed + jnp.dot(low[...], top, preferred_element_type=F32)
    prod = pushed * (u + (u - top.astype(F32)))
    energy = prod[0:8]
    for i in range(1, 24):
        energy = energy + prod[8 * i:8 * i + 8]
    for q in range(4):
        rows = pl.ds(y + 8 * q, 8)
        r = rho[x_in, rows]
        f[x_out, rows] = -3.0 * r * r * energy[:, 128 * q:128 * q + 128]


def energy_first(pos, stiff, u0, zrim, rho, u1, high, low, f):
    keep_z = jnp.where(pos[2] < 3, 1.0, 0.0)
    form_matrix(stiff[...], high, low)
    lane = iota((128, 128), 1)
    col = zrim[...] * keep_z
    for d in range(3):
        for x in range(8):
            k, q = 8 * d + x, 9 * d + x
            u1[q] = jnp.where(lane == 127, pltpu.roll(col, 127 - k, 1), next_lane(u0[q]))

    def group(c, j):
        x = c // 3
        y = pl.multiple_of((c - 3 * x) * 32, 32)
        energy_group(u0, u1, high, low, rho, f, x, y, x, x)

    planes(0, 12, 4, group)


def energy_second(u0, u1, high, low, rho, f):
    def group(c, j):
        x = c // 3
        y = pl.multiple_of((c - 3 * x) * 32, 32)
        energy_group(u0, u1, high, low, rho, f, x + 4, y, x + 4, x)

    planes(0, 9, 3, group)


def energy_last(pos, u0, u1, high, low, rho, xface, yrim, zrim, xrim, fa, fb, f, lead, tail, pack, w0, w1):
    gx, gy, gz = pos[0], pos[1], pos[2]
    keep_x = jnp.where(gx < 7, 1.0, 0.0)
    keep_y = jnp.where(gy < 3, 1.0, 0.0)
    keep_z = jnp.where(gz < 3, 1.0, 0.0)
    lane = iota((128, 128), 1)
    lane8 = iota((8, 128), 1)
    for d in range(3):
        for x in range(9):
            k, q = 8 * d + x, 9 * d + x
            if x < 8:
                rows = pl.ds(0, 128) if x == 7 else pl.ds(96, 32)
                w0[q, rows] = u0[q, rows]
                w1[q, rows] = u1[q, rows]
                row = yrim[pl.ds(k, 1)]
                corner = yrim[pl.ds(24, 8)]
            else:
                k = 8 * d
                body = xface[d] * keep_x
                col = xrim[pl.ds(32, 128)] * (keep_x * keep_z)
                w0[q, pl.ds(0, 128)] = body
                w1[q, pl.ds(0, 128)] = jnp.where(
                    lane == 127, pltpu.roll(col, 127 - k, 1), next_lane(body))
                row = xrim[pl.ds(k, 1)] * keep_x
                corner = xrim[pl.ds(24, 8)] * keep_x
            row = jnp.broadcast_to(row, (8, 128)) * keep_y
            corner = jnp.broadcast_to(corner[0:1], (8, 128)) * (keep_y * keep_z)
            w0[q, pl.ds(128, 8)] = row
            w1[q, pl.ds(128, 8)] = jnp.where(
                lane8 == 127, pltpu.roll(corner, 127 - k, 1), next_lane(row))
    for x in range(4):
        f[x, pl.ds(0, 96)] = fa[x, pl.ds(0, 96)]
    for x in range(3):
        f[4 + x, pl.ds(0, 96)] = fb[x, pl.ds(0, 96)]
    for x in range(7):
        energy_group(w0, w1, high, low, rho, f, x, 96, x, x)
    for q in range(4):
        energy_group(w0, w1, high, low, rho, f, 7, 32 * q, 7, 7)
    acc = jnp.zeros((128, 128), F32)
    for x in range(8):
        value = f[x]
        if x < 7:
            lead[x] = value
        if x > 0:
            tail[x - 1] = value
        here = (lane >= 16 * x) & (lane < 16 * x + 16)
        acc = jnp.where(here, pltpu.roll(value, (16 * x + 8) % 128, 1), acc)
    pack[...] = acc


def spread(value, x):
    return pltpu.roll(value, (248 - 16 * x) % 128, 1)


def first_kernel(pos, fl, fc, fr, hl, hc, hr, wm, ws, dm, t0, r0, tr0, zz,
                 fm, fs, vm, vs, out, z_low, z_high, am, as_, tmp):
    zero_pads((fm, fs, vm, vs, am, as_), 1, 22)
    for b, (blk, halo) in enumerate(((fl, hl), (fc, hc), (fr, hr))):
        for x in range(1 if b == 0 else 0, 7 if b == 2 else 8):
            p = 8 * b + x
            i = x_index(pos[0] * 8 + p - 8, 64)
            parts = (
                (8, 8, halo[pl.ds(8 * x, 8)], spread(halo[pl.ds(64, 8)], x)),
                (16, 128, blk[x - 1 if b == 0 else x], spread(halo[pl.ds(144, 128)], x)),
                (144, 8, halo[pl.ds(72 + 8 * x, 8)], spread(halo[pl.ds(136, 8)], x)),
            )
            for start, size, main, side in parts:
                rows = pl.ds(start, size)
                fm[p, rows] = main
                fs[p, rows] = side
                am[p, rows] = wm[i, rows] * main
                as_[p, rows] = ws[i, rows] * side
    level0_sweep(pos, (am, as_), (vm, vs), fm, fs, wm, ws, t0, 2, 21, True)
    level0_restrict(pos, (vm, vs), fm, dm, r0, tr0, zz, tmp, out, z_low, z_high)


def middle_kernel(pos, *refs):
    blocks, tables = refs[:8], refs[8:15]
    up0, wm, ws, dm, t0, r0, tr0, zz, fm, fs, vm, vs = refs[15:27]
    om, os_, out, z_low, z_high, am, as_, bm, bs, f1, va, vb, f2, a2, b2, tmp = refs[27:]
    zero_pads((am, as_, bm, bs, om, os_), 2, 21)
    coarse_levels(pos, blocks, tables, f1, va, vb, f2, a2, b2, tmp)
    level0_prolong(pos, vb, up0, (vm, vs), (am, as_), 2, 21)
    level0_sweep(pos, (am, as_), (bm, bs), fm, fs, wm, ws, t0, 3, 20, True)
    level0_sweep(pos, (bm, bs), (am, as_), fm, fs, wm, ws, t0, 4, 19, True)
    level0_sweep(pos, (am, as_), (bm, bs), fm, fs, wm, ws, t0, 5, 18, True)
    level0_sweep(pos, (bm, bs), (om, os_), fm, fs, wm, ws, t0, 6, 17, True)
    level0_restrict(pos, (om, os_), fm, dm, r0, tr0, zz, tmp, out, z_low, z_high)


def last_kernel(pos, *refs):
    blocks, tables = refs[:8], refs[8:15]
    up0, wm, ws, t0, fm, fs, vm, vs, out = refs[15:24]
    am, as_, bm, bs, f1, va, vb, f2, a2, b2, tmp = refs[24:]
    zero_pads((am, as_, bm, bs), 6, 17)
    coarse_levels(pos, blocks, tables, f1, va, vb, f2, a2, b2, tmp)
    level0_prolong(pos, vb, up0, (vm, vs), (am, as_), 6, 17)
    level0_sweep(pos, (am, as_), (bm, bs), fm, fs, wm, ws, t0, 7, 16, True)
    level0_sweep(pos, (bm, bs), (am, as_), fm, fs, wm, ws, t0, 8, 15, False)
    for x in range(8):
        out[x] = am[8 + x, pl.ds(16, 128)]


SMEM = pl.BlockSpec(memory_space=pltpu.SMEM)
VM = pl.BlockSpec(memory_space=pltpu.VMEM)


def shape(*dims):
    return jax.ShapeDtypeStruct(dims, F32)


def half_shape(*dims):
    return jax.ShapeDtypeStruct(dims, BF16)


def vmem(*dims):
    return pltpu.VMEM(dims, F32)


def call(kernel, outs, scratch, scalars, args, name, limit=12):
    specs = [SMEM] * scalars + [VM] * (len(args) - scalars)
    return pl.pallas_call(
        kernel,
        out_shape=outs,
        in_specs=specs,
        out_specs=[VM] * len(outs),
        scratch_shapes=scratch,
        compiler_params=pltpu.CompilerParams(vmem_limit_bytes=limit << 20),
        name=name,
    )(*args)


def shifted(value, axis, step):
    size = lax.axis_size(axis)
    return lax.ppermute(value, axis, [(i, (i + step) % size) for i in range(size)])


def swapped(value):
    return lax.ppermute(value, "gx", [(i, i ^ 1) for i in range(lax.axis_size("gx"))])


COARSE_SCRATCH = [
    vmem(PL1, R1, 128), vmem(PL1, R1, 128), vmem(PL1, R1, 128),
    vmem(10, R2, 128), vmem(10, R2, 128), vmem(10, R2, 128), vmem(32, 128, 128),
]
WIDE = vmem(PL0, R0, 128)


def gather_level1(own, z_low, z_high):
    lane = lax.broadcasted_iota(jnp.int32, (64, 128), 1)
    right, left = shifted(z_low, "gz", -1), shifted(z_high, "gz", 1)
    wide = []
    for k in range(4):
        rim = jnp.where(lane < 96, jnp.roll(right, 64 - 32 * k, 1), jnp.roll(left, 96 - 32 * k, 1))
        wide.append(jnp.where(lane < 64, own[k], rim))
    own = jnp.stack(wide)
    low, high = shifted(own[:, 40:], "gy", 1), shifted(own[:, :24], "gy", -1)
    own = jnp.concatenate([low, own, high], axis=1)
    blocks = []
    for m in range(4):
        part = own if m == 0 else shifted(own, "gx", 2 * m)
        blocks += [part, swapped(part)]
    return blocks


def per_device(u, rho, stiff):
    pos = jnp.stack([lax.axis_index(a) for a in ("gx", "gy", "gz")]).astype(jnp.int32)
    t = shape(3, R0, 128)
    wm, ws, dm, w1, d1, w2, t0, t1, r0, tr0, dd, tdd, uu, up0, zz = call(
        setup_kernel,
        [t, t, t, shape(3, R1, 128), shape(3, R1, 128), shape(3, R2, 128),
         half_shape(256, 256), half_shape(256, 128), half_shape(128, 128), half_shape(256, 128),
         half_shape(256, 128), half_shape(256, 128), half_shape(128, 256), half_shape(128, 256),
         half_shape(512, 256)],
        [], 1, [pos], "setup")
    u0, cols, rows = call(
        rim_kernel, [shape(27, 128, 128), shape(128, 128), shape(24, 128)], [], 0, [u], "rims")
    xface = shifted(u[:, 0], "gx", -1)
    zrim = shifted(cols, "gz", -1)
    yrim = shifted(jnp.concatenate([rows, zrim[:8]], axis=0), "gy", -1)
    mat = half_shape(192, 192)
    u1, high, low, fa = call(
        energy_first, [shape(27, 128, 128), mat, mat, shape(4, 128, 128)],
        [], 1, [pos, stiff, u0, zrim, rho], "energy_first")
    yrim, fa = lax.optimization_barrier((yrim, fa))
    xrim = shifted(jnp.concatenate([yrim, zrim], axis=0), "gx", -1)
    (fb,) = call(
        energy_second, [shape(3, 128, 128)], [], 0, [u0, u1, high, low, rho], "energy_second")
    f, lead, tail, pack = call(
        energy_last, [shape(8, 128, 128), shape(7, 128, 128), shape(7, 128, 128), shape(128, 128)],
        [vmem(27, 136, 128), vmem(27, 136, 128)], 1,
        [pos, u0, u1, high, low, rho, xface, yrim, zrim, xrim, fa, fb], "energy_last")

    fl, fr = shifted(tail, "gx", 1), shifted(lead, "gx", -1)
    lane = lax.broadcasted_iota(jnp.int32, pack.shape, 1)
    from_left = jnp.bitwise_and(lane, 15) < 8
    z = jnp.where(from_left, shifted(pack, "gz", 1), shifted(pack, "gz", -1))
    up = jnp.concatenate([f[:, 120:].reshape(64, 128), z[120:]], axis=0)
    down = jnp.concatenate([f[:, :8].reshape(64, 128), z[:8]], axis=0)
    h = jnp.concatenate([shifted(up, "gy", 1), shifted(down, "gy", -1), z], axis=0)
    hl, hr = shifted(h, "gx", 1), shifted(h, "gx", -1)

    wide = shape(PL0, R0, 128)
    level1 = [shape(4, 64, 128), shape(64, 128), shape(64, 128)]
    fm, fs, vm, vs, *f1 = call(
        first_kernel, [wide, wide, wide, wide, *level1],
        [WIDE, WIDE, vmem(12, 128, 128)], 1,
        [pos, fl, f, fr, hl, h, hr, wm, ws, dm, t0, r0, tr0, zz], "first")
    tables = [w1, d1, w2, t1, dd, tdd, uu, up0]
    vm, vs, *f1 = call(
        middle_kernel, [wide, wide, *level1], [WIDE] * 4 + COARSE_SCRATCH, 1,
        [pos, *gather_level1(*f1), *tables, wm, ws, dm, t0, r0, tr0, zz, fm, fs, vm, vs], "middle", 24)
    (out,) = call(
        last_kernel, [shape(8, 128, 128)], [WIDE] * 4 + COARSE_SCRATCH, 1,
        [pos, *gather_level1(*f1), *tables, wm, ws, t0, fm, fs, vm, vs], "last", 24)
    return out


def solution(mesh):
    return jax.shard_map(
        per_device,
        mesh=mesh,
        in_specs=(P(None, "gx", "gy", "gz"), P("gx", "gy", "gz"), P()),
        out_specs=P("gx", "gy", "gz"),
        check_vma=False,
    )
```

```python
import jax
import jax.numpy as jnp
from jax import lax
from jax.experimental import pallas as pl
from jax.experimental.pallas import tpu as pltpu
from jax.sharding import PartitionSpec as P

FILTER_COEF = 36.0
DAMPING = 0.95
S0 = FILTER_COEF
S1 = FILTER_COEF / 4.0
S2 = FILTER_COEF / 16.0
KEEP = 1.0 - DAMPING
HIGH = lax.Precision.HIGHEST
F32 = jnp.float32
BF16 = jnp.bfloat16

PL0, R0 = 24, 160
PL1, R1 = 42, 128
R2 = 72


def iota(shape, dim):
    return lax.broadcasted_iota(jnp.int32, shape, dim)


def next_lane(value):
    return pltpu.roll(value, 127, 1)


def prev_lane(value):
    return pltpu.roll(value, 1, 1)


def axis_count(place, total):
    return jnp.where(place > 0, 1.0, 0.0) + jnp.where(place < total - 1, 1.0, 0.0)


def planes(start, count, unroll, body):
    step = max(u for u in range(1, unroll + 1) if count % u == 0)
    if step == count:
        for j in range(count):
            body(start + j, j)
        return

    def block(k, carry):
        for j in range(step):
            body(start + k * step + j, j)
        return carry

    lax.fori_loop(0, count // step, block, 0)


def make_tables(weight, diag, rows, row_off, lane_place, lane_ok, base_y, base_z, total, scale):
    y = iota((rows, 128), 0) - row_off + base_y
    z = lane_place + base_z
    inside = lane_ok & (y >= 0) & (y < total) & (z >= 0) & (z < total)
    count = axis_count(y, total) + axis_count(z, total)
    weight[0] = jnp.zeros((rows, 128), F32)
    for i in (1, 2):
        value = 1.0 + scale * (count + float(i))
        weight[i] = jnp.where(inside, DAMPING / value, 0.0)
        if diag is not None:
            diag[i] = value


def x_index(place, total):
    edge = (place == 0) | (place == total - 1)
    out = (place < 0) | (place >= total)
    return jnp.where(out, 0, jnp.where(edge, 1, 2))


def side_place(lane):
    return jnp.where(lane < 64, lane + 128, lane - 128)


def level1_place(lane):
    return jnp.where(lane < 96, lane, lane - 128)


def level1_ok(place):
    return (place >= -22) & (place < 86)


def half(place):
    return lax.shift_right_arithmetic(place, 1)


def hits(cond):
    return jnp.where(cond, 1.0, 0.0)


def level0_place(index):
    side = index - 128
    ok = (index < 128) | (side < 8) | (side >= 120)
    return jnp.where(index < 128, index, side_place(side)), ok


def setup_kernel(pos, wm, ws, dm, w1, d1, w2, t0, t1, r0, tr0, dd, tdd, uu, up0, zz):
    gy, gz = pos[1], pos[2]
    lane = iota((R0, 128), 1)
    make_tables(wm, dm, R0, 16, lane, lane >= 0, gy * 128, gz * 128, 512, S0)
    ok = (lane < 8) | (lane >= 120)
    make_tables(ws, None, R0, 16, side_place(lane), ok, gy * 128, gz * 128, 512, S0)
    z = level1_place(iota((R1, 128), 1))
    make_tables(w1, d1, R1, 32, z, level1_ok(z), gy * 64, gz * 64, 256, S1)

    lane = iota((R2, 128), 1)
    part = jnp.bitwise_and(lane, 63)
    y, z = iota((R2, 128), 0) - 20 + gy * 32, part - 11 + gz * 32
    inside = (part < 54) & (y >= 0) & (y < 128) & (z >= 0) & (z < 128)
    count = axis_count(y, 128) + axis_count(z, 128)
    for i in range(3):
        edge = {0: lane < 64, 1: lane < 0, 2: lane >= 64}[i]
        value = 1.0 + S2 * (count + jnp.where(edge, 1.0, 2.0))
        w2[i] = jnp.where(inside, DAMPING / value, 0.0)

    src, dst = iota((256, 256), 0), iota((256, 256), 1)
    step = jnp.bitwise_and(src - dst, 255)
    t0[...] = hits((step == 1) | (step == 255)).astype(BF16)
    src, dst = iota((256, 128), 0), iota((256, 128), 1)
    step = jnp.bitwise_and(src - dst, 127)
    t1[...] = hits((step == 1) | (step == 127)).astype(BF16)

    col, good = dst, dst < 64
    z, ok = level0_place(src)
    total = jnp.zeros((256, 128), F32)
    for dz in (-1, 1):
        total = total + hits(ok & good & (z + dz >= 0) & (z + dz < 128) & (half(z + dz) == col))
    tr0[...] = (0.125 * total).astype(BF16)
    r0[...] = (0.125 * hits(good & (half(src) == col) & (src < 128)))[0:128].astype(BF16)

    src5, dst5 = iota((512, 256), 0), iota((512, 256), 1)
    slot = jnp.bitwise_and(dst5, 31)
    same = lax.shift_right_logical(src5, 7) == lax.shift_right_logical(jnp.bitwise_and(dst5, 127), 5)
    edge = src5 == jnp.bitwise_and(src5, 384) + slot + jnp.where(dst5 < 128, 0, 32)
    used = (slot >= jnp.where(dst5 < 128, 0, 10)) & (slot < jnp.where(dst5 < 128, 22, 32))
    zz[...] = hits(same & edge & used).astype(BF16)

    z = level1_place(jnp.bitwise_and(src, 127))
    part = jnp.bitwise_and(dst, 63)
    good = (part < 54) & ((src < 128) == (dst < 64))
    dd[...] = (0.125 * hits(good & level1_ok(z) & (half(z) == part - 11))).astype(BF16)
    total = jnp.zeros((256, 128), F32)
    for dz in (-1, 1):
        total = total + hits(good & level1_ok(z + dz) & (half(z + dz) == part - 11))
    tdd[...] = (0.125 * total).astype(BF16)

    src, dst = iota((128, 256), 0), iota((128, 256), 1)
    z = level1_place(jnp.bitwise_and(dst, 127))
    part = jnp.bitwise_and(src, 63)
    good = (part < 54) & ((dst < 128) == (src < 64))
    uu[...] = hits(good & level1_ok(z) & (half(z) == part - 11)).astype(BF16)
    z, ok = level0_place(dst)
    up0[...] = hits(ok & (half(z) == level1_place(src))).astype(BF16)


def two_parts(value):
    top = value.astype(BF16)
    return top, (value - top.astype(F32)).astype(BF16)


def select(value, matrix):
    top, rest = two_parts(value)
    out = jnp.dot(top, matrix, preferred_element_type=F32)
    return out + jnp.dot(rest, matrix, preferred_element_type=F32)


def level0_sweep(pos, src, dst, fm, fs, wm, ws, t0, first, last, side):
    lane = iota((144, 128), 1)
    rows, up, dn = pl.ds(8, 144), pl.ds(7, 144), pl.ds(9, 144)

    def body(p, j):
        i = x_index(pos[0] * 8 + p - 8, 64)
        m, s = src[0][p, rows], src[1][p, rows]
        if j % 2:
            near = select(jnp.concatenate([m, s], axis=1), t0[...])
            near_m, near_s = near[:, :128], near[:, 128:]
        else:
            mr, sr, ml, sl = next_lane(m), next_lane(s), prev_lane(m), prev_lane(s)
            near_m = jnp.where(lane == 127, sr, mr) + jnp.where(lane == 0, sl, ml)
            near_s = jnp.where(lane == 127, mr, sr) + jnp.where(lane == 0, ml, sl)
        tot = src[0][p - 1, rows] + src[0][p + 1, rows] + src[0][p, up] + src[0][p, dn]
        dst[0][p, rows] = KEEP * m + wm[i, rows] * (fm[p, rows] + S0 * (tot + near_m))
        if side:
            tot = src[1][p - 1, rows] + src[1][p + 1, rows] + src[1][p, up] + src[1][p, dn]
            dst[1][p, rows] = KEEP * s + ws[i, rows] * (fs[p, rows] + S0 * (tot + near_s))

    planes(first, last + 1 - first, 10, body)


def level0_restrict(pos, src, fm, dm, r0, tr0, zz, tmp, out, z_low, z_high):
    rows, up, dn = pl.ds(16, 128), pl.ds(15, 128), pl.ds(17, 128)
    values = []
    for k in range(4):
        sums = [None, None, None]
        for q in (0, 1):
            p = 8 + 2 * k + q
            i = x_index(pos[0] * 8 + p - 8, 64)
            m = src[0][p, rows]
            tot = src[0][p - 1, rows] + src[0][p + 1, rows] + src[0][p, up] + src[0][p, dn]
            parts = (fm[p, rows] + S0 * tot - dm[i, rows] * m, m, src[1][p, rows])
            sums = [v if t is None else t + v for t, v in zip(sums, parts)]
        pairs = []
        for n in range(3):
            tmp[3 * k + n] = sums[n]
            pairs.append(tmp[3 * k + n, pl.ds(0, 64, stride=2)] + tmp[3 * k + n, pl.ds(1, 64, stride=2)])
        near = select(jnp.concatenate(pairs[1:], axis=1), tr0[...])
        values.append(select(pairs[0], r0[...]) + S0 * near)
        out[k] = values[k]
    edges = select(jnp.concatenate(values, axis=1), zz[...])
    z_low[...] = edges[:, :128]
    z_high[...] = edges[:, 128:]


def level1_sweep(src, dst, f, w, t1, first, count):
    mid, up, dn = pl.ds(8, 112), pl.ds(7, 112), pl.ds(9, 112)

    def body(p, j):
        i = x_index(p - 5, 32)
        m = src[p, mid]
        if j % 2:
            near = jnp.concatenate(two_parts(m), axis=1)
            near = jnp.dot(near, t1[...], preferred_element_type=F32)
        else:
            near = next_lane(m) + prev_lane(m)
        tot = src[p - 1, mid] + src[p + 1, mid] + src[p, up] + src[p, dn] + near
        dst[p, mid] = KEEP * m + w[i, mid] * (f[p, mid] + S1 * tot)

    planes(first, count, 16, body)


def level2_sweep(src, dst, f, w):
    lane = iota((56, 128), 1)
    mid, up, dn = pl.ds(8, 56), pl.ds(7, 56), pl.ds(9, 56)
    for p in range(1, 9):
        m = src[p, mid]
        if p == 1:
            before = jnp.where(lane >= 64, pltpu.roll(src[8, mid], 64, 1), 0.0)
        else:
            before = src[p - 1, mid]
        if p == 8:
            after = jnp.where(lane < 64, pltpu.roll(src[1, mid], 64, 1), 0.0)
        else:
            after = src[p + 1, mid]
        tot = before + after + src[p, up] + src[p, dn] + next_lane(m) + prev_lane(m)
        dst[p, mid] = KEEP * m + w[{1: 0, 8: 2}.get(p, 1), mid] * (f[p, mid] + S2 * tot)


def coarse_levels(pos, blocks, tables, f1, va, vb, f2, a2, b2, tmp):
    w1, d1, w2, t1, dd, tdd, uu = tables
    gx = pos[0]
    zero = jnp.zeros((R1, 128), F32)
    for p in list(range(0, 5)) + list(range(37, 42)):
        f1[p] = zero
        va[p] = zero
        vb[p] = zero
    for p in range(5, 37):
        for ref in (va, vb):
            ref[p, pl.ds(0, 8)] = jnp.zeros((8, 128), F32)
            ref[p, pl.ds(120, 8)] = jnp.zeros((8, 128), F32)
    for ref in (a2, b2):
        for p in range(1, 9):
            ref[p, pl.ds(0, 8)] = jnp.zeros((8, 128), F32)
            ref[p, pl.ds(64, 8)] = jnp.zeros((8, 128), F32)

    for m in range(4):
        for q in range(2):
            block = blocks[2 * m + q]
            own = gx if q == 0 else jnp.bitwise_xor(gx, 1)
            place = jnp.bitwise_and(own + 8 - 2 * m, 7)
            for j in range(4):
                p = 5 + 4 * place + j
                i = x_index(4 * place + j, 32)
                value = block[j]
                f1[p, pl.ds(8, 112)] = value
                va[p, pl.ds(8, 112)] = w1[i, pl.ds(8, 112)] * value

    level1_sweep(va, vb, f1, w1, t1, 5, 32)

    def residual(k):
        mid = pl.ds(8, 112)
        sums = [None, None]
        for q in (0, 1):
            p = 5 + 2 * k + q
            i = x_index(p - 5, 32)
            m = vb[p, mid]
            tot = vb[p - 1, mid] + vb[p + 1, mid] + vb[p, pl.ds(7, 112)] + vb[p, pl.ds(9, 112)]
            parts = (f1[p, mid] + S1 * tot - d1[i, mid] * m, m)
            sums = [v if t is None else t + v for t, v in zip(sums, parts)]
        pairs = []
        for n in range(2):
            tmp[2 * k + n, pl.ds(0, 112)] = sums[n]
            pairs.append(tmp[2 * k + n, pl.ds(0, 56, stride=2)] + tmp[2 * k + n, pl.ds(1, 56, stride=2)])
        return pairs

    def restrict(p, j):
        low, high = residual(p - 1), residual(p + 7)
        value = select(jnp.concatenate([low[0], high[0]], axis=1), dd[...])
        value = value + S1 * select(jnp.concatenate([low[1], high[1]], axis=1), tdd[...])
        f2[p, pl.ds(8, 56)] = value
        i = jnp.where(p == 1, 0, jnp.where(p == 8, 2, 1))
        a2[p, pl.ds(8, 56)] = w2[i, pl.ds(8, 56)] * value

    planes(1, 8, 8, restrict)

    src2, dst2 = a2, b2
    for _ in range(7):
        level2_sweep(src2, dst2, f2, w2)
        src2, dst2 = dst2, src2

    def prolong(p, j):
        both = select(src2[p, pl.ds(8, 56)], uu[...])
        for n, k in ((0, p - 1), (1, p + 7)):
            e = both[:, 128 * n:128 * n + 128]
            for q in (0, 1):
                for h in (0, 1):
                    rows = pl.ds(8 + h, 56, stride=2)
                    vb[5 + 2 * k + q, rows] = vb[5 + 2 * k + q, rows] + e

    planes(1, 8, 8, prolong)
    level1_sweep(vb, va, f1, w1, t1, 4 * gx + 1, 12)
    level1_sweep(va, vb, f1, w1, t1, 4 * gx + 2, 10)


def level0_prolong(pos, e1, up0, old, new, first, last):
    def body(k, j):
        e = e1[4 * pos[0] + 1 + k, pl.ds(28, 72)]
        e = select(e, up0[...])
        for q in (0, 1):
            p = 2 * k + q
            for h in (0, 1):
                rows = pl.ds(8 + h, 72, stride=2)
                new[0][p, rows] = old[0][p, rows] + e[:, :128]
                new[1][p, rows] = old[1][p, rows] + e[:, 128:]

    planes(first // 2, last // 2 + 1 - first // 2, 10, body)


def zero_pads(refs, first, last):
    zero = jnp.zeros((8, 128), F32)
    for ref in refs:
        for p in range(first, last + 1):
            ref[p, pl.ds(0, 8)] = zero
            ref[p, pl.ds(152, 8)] = zero


def rim_kernel(u, u0, cols, rows):
    lane = iota((128, 128), 1)
    acc = jnp.zeros((128, 128), F32)
    for d in range(3):
        for x in range(8):
            k = 8 * d + x
            value = u[d, x]
            u0[9 * d + x] = value
            acc = jnp.where(lane == k, pltpu.roll(value, k, 1) if k else value, acc)
            rows[pl.ds(k, 1)] = u[d, x, pl.ds(0, 1)]
    cols[...] = acc


def form_matrix(stiff, high, low):
    r, c = iota((192, 24), 0), iota((192, 24), 1)
    wide = jnp.where(lax.shift_right_logical(r, 3) == c, 1.0, 0.0)
    r, c = iota((24, 192), 0), iota((24, 192), 1)
    tall = jnp.where(lax.shift_right_logical(c, 3) == r, 1.0, 0.0)
    full = jnp.dot(wide, stiff, precision=HIGH, preferred_element_type=F32)
    full = jnp.dot(full, tall, precision=HIGH, preferred_element_type=F32)
    r, c = iota((192, 192), 0), iota((192, 192), 1)
    full = jnp.where(jnp.bitwise_and(r, 7) == jnp.bitwise_and(c, 7), full, 0.0)
    top = full.astype(BF16)
    high[...] = top
    low[...] = (full - top.astype(F32)).astype(BF16)


def energy_group(u0, u1, high, low, rho, f, x, y, x_in, x_out, shift=0):
    cols = []
    for q in range(4):
        val = []
        for ref in (u0, u1):
            for b in (0, 1):
                for a in (0, 1):
                    for d in range(3):
                        val.append(ref[9 * d + x + a, pl.ds(y + 8 * q + b, 8)])
        cols.append(jnp.concatenate(val, axis=0))
    u = jnp.concatenate(cols, axis=1)
    top = u.astype(BF16)
    pushed = jnp.dot(high[...], top, preferred_element_type=F32)
    pushed = pushed + jnp.dot(low[...], top, preferred_element_type=F32)
    prod = pushed * (u + (u - top.astype(F32)))
    energy = prod[0:8]
    for i in range(1, 24):
        energy = energy + prod[8 * i:8 * i + 8]
    for q in range(4):
        rows = pl.ds(y + shift + 8 * q, 8)
        r = rho[x_in, rows]
        f[x_out, rows] = -3.0 * r * r * energy[:, 128 * q:128 * q + 128]


def energy_setup(stiff, u0, u1, high, low):
    form_matrix(stiff[...], high, low)
    for q in range(27):
        if q % 9 < 8:
            u1[q] = next_lane(u0[q])


def energy_first(pos, u0, bare, high, low, zrim, rho, u1, f):
    lane = iota((128, 128), 1)
    col = zrim[...] * jnp.where(pos[2] < 3, 1.0, 0.0)
    for d in range(3):
        for x in range(8):
            k, q = 8 * d + x, 9 * d + x
            u1[q] = jnp.where(lane == 127, pltpu.roll(col, 127 - k, 1), bare[q])

    def group(c, j):
        x = c // 3
        y = pl.multiple_of((c - 3 * x) * 32, 32)
        energy_group(u0, u1, high, low, rho, f, x, y, x, x)

    planes(0, 12, 4, group)


def rim_row(row, corner, k, w0, w1, q, start):
    lane = iota((8, 128), 1)
    row = jnp.broadcast_to(row, (8, 128))
    corner = jnp.broadcast_to(corner, (8, 128))
    w0[q, pl.ds(start, 8)] = row
    w1[q, pl.ds(start, 8)] = jnp.where(
        lane == 127, pltpu.roll(corner, 127 - k, 1), next_lane(row))


def energy_second(pos, u0, u1, high, low, rho, yrim, fa, f, w0, w1):
    keep_y = jnp.where(pos[1] < 3, 1.0, 0.0)
    keep_z = jnp.where(pos[2] < 3, 1.0, 0.0)
    corner = yrim[pl.ds(24, 1)] * (keep_y * keep_z)
    for d in range(3):
        for x in range(8):
            k, q = 8 * d + x, 9 * d + x
            w0[q, pl.ds(0, 32)] = u0[q, pl.ds(96, 32)]
            w1[q, pl.ds(0, 32)] = u1[q, pl.ds(96, 32)]
            rim_row(yrim[pl.ds(k, 1)] * keep_y, corner, k, w0, w1, q, 32)
    for x in range(4):
        f[x, pl.ds(0, 96)] = fa[x, pl.ds(0, 96)]

    def group(c, j):
        x = c // 3
        y = pl.multiple_of((c - 3 * x) * 32, 32)
        energy_group(u0, u1, high, low, rho, f, x + 4, y, x + 4, x + 4)

    planes(0, 9, 3, group)
    for x in range(7):
        energy_group(w0, w1, high, low, rho, f, x, 0, x, x, 96)


def energy_last(pos, u0, u1, high, low, rho, xface, yrim, zrim, xrim, fb,
                f, lead, tail, pack, w0, w1):
    keep_x = jnp.where(pos[0] < 7, 1.0, 0.0)
    keep_y = jnp.where(pos[1] < 3, 1.0, 0.0)
    keep_z = jnp.where(pos[2] < 3, 1.0, 0.0)
    lane = iota((128, 128), 1)
    col = xrim[pl.ds(32, 128)] * (keep_x * keep_z)
    for d in range(3):
        k, q = 8 * d + 7, 9 * d
        w0[q, pl.ds(0, 128)] = u0[9 * d + 7]
        w1[q, pl.ds(0, 128)] = u1[9 * d + 7]
        corner = yrim[pl.ds(24, 1)] * (keep_y * keep_z)
        rim_row(yrim[pl.ds(k, 1)] * keep_y, corner, k, w0, w1, q, 128)
        k, q = 8 * d, 9 * d + 1
        body = xface[d] * keep_x
        w0[q, pl.ds(0, 128)] = body
        w1[q, pl.ds(0, 128)] = jnp.where(
            lane == 127, pltpu.roll(col, 127 - k, 1), next_lane(body))
        corner = xrim[pl.ds(24, 1)] * (keep_x * keep_y * keep_z)
        rim_row(xrim[pl.ds(k, 1)] * (keep_x * keep_y), corner, k, w0, w1, q, 128)
    for x in range(7):
        f[x] = fb[x]
    for q in range(4):
        energy_group(w0, w1, high, low, rho, f, 0, 32 * q, 7, 7)
    acc = jnp.zeros((128, 128), F32)
    for x in range(8):
        value = f[x]
        if x < 7:
            lead[x] = value
        if x > 0:
            tail[x - 1] = value
        here = (lane >= 16 * x) & (lane < 16 * x + 16)
        acc = jnp.where(here, pltpu.roll(value, (16 * x + 8) % 128, 1), acc)
    pack[...] = acc


def spread(value, x):
    return pltpu.roll(value, (248 - 16 * x) % 128, 1)


def lay_out(pos, blk, halo, base, first, last, skip, wm, ws, fm, fs, am, as_):
    for p in range(first, last + 1):
        x = p - base
        i = x_index(pos[0] * 8 + p - 8, 64)
        parts = (
            (8, 8, halo[pl.ds(8 * x, 8)], spread(halo[pl.ds(64, 8)], x)),
            (16, 128, blk[x - skip], spread(halo[pl.ds(144, 128)], x)),
            (144, 8, halo[pl.ds(72 + 8 * x, 8)], spread(halo[pl.ds(136, 8)], x)),
        )
        for start, size, main, side in parts:
            rows = pl.ds(start, size)
            fm[p, rows] = main
            fs[p, rows] = side
            am[p, rows] = wm[i, rows] * main
            as_[p, rows] = ws[i, rows] * side


def own_kernel(pos, fc, hc, wm, ws, fm, fs, am, as_):
    zero_pads((fm, fs, am, as_), 1, 22)
    lay_out(pos, fc, hc, 8, 8, 15, 0, wm, ws, fm, fs, am, as_)


def first_kernel(pos, fl, fr, hl, hr, wm, ws, dm, t0, r0, tr0, zz, *refs):
    fm, fs, am, as_, vm, vs, out, z_low, z_high, tmp = refs[4:]
    lay_out(pos, fl, hl, 0, 6, 7, 1, wm, ws, fm, fs, am, as_)
    lay_out(pos, fr, hr, 16, 16, 17, 0, wm, ws, fm, fs, am, as_)
    zero_pads((vm, vs), 7, 16)
    level0_sweep(pos, (am, as_), (vm, vs), fm, fs, wm, ws, t0, 7, 16, True)
    level0_restrict(pos, (vm, vs), fm, dm, r0, tr0, zz, tmp, out, z_low, z_high)


def outer_kernel(pos, fl, fr, hl, hr, wm, ws, t0, *refs):
    fm, fs, am, as_, vm, vs = refs[6:]
    lay_out(pos, fl, hl, 0, 1, 5, 1, wm, ws, fm, fs, am, as_)
    lay_out(pos, fr, hr, 16, 18, 22, 0, wm, ws, fm, fs, am, as_)
    zero_pads((vm, vs), 2, 6)
    zero_pads((vm, vs), 17, 21)
    level0_sweep(pos, (am, as_), (vm, vs), fm, fs, wm, ws, t0, 2, 6, True)
    level0_sweep(pos, (am, as_), (vm, vs), fm, fs, wm, ws, t0, 17, 21, True)


def middle_kernel(pos, *refs):
    blocks, tables = refs[:8], refs[8:15]
    up0, wm, ws, dm, t0, r0, tr0, zz, fm, fs, vm, vs = refs[15:27]
    om, os_, out, z_low, z_high, am, as_, bm, bs, f1, va, vb, f2, a2, b2, tmp = refs[27:]
    zero_pads((am, as_, bm, bs, om, os_), 2, 21)
    coarse_levels(pos, blocks, tables, f1, va, vb, f2, a2, b2, tmp)
    level0_prolong(pos, vb, up0, (vm, vs), (am, as_), 2, 21)
    level0_sweep(pos, (am, as_), (bm, bs), fm, fs, wm, ws, t0, 3, 20, True)
    level0_sweep(pos, (bm, bs), (am, as_), fm, fs, wm, ws, t0, 4, 19, True)
    level0_sweep(pos, (am, as_), (bm, bs), fm, fs, wm, ws, t0, 5, 18, True)
    level0_sweep(pos, (bm, bs), (om, os_), fm, fs, wm, ws, t0, 6, 17, True)
    level0_restrict(pos, (om, os_), fm, dm, r0, tr0, zz, tmp, out, z_low, z_high)


def last_kernel(pos, *refs):
    blocks, tables = refs[:8], refs[8:15]
    up0, wm, ws, t0, fm, fs, vm, vs, out = refs[15:24]
    am, as_, bm, bs, f1, va, vb, f2, a2, b2, tmp = refs[24:]
    zero_pads((am, as_, bm, bs), 6, 17)
    coarse_levels(pos, blocks, tables, f1, va, vb, f2, a2, b2, tmp)
    level0_prolong(pos, vb, up0, (vm, vs), (am, as_), 6, 17)
    level0_sweep(pos, (am, as_), (bm, bs), fm, fs, wm, ws, t0, 7, 16, True)
    level0_sweep(pos, (bm, bs), (am, as_), fm, fs, wm, ws, t0, 8, 15, False)
    for x in range(8):
        out[x] = am[8 + x, pl.ds(16, 128)]


SMEM = pl.BlockSpec(memory_space=pltpu.SMEM)
VM = pl.BlockSpec(memory_space=pltpu.VMEM)


def shape(*dims):
    return jax.ShapeDtypeStruct(dims, F32)


def half_shape(*dims):
    return jax.ShapeDtypeStruct(dims, BF16)


def vmem(*dims):
    return pltpu.VMEM(dims, F32)


def call(kernel, outs, scratch, scalars, args, name, limit=12, in_place=None):
    specs = [SMEM] * scalars + [VM] * (len(args) - scalars)
    return pl.pallas_call(
        kernel,
        out_shape=outs,
        in_specs=specs,
        out_specs=[VM] * len(outs),
        scratch_shapes=scratch,
        input_output_aliases=in_place or {},
        compiler_params=pltpu.CompilerParams(vmem_limit_bytes=limit << 20),
        name=name,
    )(*args)


def shifted(value, axis, step):
    size = lax.axis_size(axis)
    return lax.ppermute(value, axis, [(i, (i + step) % size) for i in range(size)])


def swapped(value):
    return lax.ppermute(value, "gx", [(i, i ^ 1) for i in range(lax.axis_size("gx"))])


COARSE_SCRATCH = [
    vmem(PL1, R1, 128), vmem(PL1, R1, 128), vmem(PL1, R1, 128),
    vmem(10, R2, 128), vmem(10, R2, 128), vmem(10, R2, 128), vmem(32, 128, 128),
]
WIDE = vmem(PL0, R0, 128)


def extend_level1(own, z_low, z_high):
    lane = lax.broadcasted_iota(jnp.int32, (64, 128), 1)
    right, left = shifted(z_low, "gz", -1), shifted(z_high, "gz", 1)
    wide = []
    for k in range(4):
        rim = jnp.where(lane < 96, jnp.roll(right, 64 - 32 * k, 1), jnp.roll(left, 96 - 32 * k, 1))
        wide.append(jnp.where(lane < 64, own[k], rim))
    own = jnp.stack(wide)
    low, high = shifted(own[:, 40:], "gy", 1), shifted(own[:, :24], "gy", -1)
    return jnp.concatenate([low, own, high], axis=1)


def gather_level1(own, meanwhile):
    parts = [own] + [shifted(own, "gx", 2 * m) for m in range(1, 4)]
    if meanwhile:
        parts[3], meanwhile = lax.optimization_barrier((parts[3], meanwhile))
    return [v for part in parts for v in (part, swapped(part))], meanwhile


def per_device(u, rho, stiff):
    pos = jnp.stack([lax.axis_index(a) for a in ("gx", "gy", "gz")]).astype(jnp.int32)
    t = shape(3, R0, 128)
    wm, ws, dm, w1, d1, w2, t0, t1, r0, tr0, dd, tdd, uu, up0, zz = call(
        setup_kernel,
        [t, t, t, shape(3, R1, 128), shape(3, R1, 128), shape(3, R2, 128),
         half_shape(256, 256), half_shape(256, 128), half_shape(128, 128), half_shape(256, 128),
         half_shape(256, 128), half_shape(256, 128), half_shape(128, 256), half_shape(128, 256),
         half_shape(512, 256)],
        [], 1, [pos], "setup")
    u0, cols, rows = call(
        rim_kernel, [shape(27, 128, 128), shape(128, 128), shape(24, 128)], [], 0, [u], "rims")
    xface = shifted(u[:, 0], "gx", -1)
    zrim = shifted(cols, "gz", -1)
    mat = half_shape(192, 192)
    bare, high, low = call(
        energy_setup, [shape(27, 128, 128), mat, mat], [], 0, [stiff, u0], "energy_setup")
    zrim, bare = lax.optimization_barrier((zrim, bare))
    yrim = shifted(jnp.concatenate([rows, zrim[:8]], axis=0), "gy", -1)
    u1, fa = call(
        energy_first, [shape(27, 128, 128), shape(4, 128, 128)],
        [], 1, [pos, u0, bare, high, low, zrim, rho], "energy_first")
    yrim, fa = lax.optimization_barrier((yrim, fa))
    xrim = shifted(jnp.concatenate([yrim, zrim], axis=0), "gx", -1)
    (fb,) = call(
        energy_second, [shape(7, 128, 128)], [vmem(27, 40, 128), vmem(27, 40, 128)], 1,
        [pos, u0, u1, high, low, rho, yrim, fa], "energy_second")
    f, lead, tail, pack = call(
        energy_last, [shape(8, 128, 128), shape(7, 128, 128), shape(7, 128, 128), shape(128, 128)],
        [vmem(27, 136, 128), vmem(27, 136, 128)], 1,
        [pos, u0, u1, high, low, rho, xface, yrim, zrim, xrim, fb], "energy_last")

    fl, fr = shifted(tail, "gx", 1), shifted(lead, "gx", -1)
    lane = lax.broadcasted_iota(jnp.int32, pack.shape, 1)
    from_left = jnp.bitwise_and(lane, 15) < 8
    z = jnp.where(from_left, shifted(pack, "gz", 1), shifted(pack, "gz", -1))
    up = jnp.concatenate([f[:, 120:].reshape(64, 128), z[120:]], axis=0)
    down = jnp.concatenate([f[:, :8].reshape(64, 128), z[:8]], axis=0)
    h = jnp.concatenate([shifted(up, "gy", 1), shifted(down, "gy", -1), z], axis=0)
    wide = shape(PL0, R0, 128)
    level1 = [shape(4, 64, 128), shape(64, 128), shape(64, 128)]
    state = call(own_kernel, [wide] * 4, [], 1, [pos, f, h, wm, ws], "own")
    hl, hr = shifted(h, "gx", 1), shifted(h, "gx", -1)
    *state, vm, vs, f1, z_low, z_high = call(
        first_kernel, [wide] * 6 + level1, [vmem(12, 128, 128)], 1,
        [pos, fl, fr, hl, hr, wm, ws, dm, t0, r0, tr0, zz, *state], "first",
        in_place={12 + n: n for n in range(4)})
    own = extend_level1(f1, z_low, z_high)
    own, hl = lax.optimization_barrier((own, hl))
    fm, fs, _, _, vm, vs = call(
        outer_kernel, [wide] * 6, [], 1,
        [pos, fl, fr, hl, hr, wm, ws, t0, *state, vm, vs], "outer",
        in_place={8 + n: n for n in range(6)})
    blocks, (fm, fs, vm, vs) = gather_level1(own, (fm, fs, vm, vs))
    tables = [w1, d1, w2, t1, dd, tdd, uu, up0]
    vm, vs, *f1 = call(
        middle_kernel, [wide, wide, *level1], [WIDE] * 4 + COARSE_SCRATCH, 1,
        [pos, *blocks, *tables, wm, ws, dm, t0, r0, tr0, zz, fm, fs, vm, vs], "middle", 24)
    blocks, _ = gather_level1(extend_level1(*f1), ())
    (out,) = call(
        last_kernel, [shape(8, 128, 128)], [WIDE] * 4 + COARSE_SCRATCH, 1,
        [pos, *blocks, *tables, wm, ws, t0, fm, fs, vm, vs], "last", 24)
    return out


def solution(mesh):
    return jax.shard_map(
        per_device,
        mesh=mesh,
        in_specs=(P(None, "gx", "gy", "gz"), P("gx", "gy", "gz"), P()),
        out_specs=P("gx", "gy", "gz"),
        check_vma=False,
    )
```

```python
import jax
import jax.numpy as jnp
from jax import lax
from jax.experimental import pallas as pl
from jax.experimental.pallas import tpu as pltpu
from jax.sharding import PartitionSpec as P

FILTER_COEF = 36.0
DAMPING = 0.95
S0 = FILTER_COEF
S1 = FILTER_COEF / 4.0
S2 = FILTER_COEF / 16.0
KEEP = 1.0 - DAMPING
HIGH = lax.Precision.HIGHEST
F32 = jnp.float32
BF16 = jnp.bfloat16

PL0, R0 = 24, 160
PL1, R1 = 42, 128
R2 = 72


def iota(shape, dim):
    return lax.broadcasted_iota(jnp.int32, shape, dim)


def next_lane(value):
    return pltpu.roll(value, 127, 1)


def prev_lane(value):
    return pltpu.roll(value, 1, 1)


def axis_count(place, total):
    return jnp.where(place > 0, 1.0, 0.0) + jnp.where(place < total - 1, 1.0, 0.0)


def planes(start, count, unroll, body):
    step = max(u for u in range(1, unroll + 1) if count % u == 0)
    if step == count:
        for j in range(count):
            body(start + j, j)
        return

    def block(k, carry):
        for j in range(step):
            body(start + k * step + j, j)
        return carry

    lax.fori_loop(0, count // step, block, 0)


def make_tables(weight, diag, rows, row_off, lane_place, lane_ok, base_y, base_z, total, scale):
    y = iota((rows, 128), 0) - row_off + base_y
    z = lane_place + base_z
    inside = lane_ok & (y >= 0) & (y < total) & (z >= 0) & (z < total)
    count = axis_count(y, total) + axis_count(z, total)
    weight[0] = jnp.zeros((rows, 128), F32)
    for i in (1, 2):
        value = 1.0 + scale * (count + float(i))
        weight[i] = jnp.where(inside, DAMPING / value, 0.0)
        if diag is not None:
            diag[i] = value


def x_index(place, total):
    edge = (place == 0) | (place == total - 1)
    out = (place < 0) | (place >= total)
    return jnp.where(out, 0, jnp.where(edge, 1, 2))


def side_place(lane):
    return jnp.where(lane < 64, lane + 128, lane - 128)


def level1_place(lane):
    return jnp.where(lane < 96, lane, lane - 128)


def level1_ok(place):
    return (place >= -22) & (place < 86)


def half(place):
    return lax.shift_right_arithmetic(place, 1)


def hits(cond):
    return jnp.where(cond, 1.0, 0.0)


def level0_place(index):
    side = index - 128
    ok = (index < 128) | (side < 8) | (side >= 120)
    return jnp.where(index < 128, index, side_place(side)), ok


def setup_kernel(pos, wm, ws, dm, w1, d1, w2, t0, t1, r0, tr0, dd, tdd, uu, up0, zz):
    gy, gz = pos[1], pos[2]
    lane = iota((R0, 128), 1)
    make_tables(wm, dm, R0, 16, lane, lane >= 0, gy * 128, gz * 128, 512, S0)
    ok = (lane < 8) | (lane >= 120)
    make_tables(ws, None, R0, 16, side_place(lane), ok, gy * 128, gz * 128, 512, S0)
    z = level1_place(iota((R1, 128), 1))
    make_tables(w1, d1, R1, 32, z, level1_ok(z), gy * 64, gz * 64, 256, S1)

    lane = iota((R2, 128), 1)
    part = jnp.bitwise_and(lane, 63)
    y, z = iota((R2, 128), 0) - 20 + gy * 32, part - 11 + gz * 32
    inside = (part < 54) & (y >= 0) & (y < 128) & (z >= 0) & (z < 128)
    count = axis_count(y, 128) + axis_count(z, 128)
    for i in range(3):
        edge = {0: lane < 64, 1: lane < 0, 2: lane >= 64}[i]
        value = 1.0 + S2 * (count + jnp.where(edge, 1.0, 2.0))
        w2[i] = jnp.where(inside, DAMPING / value, 0.0)

    src, dst = iota((256, 256), 0), iota((256, 256), 1)
    step = jnp.bitwise_and(src - dst, 255)
    t0[...] = hits((step == 1) | (step == 255)).astype(BF16)
    src, dst = iota((256, 128), 0), iota((256, 128), 1)
    step = jnp.bitwise_and(src - dst, 127)
    t1[...] = hits((step == 1) | (step == 127)).astype(BF16)

    col, good = dst, dst < 64
    z, ok = level0_place(src)
    total = jnp.zeros((256, 128), F32)
    for dz in (-1, 1):
        total = total + hits(ok & good & (z + dz >= 0) & (z + dz < 128) & (half(z + dz) == col))
    tr0[...] = (0.125 * total).astype(BF16)
    r0[...] = (0.125 * hits(good & (half(src) == col) & (src < 128)))[0:128].astype(BF16)

    src5, dst5 = iota((512, 256), 0), iota((512, 256), 1)
    slot = jnp.bitwise_and(dst5, 31)
    same = lax.shift_right_logical(src5, 7) == lax.shift_right_logical(jnp.bitwise_and(dst5, 127), 5)
    edge = src5 == jnp.bitwise_and(src5, 384) + slot + jnp.where(dst5 < 128, 0, 32)
    used = (slot >= jnp.where(dst5 < 128, 0, 10)) & (slot < jnp.where(dst5 < 128, 22, 32))
    zz[...] = hits(same & edge & used).astype(BF16)

    z = level1_place(jnp.bitwise_and(src, 127))
    part = jnp.bitwise_and(dst, 63)
    good = (part < 54) & ((src < 128) == (dst < 64))
    dd[...] = (0.125 * hits(good & level1_ok(z) & (half(z) == part - 11))).astype(BF16)
    total = jnp.zeros((256, 128), F32)
    for dz in (-1, 1):
        total = total + hits(good & level1_ok(z + dz) & (half(z + dz) == part - 11))
    tdd[...] = (0.125 * total).astype(BF16)

    src, dst = iota((128, 256), 0), iota((128, 256), 1)
    z = level1_place(jnp.bitwise_and(dst, 127))
    part = jnp.bitwise_and(src, 63)
    good = (part < 54) & ((dst < 128) == (src < 64))
    uu[...] = hits(good & level1_ok(z) & (half(z) == part - 11)).astype(BF16)
    z, ok = level0_place(dst)
    up0[...] = hits(ok & (half(z) == level1_place(src))).astype(BF16)


def two_parts(value):
    top = value.astype(BF16)
    return top, (value - top.astype(F32)).astype(BF16)


def select(value, matrix):
    top, rest = two_parts(value)
    out = jnp.dot(top, matrix, preferred_element_type=F32)
    return out + jnp.dot(rest, matrix, preferred_element_type=F32)


def level0_sweep(pos, src, dst, fm, fs, wm, ws, t0, first, last, side):
    lane = iota((144, 128), 1)
    rows, up, dn = pl.ds(8, 144), pl.ds(7, 144), pl.ds(9, 144)

    def body(p, j):
        i = x_index(pos[0] * 8 + p - 8, 64)
        m, s = src[0][p, rows], src[1][p, rows]
        if j % 2:
            near = select(jnp.concatenate([m, s], axis=1), t0[...])
            near_m, near_s = near[:, :128], near[:, 128:]
        else:
            mr, sr, ml, sl = next_lane(m), next_lane(s), prev_lane(m), prev_lane(s)
            near_m = jnp.where(lane == 127, sr, mr) + jnp.where(lane == 0, sl, ml)
            near_s = jnp.where(lane == 127, mr, sr) + jnp.where(lane == 0, ml, sl)
        tot = src[0][p - 1, rows] + src[0][p + 1, rows] + src[0][p, up] + src[0][p, dn]
        dst[0][p, rows] = KEEP * m + wm[i, rows] * (fm[p, rows] + S0 * (tot + near_m))
        if side:
            tot = src[1][p - 1, rows] + src[1][p + 1, rows] + src[1][p, up] + src[1][p, dn]
            dst[1][p, rows] = KEEP * s + ws[i, rows] * (fs[p, rows] + S0 * (tot + near_s))

    planes(first, last + 1 - first, 10, body)


def level0_restrict(pos, src, fm, dm, r0, tr0, zz, tmp, out, z_low, z_high):
    rows, up, dn = pl.ds(16, 128), pl.ds(15, 128), pl.ds(17, 128)
    values = []
    for k in range(4):
        sums = [None, None, None]
        for q in (0, 1):
            p = 8 + 2 * k + q
            i = x_index(pos[0] * 8 + p - 8, 64)
            m = src[0][p, rows]
            tot = src[0][p - 1, rows] + src[0][p + 1, rows] + src[0][p, up] + src[0][p, dn]
            parts = (fm[p, rows] + S0 * tot - dm[i, rows] * m, m, src[1][p, rows])
            sums = [v if t is None else t + v for t, v in zip(sums, parts)]
        pairs = []
        for n in range(3):
            tmp[3 * k + n, pl.ds(0, 128)] = sums[n]
            pairs.append(tmp[3 * k + n, pl.ds(0, 64, stride=2)] + tmp[3 * k + n, pl.ds(1, 64, stride=2)])
        near = select(jnp.concatenate(pairs[1:], axis=1), tr0[...])
        values.append(select(pairs[0], r0[...]) + S0 * near)
        out[k] = values[k]
    edges = select(jnp.concatenate(values, axis=1), zz[...])
    z_low[...] = edges[:, :128]
    z_high[...] = edges[:, 128:]


def level1_sweep(src, dst, f, w, t1, first, count):
    mid, up, dn = pl.ds(8, 112), pl.ds(7, 112), pl.ds(9, 112)

    def body(p, j):
        i = x_index(p - 5, 32)
        m = src[p, mid]
        if j % 2:
            near = jnp.concatenate(two_parts(m), axis=1)
            near = jnp.dot(near, t1[...], preferred_element_type=F32)
        else:
            near = next_lane(m) + prev_lane(m)
        tot = src[p - 1, mid] + src[p + 1, mid] + src[p, up] + src[p, dn] + near
        dst[p, mid] = KEEP * m + w[i, mid] * (f[p, mid] + S1 * tot)

    planes(first, count, 16, body)


def level2_sweep(src, dst, f, w):
    lane = iota((56, 128), 1)
    mid, up, dn = pl.ds(8, 56), pl.ds(7, 56), pl.ds(9, 56)
    for p in range(1, 9):
        m = src[p, mid]
        if p == 1:
            before = jnp.where(lane >= 64, pltpu.roll(src[8, mid], 64, 1), 0.0)
        else:
            before = src[p - 1, mid]
        if p == 8:
            after = jnp.where(lane < 64, pltpu.roll(src[1, mid], 64, 1), 0.0)
        else:
            after = src[p + 1, mid]
        tot = before + after + src[p, up] + src[p, dn] + next_lane(m) + prev_lane(m)
        dst[p, mid] = KEEP * m + w[{1: 0, 8: 2}.get(p, 1), mid] * (f[p, mid] + S2 * tot)


def coarse_levels(pos, blocks, tables, f1, va, vb, f2, a2, b2, tmp):
    w1, d1, w2, t1, dd, tdd, uu = tables
    gx = pos[0]
    zero = jnp.zeros((R1, 128), F32)
    for p in list(range(0, 5)) + list(range(37, 42)):
        f1[p] = zero
        va[p] = zero
        vb[p] = zero
    for p in range(5, 37):
        for ref in (va, vb):
            ref[p, pl.ds(0, 8)] = jnp.zeros((8, 128), F32)
            ref[p, pl.ds(120, 8)] = jnp.zeros((8, 128), F32)
    for ref in (a2, b2):
        for p in range(1, 9):
            ref[p, pl.ds(0, 8)] = jnp.zeros((8, 128), F32)
            ref[p, pl.ds(64, 8)] = jnp.zeros((8, 128), F32)

    for m in range(4):
        for q in range(2):
            block = blocks[2 * m + q]
            own = gx if q == 0 else jnp.bitwise_xor(gx, 1)
            place = jnp.bitwise_and(own + 8 - 2 * (0, 1, 3, 2)[m], 7)
            for j in range(4):
                p = 5 + 4 * place + j
                i = x_index(4 * place + j, 32)
                value = block[j]
                f1[p, pl.ds(8, 112)] = value
                va[p, pl.ds(8, 112)] = w1[i, pl.ds(8, 112)] * value

    level1_sweep(va, vb, f1, w1, t1, 5, 32)

    def residual(k):
        mid = pl.ds(8, 112)
        sums = [None, None]
        for q in (0, 1):
            p = 5 + 2 * k + q
            i = x_index(p - 5, 32)
            m = vb[p, mid]
            tot = vb[p - 1, mid] + vb[p + 1, mid] + vb[p, pl.ds(7, 112)] + vb[p, pl.ds(9, 112)]
            parts = (f1[p, mid] + S1 * tot - d1[i, mid] * m, m)
            sums = [v if t is None else t + v for t, v in zip(sums, parts)]
        pairs = []
        for n in range(2):
            tmp[2 * k + n, pl.ds(0, 112)] = sums[n]
            pairs.append(tmp[2 * k + n, pl.ds(0, 56, stride=2)] + tmp[2 * k + n, pl.ds(1, 56, stride=2)])
        return pairs

    def restrict(p, j):
        low, high = residual(p - 1), residual(p + 7)
        value = select(jnp.concatenate([low[0], high[0]], axis=1), dd[...])
        value = value + S1 * select(jnp.concatenate([low[1], high[1]], axis=1), tdd[...])
        f2[p, pl.ds(8, 56)] = value
        i = jnp.where(p == 1, 0, jnp.where(p == 8, 2, 1))
        a2[p, pl.ds(8, 56)] = w2[i, pl.ds(8, 56)] * value

    planes(1, 8, 8, restrict)

    src2, dst2 = a2, b2
    for _ in range(7):
        level2_sweep(src2, dst2, f2, w2)
        src2, dst2 = dst2, src2

    def prolong(p, j):
        both = select(src2[p, pl.ds(8, 56)], uu[...])
        for n, k in ((0, p - 1), (1, p + 7)):
            e = both[:, 128 * n:128 * n + 128]
            for q in (0, 1):
                for h in (0, 1):
                    rows = pl.ds(8 + h, 56, stride=2)
                    vb[5 + 2 * k + q, rows] = vb[5 + 2 * k + q, rows] + e

    planes(1, 8, 8, prolong)
    level1_sweep(vb, va, f1, w1, t1, 4 * gx + 1, 12)
    level1_sweep(va, vb, f1, w1, t1, 4 * gx + 2, 10)


def level0_prolong(pos, e1, up0, old, new, first, last):
    def body(k, j):
        e = e1[4 * pos[0] + 1 + k, pl.ds(28, 72)]
        e = select(e, up0[...])
        for q in (0, 1):
            p = 2 * k + q
            for h in (0, 1):
                rows = pl.ds(8 + h, 72, stride=2)
                new[0][p, rows] = old[0][p, rows] + e[:, :128]
                new[1][p, rows] = old[1][p, rows] + e[:, 128:]

    planes(first // 2, last // 2 + 1 - first // 2, 10, body)


def zero_pads(refs, first, last):
    zero = jnp.zeros((8, 128), F32)
    for ref in refs:
        for p in range(first, last + 1):
            ref[p, pl.ds(0, 8)] = zero
            ref[p, pl.ds(152, 8)] = zero


def rim_kernel(u, u0, cols, rows):
    lane = iota((128, 128), 1)
    acc = jnp.zeros((128, 128), F32)
    for d in range(3):
        for x in range(8):
            k = 8 * d + x
            value = u[d, x]
            u0[9 * d + x] = value
            acc = jnp.where(lane == k, pltpu.roll(value, k, 1) if k else value, acc)
            rows[pl.ds(k, 1)] = u[d, x, pl.ds(0, 1)]
    cols[...] = acc


def form_matrix(stiff, high, low):
    r, c = iota((192, 24), 0), iota((192, 24), 1)
    wide = jnp.where(lax.shift_right_logical(r, 3) == c, 1.0, 0.0)
    r, c = iota((24, 192), 0), iota((24, 192), 1)
    tall = jnp.where(lax.shift_right_logical(c, 3) == r, 1.0, 0.0)
    full = jnp.dot(wide, stiff, precision=HIGH, preferred_element_type=F32)
    full = jnp.dot(full, tall, precision=HIGH, preferred_element_type=F32)
    r, c = iota((192, 192), 0), iota((192, 192), 1)
    full = jnp.where(jnp.bitwise_and(r, 7) == jnp.bitwise_and(c, 7), full, 0.0)
    top = full.astype(BF16)
    high[...] = top
    low[...] = (full - top.astype(F32)).astype(BF16)


def energy_group(u0, u1, high, low, rho, f, x, y, x_in, x_out, shift=0):
    cols = []
    for q in range(4):
        val = []
        for ref in (u0, u1):
            for b in (0, 1):
                for a in (0, 1):
                    for d in range(3):
                        val.append(ref[9 * d + x + a, pl.ds(y + 8 * q + b, 8)])
        cols.append(jnp.concatenate(val, axis=0))
    u = jnp.concatenate(cols, axis=1)
    top = u.astype(BF16)
    pushed = jnp.dot(high[...], top, preferred_element_type=F32)
    pushed = pushed + jnp.dot(low[...], top, preferred_element_type=F32)
    prod = pushed * (u + (u - top.astype(F32)))
    energy = prod[0:8]
    for i in range(1, 24):
        energy = energy + prod[8 * i:8 * i + 8]
    for q in range(4):
        rows = pl.ds(y + shift + 8 * q, 8)
        r = rho[x_in, rows]
        f[x_out, rows] = -3.0 * r * r * energy[:, 128 * q:128 * q + 128]


def energy_setup(stiff, u0, u1, high, low):
    form_matrix(stiff[...], high, low)
    for q in range(27):
        if q % 9 < 8:
            u1[q] = next_lane(u0[q])


def energy_first(pos, u0, bare, high, low, zrim, rho, u1, f):
    lane = iota((128, 128), 1)
    col = zrim[...] * jnp.where(pos[2] < 3, 1.0, 0.0)
    for d in range(3):
        for x in range(8):
            k, q = 8 * d + x, 9 * d + x
            u1[q] = jnp.where(lane == 127, pltpu.roll(col, 127 - k, 1), bare[q])

    def group(c, j):
        x = c // 3
        y = pl.multiple_of((c - 3 * x) * 32, 32)
        energy_group(u0, u1, high, low, rho, f, x, y, x, x)

    planes(0, 12, 4, group)


def rim_row(row, corner, k, w0, w1, q, start):
    lane = iota((8, 128), 1)
    row = jnp.broadcast_to(row, (8, 128))
    corner = jnp.broadcast_to(corner, (8, 128))
    w0[q, pl.ds(start, 8)] = row
    w1[q, pl.ds(start, 8)] = jnp.where(
        lane == 127, pltpu.roll(corner, 127 - k, 1), next_lane(row))


def energy_second(pos, u0, u1, high, low, rho, yrim, fa, f, w0, w1):
    keep_y = jnp.where(pos[1] < 3, 1.0, 0.0)
    keep_z = jnp.where(pos[2] < 3, 1.0, 0.0)
    corner = yrim[pl.ds(24, 1)] * (keep_y * keep_z)
    for d in range(3):
        for x in range(8):
            k, q = 8 * d + x, 9 * d + x
            w0[q, pl.ds(0, 32)] = u0[q, pl.ds(96, 32)]
            w1[q, pl.ds(0, 32)] = u1[q, pl.ds(96, 32)]
            rim_row(yrim[pl.ds(k, 1)] * keep_y, corner, k, w0, w1, q, 32)
    for x in range(4):
        f[x, pl.ds(0, 96)] = fa[x, pl.ds(0, 96)]

    def group(c, j):
        x = c // 3
        y = pl.multiple_of((c - 3 * x) * 32, 32)
        energy_group(u0, u1, high, low, rho, f, x + 4, y, x + 4, x + 4)

    planes(0, 9, 3, group)
    for x in range(7):
        energy_group(w0, w1, high, low, rho, f, x, 0, x, x, 96)


def energy_last(pos, u0, u1, high, low, rho, xface, yrim, zrim, xrim, fb,
                f, lead, tail, pack, w0, w1):
    keep_x = jnp.where(pos[0] < 7, 1.0, 0.0)
    keep_y = jnp.where(pos[1] < 3, 1.0, 0.0)
    keep_z = jnp.where(pos[2] < 3, 1.0, 0.0)
    lane = iota((128, 128), 1)
    col = xrim[pl.ds(32, 128)] * (keep_x * keep_z)
    for d in range(3):
        k, q = 8 * d + 7, 9 * d
        w0[q, pl.ds(0, 128)] = u0[9 * d + 7]
        w1[q, pl.ds(0, 128)] = u1[9 * d + 7]
        corner = yrim[pl.ds(24, 1)] * (keep_y * keep_z)
        rim_row(yrim[pl.ds(k, 1)] * keep_y, corner, k, w0, w1, q, 128)
        k, q = 8 * d, 9 * d + 1
        body = xface[d] * keep_x
        w0[q, pl.ds(0, 128)] = body
        w1[q, pl.ds(0, 128)] = jnp.where(
            lane == 127, pltpu.roll(col, 127 - k, 1), next_lane(body))
        corner = xrim[pl.ds(24, 1)] * (keep_x * keep_y * keep_z)
        rim_row(xrim[pl.ds(k, 1)] * (keep_x * keep_y), corner, k, w0, w1, q, 128)
    for x in range(7):
        f[x] = fb[x]
    for q in range(4):
        energy_group(w0, w1, high, low, rho, f, 0, 32 * q, 7, 7)
    acc = jnp.zeros((128, 128), F32)
    for x in range(8):
        value = f[x]
        if x < 7:
            lead[x] = value
        if x > 0:
            tail[x - 1] = value
        here = (lane >= 16 * x) & (lane < 16 * x + 16)
        acc = jnp.where(here, pltpu.roll(value, (16 * x + 8) % 128, 1), acc)
    pack[...] = acc


def spread(value, x):
    return pltpu.roll(value, (248 - 16 * x) % 128, 1)


def lay_out(pos, blk, halo, base, first, last, skip, wm, ws, fm, fs, am, as_):
    for p in range(first, last + 1):
        x = p - base
        i = x_index(pos[0] * 8 + p - 8, 64)
        parts = (
            (8, 8, halo[pl.ds(8 * x, 8)], spread(halo[pl.ds(64, 8)], x)),
            (16, 128, blk[x - skip], spread(halo[pl.ds(144, 128)], x)),
            (144, 8, halo[pl.ds(72 + 8 * x, 8)], spread(halo[pl.ds(136, 8)], x)),
        )
        for start, size, main, side in parts:
            rows = pl.ds(start, size)
            fm[p, rows] = main
            fs[p, rows] = side
            am[p, rows] = wm[i, rows] * main
            as_[p, rows] = ws[i, rows] * side


def own_kernel(pos, fc, hc, wm, ws, fm, fs, am, as_):
    zero_pads((fm, fs, am, as_), 1, 22)
    lay_out(pos, fc, hc, 8, 8, 15, 0, wm, ws, fm, fs, am, as_)


def first_kernel(pos, fl, fr, hl, hr, wm, ws, dm, t0, r0, tr0, zz, *refs):
    fm, fs, am, as_, vm, vs, out, z_low, z_high, tmp = refs[4:]
    lay_out(pos, fl, hl, 0, 6, 7, 1, wm, ws, fm, fs, am, as_)
    lay_out(pos, fr, hr, 16, 16, 17, 0, wm, ws, fm, fs, am, as_)
    zero_pads((vm, vs), 7, 16)
    level0_sweep(pos, (am, as_), (vm, vs), fm, fs, wm, ws, t0, 7, 16, True)
    level0_restrict(pos, (vm, vs), fm, dm, r0, tr0, zz, tmp, out, z_low, z_high)


def outer_kernel(pos, fl, fr, hl, hr, wm, ws, t0, *refs):
    fm, fs, am, as_, vm, vs = refs[6:]
    lay_out(pos, fl, hl, 0, 1, 5, 1, wm, ws, fm, fs, am, as_)
    lay_out(pos, fr, hr, 16, 18, 22, 0, wm, ws, fm, fs, am, as_)
    zero_pads((vm, vs), 2, 6)
    zero_pads((vm, vs), 17, 21)
    level0_sweep(pos, (am, as_), (vm, vs), fm, fs, wm, ws, t0, 2, 6, True)
    level0_sweep(pos, (am, as_), (vm, vs), fm, fs, wm, ws, t0, 17, 21, True)


def middle_kernel(pos, *refs):
    blocks, tables = refs[:8], refs[8:15]
    up0, wm, ws, dm, t0, r0, tr0, zz, fm, fs, vm, vs = refs[15:27]
    om, os_, out, z_low, z_high, am, as_, bm, bs, f1, va, vb, f2, a2, b2, tmp = refs[27:]
    zero_pads((am, as_, bm, bs, om, os_), 2, 21)
    coarse_levels(pos, blocks, tables, f1, va, vb, f2, a2, b2, tmp)
    level0_prolong(pos, vb, up0, (vm, vs), (am, as_), 2, 21)
    level0_sweep(pos, (am, as_), (bm, bs), fm, fs, wm, ws, t0, 3, 20, True)
    level0_sweep(pos, (bm, bs), (am, as_), fm, fs, wm, ws, t0, 4, 19, True)
    level0_sweep(pos, (am, as_), (bm, bs), fm, fs, wm, ws, t0, 5, 18, True)
    level0_sweep(pos, (bm, bs), (om, os_), fm, fs, wm, ws, t0, 6, 17, True)
    level0_restrict(pos, (om, os_), fm, dm, r0, tr0, zz, tmp, out, z_low, z_high)


def last_kernel(pos, *refs):
    blocks, tables = refs[:8], refs[8:15]
    up0, wm, ws, t0, fm, fs, vm, vs, out = refs[15:24]
    am, as_, bm, bs, f1, va, vb, f2, a2, b2, tmp = refs[24:]
    zero_pads((am, as_, bm, bs), 6, 17)
    coarse_levels(pos, blocks, tables, f1, va, vb, f2, a2, b2, tmp)
    level0_prolong(pos, vb, up0, (vm, vs), (am, as_), 6, 17)
    level0_sweep(pos, (am, as_), (bm, bs), fm, fs, wm, ws, t0, 7, 16, True)
    level0_sweep(pos, (bm, bs), (am, as_), fm, fs, wm, ws, t0, 8, 15, False)
    for x in range(8):
        out[x] = am[8 + x, pl.ds(16, 128)]


SMEM = pl.BlockSpec(memory_space=pltpu.SMEM)
VM = pl.BlockSpec(memory_space=pltpu.VMEM)


def shape(*dims):
    return jax.ShapeDtypeStruct(dims, F32)


def half_shape(*dims):
    return jax.ShapeDtypeStruct(dims, BF16)


def vmem(*dims):
    return pltpu.VMEM(dims, F32)


def call(kernel, outs, scratch, scalars, args, name, limit=12, in_place=None):
    specs = [SMEM] * scalars + [VM] * (len(args) - scalars)
    return pl.pallas_call(
        kernel,
        out_shape=outs,
        in_specs=specs,
        out_specs=[VM] * len(outs),
        scratch_shapes=scratch,
        input_output_aliases=in_place or {},
        compiler_params=pltpu.CompilerParams(vmem_limit_bytes=limit << 20),
        name=name,
    )(*args)


def shifted(value, axis, step):
    size = lax.axis_size(axis)
    return lax.ppermute(value, axis, [(i, (i + step) % size) for i in range(size)])


def swapped(value):
    return lax.ppermute(value, "gx", [(i, i ^ 1) for i in range(lax.axis_size("gx"))])


COARSE_SCRATCH = [
    vmem(PL1, R1, 128), vmem(PL1, R1, 128), vmem(PL1, R1, 128),
    vmem(10, R2, 128), vmem(10, R2, 128), vmem(10, R2, 128), vmem(32, 136, 128),
]
WIDE = vmem(PL0, R0, 128)


def extend_level1(own, z_low, z_high):
    lane = lax.broadcasted_iota(jnp.int32, (64, 128), 1)
    right, left = shifted(z_low, "gz", -1), shifted(z_high, "gz", 1)
    wide = []
    for k in range(4):
        rim = jnp.where(lane < 96, jnp.roll(right, 64 - 32 * k, 1), jnp.roll(left, 96 - 32 * k, 1))
        wide.append(jnp.where(lane < 64, own[k], rim))
    own = jnp.stack(wide)
    low, high = shifted(own[:, 40:], "gy", 1), shifted(own[:, :24], "gy", -1)
    return jnp.concatenate([low, own, high], axis=1)


def gather_level1(own, meanwhile):
    parts = [own] + [shifted(own, "gx", 2 * m) for m in (1, 3, 2)]
    if meanwhile:
        parts[3], meanwhile = lax.optimization_barrier((parts[3], meanwhile))
    return [v for part in parts for v in (part, swapped(part))], meanwhile


def per_device(u, rho, stiff):
    pos = jnp.stack([lax.axis_index(a) for a in ("gx", "gy", "gz")]).astype(jnp.int32)
    t = shape(3, R0, 128)
    wm, ws, dm, w1, d1, w2, t0, t1, r0, tr0, dd, tdd, uu, up0, zz = call(
        setup_kernel,
        [t, t, t, shape(3, R1, 128), shape(3, R1, 128), shape(3, R2, 128),
         half_shape(256, 256), half_shape(256, 128), half_shape(128, 128), half_shape(256, 128),
         half_shape(256, 128), half_shape(256, 128), half_shape(128, 256), half_shape(128, 256),
         half_shape(512, 256)],
        [], 1, [pos], "setup")
    u0, cols, rows = call(
        rim_kernel, [shape(27, 128, 128), shape(128, 128), shape(24, 128)], [], 0, [u], "rims")
    xface = shifted(u[:, 0], "gx", -1)
    zrim = shifted(cols, "gz", -1)
    mat = half_shape(192, 192)
    bare, high, low = call(
        energy_setup, [shape(27, 128, 128), mat, mat], [], 0, [stiff, u0], "energy_setup")
    zrim, bare = lax.optimization_barrier((zrim, bare))
    yrim = shifted(jnp.concatenate([rows, zrim[:8]], axis=0), "gy", -1)
    u1, fa = call(
        energy_first, [shape(27, 128, 128), shape(4, 128, 128)],
        [], 1, [pos, u0, bare, high, low, zrim, rho], "energy_first")
    yrim, fa = lax.optimization_barrier((yrim, fa))
    xrim = shifted(jnp.concatenate([yrim, zrim], axis=0), "gx", -1)
    (fb,) = call(
        energy_second, [shape(7, 128, 128)], [vmem(27, 40, 128), vmem(27, 40, 128)], 1,
        [pos, u0, u1, high, low, rho, yrim, fa], "energy_second")
    f, lead, tail, pack = call(
        energy_last, [shape(8, 128, 128), shape(7, 128, 128), shape(7, 128, 128), shape(128, 128)],
        [vmem(27, 136, 128), vmem(27, 136, 128)], 1,
        [pos, u0, u1, high, low, rho, xface, yrim, zrim, xrim, fb], "energy_last")

    fl, fr = shifted(tail, "gx", 1), shifted(lead, "gx", -1)
    lane = lax.broadcasted_iota(jnp.int32, pack.shape, 1)
    from_left = jnp.bitwise_and(lane, 15) < 8
    z = jnp.where(from_left, shifted(pack, "gz", 1), shifted(pack, "gz", -1))
    up = jnp.concatenate([f[:, 120:].reshape(64, 128), z[120:]], axis=0)
    down = jnp.concatenate([f[:, :8].reshape(64, 128), z[:8]], axis=0)
    h = jnp.concatenate([shifted(up, "gy", 1), shifted(down, "gy", -1), z], axis=0)
    wide = shape(PL0, R0, 128)
    level1 = [shape(4, 64, 128), shape(64, 128), shape(64, 128)]
    state = call(own_kernel, [wide] * 4, [], 1, [pos, f, h, wm, ws], "own")
    hl, hr = shifted(h, "gx", 1), shifted(h, "gx", -1)
    *state, vm, vs, f1, z_low, z_high = call(
        first_kernel, [wide] * 6 + level1, [vmem(12, 136, 128)], 1,
        [pos, fl, fr, hl, hr, wm, ws, dm, t0, r0, tr0, zz, *state], "first",
        in_place={12 + n: n for n in range(4)})
    own = extend_level1(f1, z_low, z_high)
    own, hl = lax.optimization_barrier((own, hl))
    fm, fs, _, _, vm, vs = call(
        outer_kernel, [wide] * 6, [], 1,
        [pos, fl, fr, hl, hr, wm, ws, t0, *state, vm, vs], "outer",
        in_place={8 + n: n for n in range(6)})
    blocks, (fm, fs, vm, vs) = gather_level1(own, (fm, fs, vm, vs))
    tables = [w1, d1, w2, t1, dd, tdd, uu, up0]
    vm, vs, *f1 = call(
        middle_kernel, [wide, wide, *level1], [WIDE] * 4 + COARSE_SCRATCH, 1,
        [pos, *blocks, *tables, wm, ws, dm, t0, r0, tr0, zz, fm, fs, vm, vs], "middle", 24)
    blocks, _ = gather_level1(extend_level1(*f1), ())
    (out,) = call(
        last_kernel, [shape(8, 128, 128)], [WIDE] * 4 + COARSE_SCRATCH, 1,
        [pos, *blocks, *tables, wm, ws, t0, fm, fs, vm, vs], "last", 24)
    return out


def solution(mesh):
    return jax.shard_map(
        per_device,
        mesh=mesh,
        in_specs=(P(None, "gx", "gy", "gz"), P("gx", "gy", "gz"), P()),
        out_specs=P("gx", "gy", "gz"),
        check_vma=False,
    )
```

```python
import jax
import jax.numpy as jnp
from jax import lax
from jax.experimental import pallas as pl
from jax.experimental.pallas import tpu as pltpu
from jax.sharding import PartitionSpec as P

FILTER_COEF = 36.0
DAMPING = 0.95
S0 = FILTER_COEF
S1 = FILTER_COEF / 4.0
S2 = FILTER_COEF / 16.0
KEEP = 1.0 - DAMPING
HIGH = lax.Precision.HIGHEST
F32 = jnp.float32
BF16 = jnp.bfloat16

PL0, R0 = 24, 160
PL1, R1 = 42, 128
R2 = 72


def iota(shape, dim):
    return lax.broadcasted_iota(jnp.int32, shape, dim)


def next_lane(value):
    return pltpu.roll(value, 127, 1)


def prev_lane(value):
    return pltpu.roll(value, 1, 1)


def axis_count(place, total):
    return jnp.where(place > 0, 1.0, 0.0) + jnp.where(place < total - 1, 1.0, 0.0)


def planes(start, count, unroll, body):
    step = max(u for u in range(1, unroll + 1) if count % u == 0)
    if step == count:
        for j in range(count):
            body(start + j, j)
        return

    def block(k, carry):
        for j in range(step):
            body(start + k * step + j, j)
        return carry

    lax.fori_loop(0, count // step, block, 0)


def make_tables(weight, diag, rows, row_off, lane_place, lane_ok, base_y, base_z, total, scale):
    y = iota((rows, 128), 0) - row_off + base_y
    z = lane_place + base_z
    inside = lane_ok & (y >= 0) & (y < total) & (z >= 0) & (z < total)
    count = axis_count(y, total) + axis_count(z, total)
    weight[0] = jnp.zeros((rows, 128), F32)
    for i in (1, 2):
        value = 1.0 + scale * (count + float(i))
        weight[i] = jnp.where(inside, DAMPING / value, 0.0)
        if diag is not None:
            diag[i] = value


def x_index(place, total):
    edge = (place == 0) | (place == total - 1)
    out = (place < 0) | (place >= total)
    return jnp.where(out, 0, jnp.where(edge, 1, 2))


def side_place(lane):
    return jnp.where(lane < 64, lane + 128, lane - 128)


def level1_place(lane):
    return jnp.where(lane < 96, lane, lane - 128)


def level1_ok(place):
    return (place >= -22) & (place < 86)


def half(place):
    return lax.shift_right_arithmetic(place, 1)


def hits(cond):
    return jnp.where(cond, 1.0, 0.0)


def level0_place(index):
    side = index - 128
    ok = (index < 128) | (side < 8) | (side >= 120)
    return jnp.where(index < 128, index, side_place(side)), ok


def setup_kernel(pos, wm, ws, dm, w1, d1, w2, t0, t1, r0, tr0, dd, tdd, uu, up0, zz):
    gy, gz = pos[1], pos[2]
    lane = iota((R0, 128), 1)
    make_tables(wm, dm, R0, 16, lane, lane >= 0, gy * 128, gz * 128, 512, S0)
    ok = (lane < 8) | (lane >= 120)
    make_tables(ws, None, R0, 16, side_place(lane), ok, gy * 128, gz * 128, 512, S0)
    z = level1_place(iota((R1, 128), 1))
    make_tables(w1, d1, R1, 32, z, level1_ok(z), gy * 64, gz * 64, 256, S1)

    lane = iota((R2, 128), 1)
    part = jnp.bitwise_and(lane, 63)
    y, z = iota((R2, 128), 0) - 20 + gy * 32, part - 11 + gz * 32
    inside = (part < 54) & (y >= 0) & (y < 128) & (z >= 0) & (z < 128)
    count = axis_count(y, 128) + axis_count(z, 128)
    for i in range(3):
        edge = {0: lane < 64, 1: lane < 0, 2: lane >= 64}[i]
        value = 1.0 + S2 * (count + jnp.where(edge, 1.0, 2.0))
        w2[i] = jnp.where(inside, DAMPING / value, 0.0)

    src, dst = iota((256, 256), 0), iota((256, 256), 1)
    step = jnp.bitwise_and(src - dst, 255)
    t0[...] = hits((step == 1) | (step == 255)).astype(BF16)
    src, dst = iota((256, 128), 0), iota((256, 128), 1)
    step = jnp.bitwise_and(src - dst, 127)
    t1[...] = hits((step == 1) | (step == 127)).astype(BF16)

    col, good = dst, dst < 64
    z, ok = level0_place(src)
    total = jnp.zeros((256, 128), F32)
    for dz in (-1, 1):
        total = total + hits(ok & good & (z + dz >= 0) & (z + dz < 128) & (half(z + dz) == col))
    tr0[...] = (0.125 * total).astype(BF16)
    r0[...] = (0.125 * hits(good & (half(src) == col) & (src < 128)))[0:128].astype(BF16)

    src5, dst5 = iota((512, 256), 0), iota((512, 256), 1)
    slot = jnp.bitwise_and(dst5, 31)
    same = lax.shift_right_logical(src5, 7) == lax.shift_right_logical(jnp.bitwise_and(dst5, 127), 5)
    edge = src5 == jnp.bitwise_and(src5, 384) + slot + jnp.where(dst5 < 128, 0, 32)
    used = (slot >= jnp.where(dst5 < 128, 0, 10)) & (slot < jnp.where(dst5 < 128, 22, 32))
    zz[...] = hits(same & edge & used).astype(BF16)

    z = level1_place(jnp.bitwise_and(src, 127))
    part = jnp.bitwise_and(dst, 63)
    good = (part < 54) & ((src < 128) == (dst < 64))
    dd[...] = (0.125 * hits(good & level1_ok(z) & (half(z) == part - 11))).astype(BF16)
    total = jnp.zeros((256, 128), F32)
    for dz in (-1, 1):
        total = total + hits(good & level1_ok(z + dz) & (half(z + dz) == part - 11))
    tdd[...] = (0.125 * total).astype(BF16)

    src, dst = iota((128, 256), 0), iota((128, 256), 1)
    z = level1_place(jnp.bitwise_and(dst, 127))
    part = jnp.bitwise_and(src, 63)
    good = (part < 54) & ((dst < 128) == (src < 64))
    uu[...] = hits(good & level1_ok(z) & (half(z) == part - 11)).astype(BF16)
    z, ok = level0_place(dst)
    up0[...] = hits(ok & (half(z) == level1_place(src))).astype(BF16)


def two_parts(value):
    top = value.astype(BF16)
    return top, (value - top.astype(F32)).astype(BF16)


def select(value, matrix):
    top, rest = two_parts(value)
    out = jnp.dot(top, matrix, preferred_element_type=F32)
    return out + jnp.dot(rest, matrix, preferred_element_type=F32)


def level0_sweep(pos, src, dst, fm, fs, wm, ws, t0, first, last, side):
    start, size = (8, 144) if side else (16, 128)
    lane = iota((size, 128), 1)
    rows, up, dn = pl.ds(start, size), pl.ds(start - 1, size), pl.ds(start + 1, size)

    def body(p, j):
        i = x_index(pos[0] * 8 + p - 8, 64)
        m, s = src[0][p, rows], src[1][p, rows]
        if j % 2:
            near = select(jnp.concatenate([m, s], axis=1), t0[...])
            near_m, near_s = near[:, :128], near[:, 128:]
        else:
            mr, sr, ml, sl = next_lane(m), next_lane(s), prev_lane(m), prev_lane(s)
            near_m = jnp.where(lane == 127, sr, mr) + jnp.where(lane == 0, sl, ml)
            near_s = jnp.where(lane == 127, mr, sr) + jnp.where(lane == 0, ml, sl)
        tot = src[0][p - 1, rows] + src[0][p + 1, rows] + src[0][p, up] + src[0][p, dn]
        dst[0][p, rows] = KEEP * m + wm[i, rows] * (fm[p, rows] + S0 * (tot + near_m))
        if side:
            tot = src[1][p - 1, rows] + src[1][p + 1, rows] + src[1][p, up] + src[1][p, dn]
            dst[1][p, rows] = KEEP * s + ws[i, rows] * (fs[p, rows] + S0 * (tot + near_s))

    planes(first, last + 1 - first, 10, body)


def level0_restrict(pos, src, fm, dm, r0, tr0, zz, tmp, out, z_low, z_high):
    rows, up, dn = pl.ds(16, 128), pl.ds(15, 128), pl.ds(17, 128)
    values = []
    for k in range(4):
        sums = [None, None, None]
        for q in (0, 1):
            p = 8 + 2 * k + q
            i = x_index(pos[0] * 8 + p - 8, 64)
            m = src[0][p, rows]
            tot = src[0][p - 1, rows] + src[0][p + 1, rows] + src[0][p, up] + src[0][p, dn]
            parts = (fm[p, rows] + S0 * tot - dm[i, rows] * m, m, src[1][p, rows])
            sums = [v if t is None else t + v for t, v in zip(sums, parts)]
        pairs = []
        for n in range(3):
            tmp[3 * k + n, pl.ds(0, 128)] = sums[n]
            pairs.append(tmp[3 * k + n, pl.ds(0, 64, stride=2)] + tmp[3 * k + n, pl.ds(1, 64, stride=2)])
        near = select(jnp.concatenate(pairs[1:], axis=1), tr0[...])
        values.append(select(pairs[0], r0[...]) + S0 * near)
        out[k] = values[k]
    edges = select(jnp.concatenate(values, axis=1), zz[...])
    z_low[...] = edges[:, :128]
    z_high[...] = edges[:, 128:]


def level1_sweep(src, dst, f, w, t1, first, count, start=8, size=112):
    mid, up, dn = pl.ds(start, size), pl.ds(start - 1, size), pl.ds(start + 1, size)

    def body(p, j):
        i = x_index(p - 5, 32)
        m = src[p, mid]
        if j % 2:
            near = jnp.concatenate(two_parts(m), axis=1)
            near = jnp.dot(near, t1[...], preferred_element_type=F32)
        else:
            near = next_lane(m) + prev_lane(m)
        tot = src[p - 1, mid] + src[p + 1, mid] + src[p, up] + src[p, dn] + near
        dst[p, mid] = KEEP * m + w[i, mid] * (f[p, mid] + S1 * tot)

    planes(first, count, 16, body)


def level2_sweep(src, dst, f, w):
    lane = iota((56, 128), 1)
    mid, up, dn = pl.ds(8, 56), pl.ds(7, 56), pl.ds(9, 56)
    for p in range(1, 9):
        m = src[p, mid]
        if p == 1:
            before = jnp.where(lane >= 64, pltpu.roll(src[8, mid], 64, 1), 0.0)
        else:
            before = src[p - 1, mid]
        if p == 8:
            after = jnp.where(lane < 64, pltpu.roll(src[1, mid], 64, 1), 0.0)
        else:
            after = src[p + 1, mid]
        tot = before + after + src[p, up] + src[p, dn] + next_lane(m) + prev_lane(m)
        dst[p, mid] = KEEP * m + w[{1: 0, 8: 2}.get(p, 1), mid] * (f[p, mid] + S2 * tot)


def coarse_levels(pos, blocks, tables, f1, va, vb, f2, a2, b2, tmp, halo):
    w1, d1, w2, t1, dd, tdd, uu = tables
    gx = pos[0]
    zero = jnp.zeros((R1, 128), F32)
    for p in list(range(0, 5)) + list(range(37, 42)):
        f1[p] = zero
        va[p] = zero
        vb[p] = zero
    for p in range(5, 37):
        for ref in (va, vb):
            ref[p, pl.ds(0, 8)] = jnp.zeros((8, 128), F32)
            ref[p, pl.ds(120, 8)] = jnp.zeros((8, 128), F32)
    for ref in (a2, b2):
        for p in range(1, 9):
            ref[p, pl.ds(0, 8)] = jnp.zeros((8, 128), F32)
            ref[p, pl.ds(64, 8)] = jnp.zeros((8, 128), F32)

    for m in range(4):
        for q in range(2):
            block = blocks[2 * m + q]
            own = gx if q == 0 else jnp.bitwise_xor(gx, 1)
            place = jnp.bitwise_and(own + 8 - 2 * (0, 1, 3, 2)[m], 7)
            for j in range(4):
                p = 5 + 4 * place + j
                i = x_index(4 * place + j, 32)
                value = block[j]
                f1[p, pl.ds(8, 112)] = value
                va[p, pl.ds(8, 112)] = w1[i, pl.ds(8, 112)] * value

    level1_sweep(va, vb, f1, w1, t1, 5, 32)

    def residual(k):
        mid = pl.ds(8, 112)
        sums = [None, None]
        for q in (0, 1):
            p = 5 + 2 * k + q
            i = x_index(p - 5, 32)
            m = vb[p, mid]
            tot = vb[p - 1, mid] + vb[p + 1, mid] + vb[p, pl.ds(7, 112)] + vb[p, pl.ds(9, 112)]
            parts = (f1[p, mid] + S1 * tot - d1[i, mid] * m, m)
            sums = [v if t is None else t + v for t, v in zip(sums, parts)]
        pairs = []
        for n in range(2):
            tmp[2 * k + n, pl.ds(0, 112)] = sums[n]
            pairs.append(tmp[2 * k + n, pl.ds(0, 56, stride=2)] + tmp[2 * k + n, pl.ds(1, 56, stride=2)])
        return pairs

    def restrict(p, j):
        low, high = residual(p - 1), residual(p + 7)
        value = select(jnp.concatenate([low[0], high[0]], axis=1), dd[...])
        value = value + S1 * select(jnp.concatenate([low[1], high[1]], axis=1), tdd[...])
        f2[p, pl.ds(8, 56)] = value
        i = jnp.where(p == 1, 0, jnp.where(p == 8, 2, 1))
        a2[p, pl.ds(8, 56)] = w2[i, pl.ds(8, 56)] * value

    planes(1, 8, 8, restrict)

    src2, dst2 = a2, b2
    for _ in range(7):
        level2_sweep(src2, dst2, f2, w2)
        src2, dst2 = dst2, src2

    def prolong(p, j):
        both = select(src2[p, pl.ds(8, 56)], uu[...])
        for n, k in ((0, p - 1), (1, p + 7)):
            e = both[:, 128 * n:128 * n + 128]
            for q in (0, 1):
                for h in (0, 1):
                    rows = pl.ds(8 + h, 56, stride=2)
                    vb[5 + 2 * k + q, rows] = vb[5 + 2 * k + q, rows] + e

    planes(1, 8, 8, prolong)
    level1_sweep(vb, va, f1, w1, t1, 4 * gx + 4 - halo, 6 + 2 * halo, 24, 80)
    level1_sweep(va, vb, f1, w1, t1, 4 * gx + 5 - halo, 4 + 2 * halo, 24, 80)


def level0_prolong(pos, e1, up0, old, new, first, last):
    def body(k, j):
        e = e1[4 * pos[0] + 1 + k, pl.ds(28, 72)]
        e = select(e, up0[...])
        for q in (0, 1):
            p = 2 * k + q
            for h in (0, 1):
                rows = pl.ds(8 + h, 72, stride=2)
                new[0][p, rows] = old[0][p, rows] + e[:, :128]
                new[1][p, rows] = old[1][p, rows] + e[:, 128:]

    planes(first // 2, last // 2 + 1 - first // 2, 10, body)


def zero_pads(refs, first, last):
    zero = jnp.zeros((8, 128), F32)
    for ref in refs:
        for p in range(first, last + 1):
            ref[p, pl.ds(0, 8)] = zero
            ref[p, pl.ds(152, 8)] = zero


def rim_kernel(u, u0, cols, rows):
    lane = iota((128, 128), 1)
    acc = jnp.zeros((128, 128), F32)
    for d in range(3):
        for x in range(8):
            k = 8 * d + x
            value = u[d, x]
            u0[9 * d + x] = value
            acc = jnp.where(lane == k, pltpu.roll(value, k, 1) if k else value, acc)
            rows[pl.ds(k, 1)] = u[d, x, pl.ds(0, 1)]
    cols[...] = acc


def form_matrix(stiff, high, low):
    r, c = iota((192, 24), 0), iota((192, 24), 1)
    wide = jnp.where(lax.shift_right_logical(r, 3) == c, 1.0, 0.0)
    r, c = iota((24, 192), 0), iota((24, 192), 1)
    tall = jnp.where(lax.shift_right_logical(c, 3) == r, 1.0, 0.0)
    full = jnp.dot(wide, stiff, precision=HIGH, preferred_element_type=F32)
    full = jnp.dot(full, tall, precision=HIGH, preferred_element_type=F32)
    r, c = iota((192, 192), 0), iota((192, 192), 1)
    full = jnp.where(jnp.bitwise_and(r, 7) == jnp.bitwise_and(c, 7), full, 0.0)
    top = full.astype(BF16)
    high[...] = top
    low[...] = (full - top.astype(F32)).astype(BF16)


def energy_group(u0, u1, high, low, rho, f, x, y, x_in, x_out, shift=0):
    cols = []
    for q in range(4):
        val = []
        for ref in (u0, u1):
            for b in (0, 1):
                for a in (0, 1):
                    for d in range(3):
                        val.append(ref[9 * d + x + a, pl.ds(y + 8 * q + b, 8)])
        cols.append(jnp.concatenate(val, axis=0))
    u = jnp.concatenate(cols, axis=1)
    top = u.astype(BF16)
    pushed = jnp.dot(high[...], top, preferred_element_type=F32)
    pushed = pushed + jnp.dot(low[...], top, preferred_element_type=F32)
    prod = pushed * (u + (u - top.astype(F32)))
    energy = prod[0:8]
    for i in range(1, 24):
        energy = energy + prod[8 * i:8 * i + 8]
    for q in range(4):
        rows = pl.ds(y + shift + 8 * q, 8)
        r = rho[x_in, rows]
        f[x_out, rows] = -3.0 * r * r * energy[:, 128 * q:128 * q + 128]


def energy_setup(stiff, u0, u1, high, low):
    form_matrix(stiff[...], high, low)
    for q in range(27):
        if q % 9 < 8:
            u1[q] = next_lane(u0[q])


def energy_first(pos, u0, bare, high, low, zrim, rho, u1, f):
    lane = iota((128, 128), 1)
    col = zrim[...] * jnp.where(pos[2] < 3, 1.0, 0.0)
    for d in range(3):
        for x in range(8):
            k, q = 8 * d + x, 9 * d + x
            u1[q] = jnp.where(lane == 127, pltpu.roll(col, 127 - k, 1), bare[q])

    def group(c, j):
        x = c // 3
        y = pl.multiple_of((c - 3 * x) * 32, 32)
        energy_group(u0, u1, high, low, rho, f, x, y, x, x)

    planes(0, 12, 4, group)


def rim_row(row, corner, k, w0, w1, q, start):
    lane = iota((8, 128), 1)
    row = jnp.broadcast_to(row, (8, 128))
    corner = jnp.broadcast_to(corner, (8, 128))
    w0[q, pl.ds(start, 8)] = row
    w1[q, pl.ds(start, 8)] = jnp.where(
        lane == 127, pltpu.roll(corner, 127 - k, 1), next_lane(row))


def energy_second(pos, u0, u1, high, low, rho, yrim, fa, f, w0, w1):
    keep_y = jnp.where(pos[1] < 3, 1.0, 0.0)
    keep_z = jnp.where(pos[2] < 3, 1.0, 0.0)
    corner = yrim[pl.ds(24, 1)] * (keep_y * keep_z)
    for d in range(3):
        for x in range(8):
            k, q = 8 * d + x, 9 * d + x
            w0[q, pl.ds(0, 32)] = u0[q, pl.ds(96, 32)]
            w1[q, pl.ds(0, 32)] = u1[q, pl.ds(96, 32)]
            rim_row(yrim[pl.ds(k, 1)] * keep_y, corner, k, w0, w1, q, 32)
    for x in range(4):
        f[x, pl.ds(0, 96)] = fa[x, pl.ds(0, 96)]

    def group(c, j):
        x = c // 3
        y = pl.multiple_of((c - 3 * x) * 32, 32)
        energy_group(u0, u1, high, low, rho, f, x + 4, y, x + 4, x + 4)

    planes(0, 9, 3, group)
    for x in range(7):
        energy_group(w0, w1, high, low, rho, f, x, 0, x, x, 96)


def energy_last(pos, u0, u1, high, low, rho, xface, yrim, zrim, xrim, fb,
                f, lead, tail, pack, w0, w1):
    keep_x = jnp.where(pos[0] < 7, 1.0, 0.0)
    keep_y = jnp.where(pos[1] < 3, 1.0, 0.0)
    keep_z = jnp.where(pos[2] < 3, 1.0, 0.0)
    lane = iota((128, 128), 1)
    col = xrim[pl.ds(32, 128)] * (keep_x * keep_z)
    for d in range(3):
        k, q = 8 * d + 7, 9 * d
        w0[q, pl.ds(0, 128)] = u0[9 * d + 7]
        w1[q, pl.ds(0, 128)] = u1[9 * d + 7]
        corner = yrim[pl.ds(24, 1)] * (keep_y * keep_z)
        rim_row(yrim[pl.ds(k, 1)] * keep_y, corner, k, w0, w1, q, 128)
        k, q = 8 * d, 9 * d + 1
        body = xface[d] * keep_x
        w0[q, pl.ds(0, 128)] = body
        w1[q, pl.ds(0, 128)] = jnp.where(
            lane == 127, pltpu.roll(col, 127 - k, 1), next_lane(body))
        corner = xrim[pl.ds(24, 1)] * (keep_x * keep_y * keep_z)
        rim_row(xrim[pl.ds(k, 1)] * (keep_x * keep_y), corner, k, w0, w1, q, 128)
    for x in range(7):
        f[x] = fb[x]
    for q in range(4):
        energy_group(w0, w1, high, low, rho, f, 0, 32 * q, 7, 7)
    acc = jnp.zeros((128, 128), F32)
    for x in range(8):
        value = f[x]
        if x < 7:
            lead[x] = value
        if x > 0:
            tail[x - 1] = value
        here = (lane >= 16 * x) & (lane < 16 * x + 16)
        acc = jnp.where(here, pltpu.roll(value, (16 * x + 8) % 128, 1), acc)
    pack[...] = acc


def spread(value, x):
    return pltpu.roll(value, (248 - 16 * x) % 128, 1)


def lay_out(pos, blk, halo, base, first, last, skip, wm, ws, fm, fs, am, as_):
    for p in range(first, last + 1):
        x = p - base
        i = x_index(pos[0] * 8 + p - 8, 64)
        parts = (
            (8, 8, halo[pl.ds(8 * x, 8)], spread(halo[pl.ds(64, 8)], x)),
            (16, 128, blk[x - skip], spread(halo[pl.ds(144, 128)], x)),
            (144, 8, halo[pl.ds(72 + 8 * x, 8)], spread(halo[pl.ds(136, 8)], x)),
        )
        for start, size, main, side in parts:
            rows = pl.ds(start, size)
            fm[p, rows] = main
            fs[p, rows] = side
            am[p, rows] = wm[i, rows] * main
            as_[p, rows] = ws[i, rows] * side


def own_kernel(pos, fc, hc, wm, ws, fm, fs, am, as_):
    zero_pads((fm, fs, am, as_), 1, 22)
    lay_out(pos, fc, hc, 8, 8, 15, 0, wm, ws, fm, fs, am, as_)


def first_kernel(pos, fl, fr, hl, hr, wm, ws, dm, t0, r0, tr0, zz, *refs):
    fm, fs, am, as_, vm, vs, out, z_low, z_high, tmp = refs[4:]
    lay_out(pos, fl, hl, 0, 6, 7, 1, wm, ws, fm, fs, am, as_)
    lay_out(pos, fr, hr, 16, 16, 17, 0, wm, ws, fm, fs, am, as_)
    zero_pads((vm, vs), 7, 16)
    level0_sweep(pos, (am, as_), (vm, vs), fm, fs, wm, ws, t0, 7, 16, True)
    level0_restrict(pos, (vm, vs), fm, dm, r0, tr0, zz, tmp, out, z_low, z_high)


def outer_kernel(pos, fl, fr, hl, hr, wm, ws, t0, *refs):
    fm, fs, am, as_, vm, vs = refs[6:]
    lay_out(pos, fl, hl, 0, 1, 5, 1, wm, ws, fm, fs, am, as_)
    lay_out(pos, fr, hr, 16, 18, 22, 0, wm, ws, fm, fs, am, as_)
    zero_pads((vm, vs), 2, 6)
    zero_pads((vm, vs), 17, 21)
    level0_sweep(pos, (am, as_), (vm, vs), fm, fs, wm, ws, t0, 2, 6, True)
    level0_sweep(pos, (am, as_), (vm, vs), fm, fs, wm, ws, t0, 17, 21, True)


def middle_kernel(pos, *refs):
    blocks, tables = refs[:8], refs[8:15]
    up0, wm, ws, dm, t0, r0, tr0, zz, fm, fs, vm, vs = refs[15:27]
    om, os_, out, z_low, z_high, am, as_, bm, bs, f1, va, vb, f2, a2, b2, tmp = refs[27:]
    zero_pads((am, as_, bm, bs, om, os_), 2, 21)
    coarse_levels(pos, blocks, tables, f1, va, vb, f2, a2, b2, tmp, 3)
    level0_prolong(pos, vb, up0, (vm, vs), (am, as_), 2, 21)
    level0_sweep(pos, (am, as_), (bm, bs), fm, fs, wm, ws, t0, 3, 20, True)
    level0_sweep(pos, (bm, bs), (am, as_), fm, fs, wm, ws, t0, 4, 19, True)
    level0_sweep(pos, (am, as_), (bm, bs), fm, fs, wm, ws, t0, 5, 18, True)
    level0_sweep(pos, (bm, bs), (om, os_), fm, fs, wm, ws, t0, 6, 17, True)
    level0_restrict(pos, (om, os_), fm, dm, r0, tr0, zz, tmp, out, z_low, z_high)


def last_kernel(pos, *refs):
    blocks, tables = refs[:8], refs[8:15]
    up0, wm, ws, t0, fm, fs, vm, vs, out = refs[15:24]
    am, as_, bm, bs, f1, va, vb, f2, a2, b2, tmp = refs[24:]
    zero_pads((am, as_, bm, bs), 6, 17)
    coarse_levels(pos, blocks, tables, f1, va, vb, f2, a2, b2, tmp, 1)
    level0_prolong(pos, vb, up0, (vm, vs), (am, as_), 6, 17)
    level0_sweep(pos, (am, as_), (bm, bs), fm, fs, wm, ws, t0, 7, 16, True)
    level0_sweep(pos, (bm, bs), (am, as_), fm, fs, wm, ws, t0, 8, 15, False)
    for x in range(8):
        out[x] = am[8 + x, pl.ds(16, 128)]


SMEM = pl.BlockSpec(memory_space=pltpu.SMEM)
VM = pl.BlockSpec(memory_space=pltpu.VMEM)


def shape(*dims):
    return jax.ShapeDtypeStruct(dims, F32)


def half_shape(*dims):
    return jax.ShapeDtypeStruct(dims, BF16)


def vmem(*dims):
    return pltpu.VMEM(dims, F32)


def call(kernel, outs, scratch, scalars, args, name, limit=12, in_place=None):
    specs = [SMEM] * scalars + [VM] * (len(args) - scalars)
    return pl.pallas_call(
        kernel,
        out_shape=outs,
        in_specs=specs,
        out_specs=[VM] * len(outs),
        scratch_shapes=scratch,
        input_output_aliases=in_place or {},
        compiler_params=pltpu.CompilerParams(vmem_limit_bytes=limit << 20),
        name=name,
    )(*args)


def shifted(value, axis, step):
    size = lax.axis_size(axis)
    return lax.ppermute(value, axis, [(i, (i + step) % size) for i in range(size)])


def swapped(value):
    return lax.ppermute(value, "gx", [(i, i ^ 1) for i in range(lax.axis_size("gx"))])


COARSE_SCRATCH = [
    vmem(PL1, R1, 128), vmem(PL1, R1, 128), vmem(PL1, R1, 128),
    vmem(10, R2, 128), vmem(10, R2, 128), vmem(10, R2, 128), vmem(32, 136, 128),
]
WIDE = vmem(PL0, R0, 128)


def extend_level1(own, z_low, z_high):
    lane = lax.broadcasted_iota(jnp.int32, (64, 128), 1)
    right, left = shifted(z_low, "gz", -1), shifted(z_high, "gz", 1)
    wide = []
    for k in range(4):
        rim = jnp.where(lane < 96, jnp.roll(right, 64 - 32 * k, 1), jnp.roll(left, 96 - 32 * k, 1))
        wide.append(jnp.where(lane < 64, own[k], rim))
    own = jnp.stack(wide)
    low, high = shifted(own[:, 40:], "gy", 1), shifted(own[:, :24], "gy", -1)
    return jnp.concatenate([low, own, high], axis=1)


def gather_level1(own, meanwhile):
    parts = [own] + [shifted(own, "gx", 2 * m) for m in (1, 3, 2)]
    if meanwhile:
        parts[3], meanwhile = lax.optimization_barrier((parts[3], meanwhile))
    return [v for part in parts for v in (part, swapped(part))], meanwhile


def per_device(u, rho, stiff):
    pos = jnp.stack([lax.axis_index(a) for a in ("gx", "gy", "gz")]).astype(jnp.int32)
    t = shape(3, R0, 128)
    wm, ws, dm, w1, d1, w2, t0, t1, r0, tr0, dd, tdd, uu, up0, zz = call(
        setup_kernel,
        [t, t, t, shape(3, R1, 128), shape(3, R1, 128), shape(3, R2, 128),
         half_shape(256, 256), half_shape(256, 128), half_shape(128, 128), half_shape(256, 128),
         half_shape(256, 128), half_shape(256, 128), half_shape(128, 256), half_shape(128, 256),
         half_shape(512, 256)],
        [], 1, [pos], "setup")
    u0, cols, rows = call(
        rim_kernel, [shape(27, 128, 128), shape(128, 128), shape(24, 128)], [], 0, [u], "rims")
    xface = shifted(u[:, 0], "gx", -1)
    zrim = shifted(cols, "gz", -1)
    mat = half_shape(192, 192)
    bare, high, low = call(
        energy_setup, [shape(27, 128, 128), mat, mat], [], 0, [stiff, u0], "energy_setup")
    zrim, bare = lax.optimization_barrier((zrim, bare))
    yrim = shifted(jnp.concatenate([rows, zrim[:8]], axis=0), "gy", -1)
    u1, fa = call(
        energy_first, [shape(27, 128, 128), shape(4, 128, 128)],
        [], 1, [pos, u0, bare, high, low, zrim, rho], "energy_first")
    yrim, fa = lax.optimization_barrier((yrim, fa))
    xrim = shifted(jnp.concatenate([yrim, zrim], axis=0), "gx", -1)
    (fb,) = call(
        energy_second, [shape(7, 128, 128)], [vmem(27, 40, 128), vmem(27, 40, 128)], 1,
        [pos, u0, u1, high, low, rho, yrim, fa], "energy_second")
    f, lead, tail, pack = call(
        energy_last, [shape(8, 128, 128), shape(7, 128, 128), shape(7, 128, 128), shape(128, 128)],
        [vmem(27, 136, 128), vmem(27, 136, 128)], 1,
        [pos, u0, u1, high, low, rho, xface, yrim, zrim, xrim, fb], "energy_last")

    fl, fr = shifted(tail, "gx", 1), shifted(lead, "gx", -1)
    lane = lax.broadcasted_iota(jnp.int32, pack.shape, 1)
    from_left = jnp.bitwise_and(lane, 15) < 8
    z = jnp.where(from_left, shifted(pack, "gz", 1), shifted(pack, "gz", -1))
    up = jnp.concatenate([f[:, 120:].reshape(64, 128), z[120:]], axis=0)
    down = jnp.concatenate([f[:, :8].reshape(64, 128), z[:8]], axis=0)
    h = jnp.concatenate([shifted(up, "gy", 1), shifted(down, "gy", -1), z], axis=0)
    wide = shape(PL0, R0, 128)
    level1 = [shape(4, 64, 128), shape(64, 128), shape(64, 128)]
    state = call(own_kernel, [wide] * 4, [], 1, [pos, f, h, wm, ws], "own")
    hl, hr = shifted(h, "gx", 1), shifted(h, "gx", -1)
    *state, vm, vs, f1, z_low, z_high = call(
        first_kernel, [wide] * 6 + level1, [vmem(12, 136, 128)], 1,
        [pos, fl, fr, hl, hr, wm, ws, dm, t0, r0, tr0, zz, *state], "first",
        in_place={12 + n: n for n in range(4)})
    own = extend_level1(f1, z_low, z_high)
    own, hl = lax.optimization_barrier((own, hl))
    fm, fs, _, _, vm, vs = call(
        outer_kernel, [wide] * 6, [], 1,
        [pos, fl, fr, hl, hr, wm, ws, t0, *state, vm, vs], "outer",
        in_place={8 + n: n for n in range(6)})
    blocks, (fm, fs, vm, vs) = gather_level1(own, (fm, fs, vm, vs))
    tables = [w1, d1, w2, t1, dd, tdd, uu, up0]
    vm, vs, *f1 = call(
        middle_kernel, [wide, wide, *level1], [WIDE] * 4 + COARSE_SCRATCH, 1,
        [pos, *blocks, *tables, wm, ws, dm, t0, r0, tr0, zz, fm, fs, vm, vs], "middle", 24)
    blocks, _ = gather_level1(extend_level1(*f1), ())
    (out,) = call(
        last_kernel, [shape(8, 128, 128)], [WIDE] * 4 + COARSE_SCRATCH, 1,
        [pos, *blocks, *tables, wm, ws, t0, fm, fs, vm, vs], "last", 24)
    return out


def solution(mesh):
    return jax.shard_map(
        per_device,
        mesh=mesh,
        in_specs=(P(None, "gx", "gy", "gz"), P("gx", "gy", "gz"), P()),
        out_specs=P("gx", "gy", "gz"),
        check_vma=False,
    )
```

```python
import jax
import jax.numpy as jnp
from jax import lax
from jax.experimental import pallas as pl
from jax.experimental.pallas import tpu as pltpu
from jax.sharding import PartitionSpec as P

FILTER_COEF = 36.0
DAMPING = 0.95
S0 = FILTER_COEF
S1 = FILTER_COEF / 4.0
S2 = FILTER_COEF / 16.0
KEEP = 1.0 - DAMPING
HIGH = lax.Precision.HIGHEST
F32 = jnp.float32
BF16 = jnp.bfloat16

PL0, R0 = 24, 160
PL1, R1 = 42, 128
R2 = 72


def iota(shape, dim):
    return lax.broadcasted_iota(jnp.int32, shape, dim)


def next_lane(value):
    return pltpu.roll(value, 127, 1)


def prev_lane(value):
    return pltpu.roll(value, 1, 1)


def axis_count(place, total):
    return jnp.where(place > 0, 1.0, 0.0) + jnp.where(place < total - 1, 1.0, 0.0)


def planes(start, count, unroll, body):
    step = max(u for u in range(1, unroll + 1) if count % u == 0)
    if step == count:
        for j in range(count):
            body(start + j, j)
        return

    def block(k, carry):
        for j in range(step):
            body(start + k * step + j, j)
        return carry

    lax.fori_loop(0, count // step, block, 0)


def make_tables(weight, diag, rows, row_off, lane_place, lane_ok, base_y, base_z, total, scale):
    y = iota((rows, 128), 0) - row_off + base_y
    z = lane_place + base_z
    inside = lane_ok & (y >= 0) & (y < total) & (z >= 0) & (z < total)
    count = axis_count(y, total) + axis_count(z, total)
    weight[0] = jnp.zeros((rows, 128), F32)
    for i in (1, 2):
        value = 1.0 + scale * (count + float(i))
        weight[i] = jnp.where(inside, DAMPING / value, 0.0)
        if diag is not None:
            diag[i] = value


def x_index(place, total):
    edge = (place == 0) | (place == total - 1)
    out = (place < 0) | (place >= total)
    return jnp.where(out, 0, jnp.where(edge, 1, 2))


def side_place(lane):
    return jnp.where(lane < 64, lane + 128, lane - 128)


def level1_place(lane):
    return jnp.where(lane < 96, lane, lane - 128)


def level1_ok(place):
    return (place >= -22) & (place < 86)


def half(place):
    return lax.shift_right_arithmetic(place, 1)


def hits(cond):
    return jnp.where(cond, 1.0, 0.0)


def level0_place(index):
    side = index - 128
    ok = (index < 128) | (side < 8) | (side >= 120)
    return jnp.where(index < 128, index, side_place(side)), ok


def setup_kernel(pos, wm, ws, dm, w1, d1, w2, t0, t1, r0, tr0, dd, tdd, uu, up0, zz):
    gy, gz = pos[1], pos[2]
    lane = iota((R0, 128), 1)
    make_tables(wm, dm, R0, 16, lane, lane >= 0, gy * 128, gz * 128, 512, S0)
    ok = (lane < 8) | (lane >= 120)
    make_tables(ws, None, R0, 16, side_place(lane), ok, gy * 128, gz * 128, 512, S0)
    z = level1_place(iota((R1, 128), 1))
    make_tables(w1, d1, R1, 32, z, level1_ok(z), gy * 64, gz * 64, 256, S1)

    lane = iota((R2, 128), 1)
    part = jnp.bitwise_and(lane, 63)
    y, z = iota((R2, 128), 0) - 20 + gy * 32, part - 11 + gz * 32
    inside = (part < 54) & (y >= 0) & (y < 128) & (z >= 0) & (z < 128)
    count = axis_count(y, 128) + axis_count(z, 128)
    for i in range(3):
        edge = {0: lane < 64, 1: lane < 0, 2: lane >= 64}[i]
        value = 1.0 + S2 * (count + jnp.where(edge, 1.0, 2.0))
        w2[i] = jnp.where(inside, DAMPING / value, 0.0)

    src, dst = iota((256, 256), 0), iota((256, 256), 1)
    step = jnp.bitwise_and(src - dst, 255)
    t0[...] = hits((step == 1) | (step == 255)).astype(BF16)
    src, dst = iota((256, 128), 0), iota((256, 128), 1)
    step = jnp.bitwise_and(src - dst, 127)
    t1[...] = hits((step == 1) | (step == 127)).astype(BF16)

    col, good = dst, dst < 64
    z, ok = level0_place(src)
    total = jnp.zeros((256, 128), F32)
    for dz in (-1, 1):
        total = total + hits(ok & good & (z + dz >= 0) & (z + dz < 128) & (half(z + dz) == col))
    tr0[...] = (0.125 * total).astype(BF16)
    r0[...] = (0.125 * hits(good & (half(src) == col) & (src < 128)))[0:128].astype(BF16)

    src5, dst5 = iota((512, 256), 0), iota((512, 256), 1)
    slot = jnp.bitwise_and(dst5, 31)
    same = lax.shift_right_logical(src5, 7) == lax.shift_right_logical(jnp.bitwise_and(dst5, 127), 5)
    edge = src5 == jnp.bitwise_and(src5, 384) + slot + jnp.where(dst5 < 128, 0, 32)
    used = (slot >= jnp.where(dst5 < 128, 0, 10)) & (slot < jnp.where(dst5 < 128, 22, 32))
    zz[...] = hits(same & edge & used).astype(BF16)

    z = level1_place(jnp.bitwise_and(src, 127))
    part = jnp.bitwise_and(dst, 63)
    good = (part < 54) & ((src < 128) == (dst < 64))
    dd[...] = (0.125 * hits(good & level1_ok(z) & (half(z) == part - 11))).astype(BF16)
    total = jnp.zeros((256, 128), F32)
    for dz in (-1, 1):
        total = total + hits(good & level1_ok(z + dz) & (half(z + dz) == part - 11))
    tdd[...] = (0.125 * total).astype(BF16)

    src, dst = iota((128, 256), 0), iota((128, 256), 1)
    z = level1_place(jnp.bitwise_and(dst, 127))
    part = jnp.bitwise_and(src, 63)
    good = (part < 54) & ((dst < 128) == (src < 64))
    uu[...] = hits(good & level1_ok(z) & (half(z) == part - 11)).astype(BF16)
    z, ok = level0_place(dst)
    up0[...] = hits(ok & (half(z) == level1_place(src))).astype(BF16)


def two_parts(value):
    top = value.astype(BF16)
    return top, (value - top.astype(F32)).astype(BF16)


def select(value, matrix):
    top, rest = two_parts(value)
    out = jnp.dot(top, matrix, preferred_element_type=F32)
    return out + jnp.dot(rest, matrix, preferred_element_type=F32)


def level0_sweep(pos, src, dst, fm, fs, wm, ws, t0, first, last, side):
    start, size = (8, 144) if side else (16, 128)
    lane = iota((size, 128), 1)
    rows, up, dn = pl.ds(start, size), pl.ds(start - 1, size), pl.ds(start + 1, size)

    def body(p, j):
        i = x_index(pos[0] * 8 + p - 8, 64)
        m, s = src[0][p, rows], src[1][p, rows]
        if j % 2:
            near = select(jnp.concatenate([m, s], axis=1), t0[...])
            near_m, near_s = near[:, :128], near[:, 128:]
        else:
            mr, sr, ml, sl = next_lane(m), next_lane(s), prev_lane(m), prev_lane(s)
            near_m = jnp.where(lane == 127, sr, mr) + jnp.where(lane == 0, sl, ml)
            near_s = jnp.where(lane == 127, mr, sr) + jnp.where(lane == 0, ml, sl)
        tot = src[0][p - 1, rows] + src[0][p + 1, rows] + src[0][p, up] + src[0][p, dn]
        dst[0][p, rows] = KEEP * m + wm[i, rows] * (fm[p, rows] + S0 * (tot + near_m))
        if side:
            tot = src[1][p - 1, rows] + src[1][p + 1, rows] + src[1][p, up] + src[1][p, dn]
            dst[1][p, rows] = KEEP * s + ws[i, rows] * (fs[p, rows] + S0 * (tot + near_s))

    planes(first, last + 1 - first, 10, body)


def level0_restrict(pos, src, fm, dm, r0, tr0, zz, tmp, out, z_low, z_high):
    rows, up, dn = pl.ds(16, 128), pl.ds(15, 128), pl.ds(17, 128)
    values = []
    for k in range(4):
        sums = [None, None, None]
        for q in (0, 1):
            p = 8 + 2 * k + q
            i = x_index(pos[0] * 8 + p - 8, 64)
            m = src[0][p, rows]
            tot = src[0][p - 1, rows] + src[0][p + 1, rows] + src[0][p, up] + src[0][p, dn]
            parts = (fm[p, rows] + S0 * tot - dm[i, rows] * m, m, src[1][p, rows])
            sums = [v if t is None else t + v for t, v in zip(sums, parts)]
        pairs = []
        for n in range(3):
            tmp[3 * k + n, pl.ds(0, 128)] = sums[n]
            pairs.append(tmp[3 * k + n, pl.ds(0, 64, stride=2)] + tmp[3 * k + n, pl.ds(1, 64, stride=2)])
        near = select(jnp.concatenate(pairs[1:], axis=1), tr0[...])
        values.append(select(pairs[0], r0[...]) + S0 * near)
        out[k] = values[k]
    edges = select(jnp.concatenate(values, axis=1), zz[...])
    z_low[...] = edges[:, :128]
    z_high[...] = edges[:, 128:]


def level1_sweep(src, dst, f, w, t1, first, count, start=8, size=112):
    mid, up, dn = pl.ds(start, size), pl.ds(start - 1, size), pl.ds(start + 1, size)

    def body(p, j):
        i = x_index(p - 5, 32)
        m = src[p, mid]
        if j % 2:
            near = jnp.concatenate(two_parts(m), axis=1)
            near = jnp.dot(near, t1[...], preferred_element_type=F32)
        else:
            near = next_lane(m) + prev_lane(m)
        tot = src[p - 1, mid] + src[p + 1, mid] + src[p, up] + src[p, dn] + near
        dst[p, mid] = KEEP * m + w[i, mid] * (f[p, mid] + S1 * tot)

    planes(first, count, 16, body)


def level2_sweep(src, dst, f, w, start, size):
    lane = iota((size, 128), 1)
    mid, up, dn = pl.ds(start, size), pl.ds(start - 1, size), pl.ds(start + 1, size)
    for p in range(1, 9):
        m = src[p, mid]
        if p == 1:
            before = jnp.where(lane >= 64, pltpu.roll(src[8, mid], 64, 1), 0.0)
        else:
            before = src[p - 1, mid]
        if p == 8:
            after = jnp.where(lane < 64, pltpu.roll(src[1, mid], 64, 1), 0.0)
        else:
            after = src[p + 1, mid]
        tot = before + after + src[p, up] + src[p, dn] + next_lane(m) + prev_lane(m)
        dst[p, mid] = KEEP * m + w[{1: 0, 8: 2}.get(p, 1), mid] * (f[p, mid] + S2 * tot)


def coarse_levels(pos, blocks, tables, f1, va, vb, f2, a2, b2, tmp, halo):
    w1, d1, w2, t1, dd, tdd, uu = tables
    gx = pos[0]
    zero = jnp.zeros((R1, 128), F32)
    for p in list(range(0, 5)) + list(range(37, 42)):
        f1[p] = zero
        va[p] = zero
        vb[p] = zero
    for p in range(5, 37):
        for ref in (va, vb):
            ref[p, pl.ds(0, 8)] = jnp.zeros((8, 128), F32)
            ref[p, pl.ds(120, 8)] = jnp.zeros((8, 128), F32)
    for ref in (a2, b2):
        for p in range(1, 9):
            ref[p, pl.ds(0, 8)] = jnp.zeros((8, 128), F32)
            ref[p, pl.ds(64, 8)] = jnp.zeros((8, 128), F32)

    for m in range(4):
        for q in range(2):
            block = blocks[2 * m + q]
            own = gx if q == 0 else jnp.bitwise_xor(gx, 1)
            place = jnp.bitwise_and(own + 8 - 2 * (0, 1, 3, 2)[m], 7)
            for j in range(4):
                p = 5 + 4 * place + j
                i = x_index(4 * place + j, 32)
                value = block[j]
                f1[p, pl.ds(8, 112)] = value
                va[p, pl.ds(8, 112)] = w1[i, pl.ds(8, 112)] * value

    level1_sweep(va, vb, f1, w1, t1, 5, 32)

    def residual(k):
        mid = pl.ds(8, 112)
        sums = [None, None]
        for q in (0, 1):
            p = 5 + 2 * k + q
            i = x_index(p - 5, 32)
            m = vb[p, mid]
            tot = vb[p - 1, mid] + vb[p + 1, mid] + vb[p, pl.ds(7, 112)] + vb[p, pl.ds(9, 112)]
            parts = (f1[p, mid] + S1 * tot - d1[i, mid] * m, m)
            sums = [v if t is None else t + v for t, v in zip(sums, parts)]
        pairs = []
        for n in range(2):
            tmp[2 * k + n, pl.ds(0, 112)] = sums[n]
            pairs.append(tmp[2 * k + n, pl.ds(0, 56, stride=2)] + tmp[2 * k + n, pl.ds(1, 56, stride=2)])
        return pairs

    def restrict(p, j):
        low, high = residual(p - 1), residual(p + 7)
        value = select(jnp.concatenate([low[0], high[0]], axis=1), dd[...])
        value = value + S1 * select(jnp.concatenate([low[1], high[1]], axis=1), tdd[...])
        f2[p, pl.ds(8, 56)] = value
        i = jnp.where(p == 1, 0, jnp.where(p == 8, 2, 1))
        a2[p, pl.ds(8, 56)] = w2[i, pl.ds(8, 56)] * value

    planes(1, 8, 8, restrict)

    src2, dst2 = a2, b2
    for n in range(7):
        level2_sweep(src2, dst2, f2, w2, *((8, 56) if n < 5 else (16, 40)))
        src2, dst2 = dst2, src2

    def prolong(p, j):
        both = select(src2[p, pl.ds(16, 40)], uu[...])
        for n, k in ((0, p - 1), (1, p + 7)):
            e = both[:, 128 * n:128 * n + 128]
            for q in (0, 1):
                for h in (0, 1):
                    rows = pl.ds(24 + h, 40, stride=2)
                    vb[5 + 2 * k + q, rows] = vb[5 + 2 * k + q, rows] + e

    planes(1, 8, 8, prolong)
    level1_sweep(vb, va, f1, w1, t1, 4 * gx + 4 - halo, 6 + 2 * halo, 24, 80)
    level1_sweep(va, vb, f1, w1, t1, 4 * gx + 5 - halo, 4 + 2 * halo, 24, 80)


def level0_prolong(pos, e1, up0, old, new, first, last):
    def body(k, j):
        e = e1[4 * pos[0] + 1 + k, pl.ds(28, 72)]
        e = select(e, up0[...])
        for q in (0, 1):
            p = 2 * k + q
            for h in (0, 1):
                rows = pl.ds(8 + h, 72, stride=2)
                new[0][p, rows] = old[0][p, rows] + e[:, :128]
                new[1][p, rows] = old[1][p, rows] + e[:, 128:]

    planes(first // 2, last // 2 + 1 - first // 2, 10, body)


def zero_pads(refs, first, last):
    zero = jnp.zeros((8, 128), F32)
    for ref in refs:
        for p in range(first, last + 1):
            ref[p, pl.ds(0, 8)] = zero
            ref[p, pl.ds(152, 8)] = zero


def rim_kernel(u, u0, cols, rows):
    lane = iota((128, 128), 1)
    acc = jnp.zeros((128, 128), F32)
    for d in range(3):
        for x in range(8):
            k = 8 * d + x
            value = u[d, x]
            u0[9 * d + x] = value
            acc = jnp.where(lane == k, pltpu.roll(value, k, 1) if k else value, acc)
            rows[pl.ds(k, 1)] = u[d, x, pl.ds(0, 1)]
    cols[...] = acc


def form_matrix(stiff, high, low):
    r, c = iota((192, 24), 0), iota((192, 24), 1)
    wide = jnp.where(lax.shift_right_logical(r, 3) == c, 1.0, 0.0)
    r, c = iota((24, 192), 0), iota((24, 192), 1)
    tall = jnp.where(lax.shift_right_logical(c, 3) == r, 1.0, 0.0)
    full = jnp.dot(wide, stiff, precision=HIGH, preferred_element_type=F32)
    full = jnp.dot(full, tall, precision=HIGH, preferred_element_type=F32)
    r, c = iota((192, 192), 0), iota((192, 192), 1)
    full = jnp.where(jnp.bitwise_and(r, 7) == jnp.bitwise_and(c, 7), full, 0.0)
    top = full.astype(BF16)
    high[...] = top
    low[...] = (full - top.astype(F32)).astype(BF16)


def energy_group(u0, u1, high, low, rho, f, x, y, x_in, x_out, shift=0):
    cols = []
    for q in range(4):
        val = []
        for ref in (u0, u1):
            for b in (0, 1):
                for a in (0, 1):
                    for d in range(3):
                        val.append(ref[9 * d + x + a, pl.ds(y + 8 * q + b, 8)])
        cols.append(jnp.concatenate(val, axis=0))
    u = jnp.concatenate(cols, axis=1)
    top = u.astype(BF16)
    pushed = jnp.dot(high[...], top, preferred_element_type=F32)
    pushed = pushed + jnp.dot(low[...], top, preferred_element_type=F32)
    prod = pushed * (u + (u - top.astype(F32)))
    energy = prod[0:8]
    for i in range(1, 24):
        energy = energy + prod[8 * i:8 * i + 8]
    for q in range(4):
        rows = pl.ds(y + shift + 8 * q, 8)
        r = rho[x_in, rows]
        f[x_out, rows] = -3.0 * r * r * energy[:, 128 * q:128 * q + 128]


def energy_setup(stiff, u0, u1, high, low):
    form_matrix(stiff[...], high, low)
    for q in range(27):
        if q % 9 < 8:
            u1[q] = next_lane(u0[q])


def energy_first(pos, u0, bare, high, low, zrim, rho, u1, f):
    lane = iota((128, 128), 1)
    col = zrim[...] * jnp.where(pos[2] < 3, 1.0, 0.0)
    for d in range(3):
        for x in range(8):
            k, q = 8 * d + x, 9 * d + x
            u1[q] = jnp.where(lane == 127, pltpu.roll(col, 127 - k, 1), bare[q])

    def group(c, j):
        x = c // 3
        y = pl.multiple_of((c - 3 * x) * 32, 32)
        energy_group(u0, u1, high, low, rho, f, x, y, x, x)

    planes(0, 12, 4, group)


def rim_row(row, corner, k, w0, w1, q, start):
    lane = iota((8, 128), 1)
    row = jnp.broadcast_to(row, (8, 128))
    corner = jnp.broadcast_to(corner, (8, 128))
    w0[q, pl.ds(start, 8)] = row
    w1[q, pl.ds(start, 8)] = jnp.where(
        lane == 127, pltpu.roll(corner, 127 - k, 1), next_lane(row))


def energy_second(pos, u0, u1, high, low, rho, yrim, fa, f, w0, w1):
    keep_y = jnp.where(pos[1] < 3, 1.0, 0.0)
    keep_z = jnp.where(pos[2] < 3, 1.0, 0.0)
    corner = yrim[pl.ds(24, 1)] * (keep_y * keep_z)
    for d in range(3):
        for x in range(8):
            k, q = 8 * d + x, 9 * d + x
            w0[q, pl.ds(0, 32)] = u0[q, pl.ds(96, 32)]
            w1[q, pl.ds(0, 32)] = u1[q, pl.ds(96, 32)]
            rim_row(yrim[pl.ds(k, 1)] * keep_y, corner, k, w0, w1, q, 32)
    for x in range(4):
        f[x, pl.ds(0, 96)] = fa[x, pl.ds(0, 96)]

    def group(c, j):
        x = c // 3
        y = pl.multiple_of((c - 3 * x) * 32, 32)
        energy_group(u0, u1, high, low, rho, f, x + 4, y, x + 4, x + 4)

    planes(0, 9, 3, group)
    for x in range(7):
        energy_group(w0, w1, high, low, rho, f, x, 0, x, x, 96)


def energy_last(pos, u0, u1, high, low, rho, xface, yrim, zrim, xrim, fb,
                f, lead, tail, pack, w0, w1):
    keep_x = jnp.where(pos[0] < 7, 1.0, 0.0)
    keep_y = jnp.where(pos[1] < 3, 1.0, 0.0)
    keep_z = jnp.where(pos[2] < 3, 1.0, 0.0)
    lane = iota((128, 128), 1)
    col = xrim[pl.ds(32, 128)] * (keep_x * keep_z)
    for d in range(3):
        k, q = 8 * d + 7, 9 * d
        w0[q, pl.ds(0, 128)] = u0[9 * d + 7]
        w1[q, pl.ds(0, 128)] = u1[9 * d + 7]
        corner = yrim[pl.ds(24, 1)] * (keep_y * keep_z)
        rim_row(yrim[pl.ds(k, 1)] * keep_y, corner, k, w0, w1, q, 128)
        k, q = 8 * d, 9 * d + 1
        body = xface[d] * keep_x
        w0[q, pl.ds(0, 128)] = body
        w1[q, pl.ds(0, 128)] = jnp.where(
            lane == 127, pltpu.roll(col, 127 - k, 1), next_lane(body))
        corner = xrim[pl.ds(24, 1)] * (keep_x * keep_y * keep_z)
        rim_row(xrim[pl.ds(k, 1)] * (keep_x * keep_y), corner, k, w0, w1, q, 128)
    for x in range(7):
        f[x] = fb[x]
    for q in range(4):
        energy_group(w0, w1, high, low, rho, f, 0, 32 * q, 7, 7)
    acc = jnp.zeros((128, 128), F32)
    for x in range(8):
        value = f[x]
        if x < 7:
            lead[x] = value
        if x > 0:
            tail[x - 1] = value
        here = (lane >= 16 * x) & (lane < 16 * x + 16)
        acc = jnp.where(here, pltpu.roll(value, (16 * x + 8) % 128, 1), acc)
    pack[...] = acc


def spread(value, x):
    return pltpu.roll(value, (248 - 16 * x) % 128, 1)


def lay_out(pos, blk, halo, base, first, last, skip, wm, ws, fm, fs, am, as_):
    for p in range(first, last + 1):
        x = p - base
        i = x_index(pos[0] * 8 + p - 8, 64)
        parts = (
            (8, 8, halo[pl.ds(8 * x, 8)], spread(halo[pl.ds(64, 8)], x)),
            (16, 128, blk[x - skip], spread(halo[pl.ds(144, 128)], x)),
            (144, 8, halo[pl.ds(72 + 8 * x, 8)], spread(halo[pl.ds(136, 8)], x)),
        )
        for start, size, main, side in parts:
            rows = pl.ds(start, size)
            fm[p, rows] = main
            fs[p, rows] = side
            am[p, rows] = wm[i, rows] * main
            as_[p, rows] = ws[i, rows] * side


def own_kernel(pos, fc, hc, wm, ws, fm, fs, am, as_):
    zero_pads((fm, fs, am, as_), 1, 22)
    lay_out(pos, fc, hc, 8, 8, 15, 0, wm, ws, fm, fs, am, as_)


def first_kernel(pos, fl, fr, hl, hr, wm, ws, dm, t0, r0, tr0, zz, *refs):
    fm, fs, am, as_, vm, vs, out, z_low, z_high, tmp = refs[4:]
    lay_out(pos, fl, hl, 0, 6, 7, 1, wm, ws, fm, fs, am, as_)
    lay_out(pos, fr, hr, 16, 16, 17, 0, wm, ws, fm, fs, am, as_)
    zero_pads((vm, vs), 7, 16)
    level0_sweep(pos, (am, as_), (vm, vs), fm, fs, wm, ws, t0, 7, 16, True)
    level0_restrict(pos, (vm, vs), fm, dm, r0, tr0, zz, tmp, out, z_low, z_high)


def outer_kernel(pos, fl, fr, hl, hr, wm, ws, t0, *refs):
    fm, fs, am, as_, vm, vs = refs[6:]
    lay_out(pos, fl, hl, 0, 1, 5, 1, wm, ws, fm, fs, am, as_)
    lay_out(pos, fr, hr, 16, 18, 22, 0, wm, ws, fm, fs, am, as_)
    zero_pads((vm, vs), 2, 6)
    zero_pads((vm, vs), 17, 21)
    level0_sweep(pos, (am, as_), (vm, vs), fm, fs, wm, ws, t0, 2, 6, True)
    level0_sweep(pos, (am, as_), (vm, vs), fm, fs, wm, ws, t0, 17, 21, True)


def middle_kernel(pos, *refs):
    blocks, tables = refs[:8], refs[8:15]
    up0, wm, ws, dm, t0, r0, tr0, zz, fm, fs, vm, vs = refs[15:27]
    om, os_, out, z_low, z_high, am, as_, bm, bs, f1, va, vb, f2, a2, b2, tmp = refs[27:]
    zero_pads((am, as_, bm, bs, om, os_), 2, 21)
    coarse_levels(pos, blocks, tables, f1, va, vb, f2, a2, b2, tmp, 3)
    level0_prolong(pos, vb, up0, (vm, vs), (am, as_), 2, 21)
    level0_sweep(pos, (am, as_), (bm, bs), fm, fs, wm, ws, t0, 3, 20, True)
    level0_sweep(pos, (bm, bs), (am, as_), fm, fs, wm, ws, t0, 4, 19, True)
    level0_sweep(pos, (am, as_), (bm, bs), fm, fs, wm, ws, t0, 5, 18, True)
    level0_sweep(pos, (bm, bs), (om, os_), fm, fs, wm, ws, t0, 6, 17, True)
    level0_restrict(pos, (om, os_), fm, dm, r0, tr0, zz, tmp, out, z_low, z_high)


def last_kernel(pos, *refs):
    blocks, tables = refs[:8], refs[8:15]
    up0, wm, ws, t0, fm, fs, vm, vs, out = refs[15:24]
    am, as_, bm, bs, f1, va, vb, f2, a2, b2, tmp = refs[24:]
    zero_pads((am, as_, bm, bs), 6, 17)
    coarse_levels(pos, blocks, tables, f1, va, vb, f2, a2, b2, tmp, 1)
    level0_prolong(pos, vb, up0, (vm, vs), (am, as_), 6, 17)
    level0_sweep(pos, (am, as_), (bm, bs), fm, fs, wm, ws, t0, 7, 16, True)
    level0_sweep(pos, (bm, bs), (am, as_), fm, fs, wm, ws, t0, 8, 15, False)
    for x in range(8):
        out[x] = am[8 + x, pl.ds(16, 128)]


SMEM = pl.BlockSpec(memory_space=pltpu.SMEM)
VM = pl.BlockSpec(memory_space=pltpu.VMEM)


def shape(*dims):
    return jax.ShapeDtypeStruct(dims, F32)


def half_shape(*dims):
    return jax.ShapeDtypeStruct(dims, BF16)


def vmem(*dims):
    return pltpu.VMEM(dims, F32)


def call(kernel, outs, scratch, scalars, args, name, limit=12, in_place=None):
    specs = [SMEM] * scalars + [VM] * (len(args) - scalars)
    return pl.pallas_call(
        kernel,
        out_shape=outs,
        in_specs=specs,
        out_specs=[VM] * len(outs),
        scratch_shapes=scratch,
        input_output_aliases=in_place or {},
        compiler_params=pltpu.CompilerParams(vmem_limit_bytes=limit << 20),
        name=name,
    )(*args)


def shifted(value, axis, step):
    size = lax.axis_size(axis)
    return lax.ppermute(value, axis, [(i, (i + step) % size) for i in range(size)])


def swapped(value):
    return lax.ppermute(value, "gx", [(i, i ^ 1) for i in range(lax.axis_size("gx"))])


COARSE_SCRATCH = [
    vmem(PL1, R1, 128), vmem(PL1, R1, 128), vmem(PL1, R1, 128),
    vmem(10, R2, 128), vmem(10, R2, 128), vmem(10, R2, 128), vmem(32, 136, 128),
]
WIDE = vmem(PL0, R0, 128)


def extend_level1(own, z_low, z_high):
    lane = lax.broadcasted_iota(jnp.int32, (64, 128), 1)
    right, left = shifted(z_low, "gz", -1), shifted(z_high, "gz", 1)
    wide = []
    for k in range(4):
        rim = jnp.where(lane < 96, jnp.roll(right, 64 - 32 * k, 1), jnp.roll(left, 96 - 32 * k, 1))
        wide.append(jnp.where(lane < 64, own[k], rim))
    own = jnp.stack(wide)
    low, high = shifted(own[:, 40:], "gy", 1), shifted(own[:, :24], "gy", -1)
    return jnp.concatenate([low, own, high], axis=1)


def gather_level1(own, meanwhile):
    parts = [own] + [shifted(own, "gx", 2 * m) for m in (1, 3, 2)]
    if meanwhile:
        parts[3], meanwhile = lax.optimization_barrier((parts[3], meanwhile))
    return [v for part in parts for v in (part, swapped(part))], meanwhile


def per_device(u, rho, stiff):
    pos = jnp.stack([lax.axis_index(a) for a in ("gx", "gy", "gz")]).astype(jnp.int32)
    t = shape(3, R0, 128)
    wm, ws, dm, w1, d1, w2, t0, t1, r0, tr0, dd, tdd, uu, up0, zz = call(
        setup_kernel,
        [t, t, t, shape(3, R1, 128), shape(3, R1, 128), shape(3, R2, 128),
         half_shape(256, 256), half_shape(256, 128), half_shape(128, 128), half_shape(256, 128),
         half_shape(256, 128), half_shape(256, 128), half_shape(128, 256), half_shape(128, 256),
         half_shape(512, 256)],
        [], 1, [pos], "setup")
    u0, cols, rows = call(
        rim_kernel, [shape(27, 128, 128), shape(128, 128), shape(24, 128)], [], 0, [u], "rims")
    xface = shifted(u[:, 0], "gx", -1)
    zrim = shifted(cols, "gz", -1)
    mat = half_shape(192, 192)
    bare, high, low = call(
        energy_setup, [shape(27, 128, 128), mat, mat], [], 0, [stiff, u0], "energy_setup")
    zrim, bare = lax.optimization_barrier((zrim, bare))
    yrim = shifted(jnp.concatenate([rows, zrim[:8]], axis=0), "gy", -1)
    u1, fa = call(
        energy_first, [shape(27, 128, 128), shape(4, 128, 128)],
        [], 1, [pos, u0, bare, high, low, zrim, rho], "energy_first")
    yrim, fa = lax.optimization_barrier((yrim, fa))
    xrim = shifted(jnp.concatenate([yrim, zrim], axis=0), "gx", -1)
    (fb,) = call(
        energy_second, [shape(7, 128, 128)], [vmem(27, 40, 128), vmem(27, 40, 128)], 1,
        [pos, u0, u1, high, low, rho, yrim, fa], "energy_second")
    f, lead, tail, pack = call(
        energy_last, [shape(8, 128, 128), shape(7, 128, 128), shape(7, 128, 128), shape(128, 128)],
        [vmem(27, 136, 128), vmem(27, 136, 128)], 1,
        [pos, u0, u1, high, low, rho, xface, yrim, zrim, xrim, fb], "energy_last")

    fl, fr = shifted(tail, "gx", 1), shifted(lead, "gx", -1)
    lane = lax.broadcasted_iota(jnp.int32, pack.shape, 1)
    from_left = jnp.bitwise_and(lane, 15) < 8
    z = jnp.where(from_left, shifted(pack, "gz", 1), shifted(pack, "gz", -1))
    up = jnp.concatenate([f[:, 120:].reshape(64, 128), z[120:]], axis=0)
    down = jnp.concatenate([f[:, :8].reshape(64, 128), z[:8]], axis=0)
    h = jnp.concatenate([shifted(up, "gy", 1), shifted(down, "gy", -1), z], axis=0)
    wide = shape(PL0, R0, 128)
    level1 = [shape(4, 64, 128), shape(64, 128), shape(64, 128)]
    state = call(own_kernel, [wide] * 4, [], 1, [pos, f, h, wm, ws], "own")
    hl, hr = shifted(h, "gx", 1), shifted(h, "gx", -1)
    *state, vm, vs, f1, z_low, z_high = call(
        first_kernel, [wide] * 6 + level1, [vmem(12, 136, 128)], 1,
        [pos, fl, fr, hl, hr, wm, ws, dm, t0, r0, tr0, zz, *state], "first",
        in_place={12 + n: n for n in range(4)})
    own = extend_level1(f1, z_low, z_high)
    own, hl = lax.optimization_barrier((own, hl))
    fm, fs, _, _, vm, vs = call(
        outer_kernel, [wide] * 6, [], 1,
        [pos, fl, fr, hl, hr, wm, ws, t0, *state, vm, vs], "outer",
        in_place={8 + n: n for n in range(6)})
    blocks, (fm, fs, vm, vs) = gather_level1(own, (fm, fs, vm, vs))
    tables = [w1, d1, w2, t1, dd, tdd, uu, up0]
    vm, vs, *f1 = call(
        middle_kernel, [wide, wide, *level1], [WIDE] * 4 + COARSE_SCRATCH, 1,
        [pos, *blocks, *tables, wm, ws, dm, t0, r0, tr0, zz, fm, fs, vm, vs], "middle", 24)
    blocks, _ = gather_level1(extend_level1(*f1), ())
    (out,) = call(
        last_kernel, [shape(8, 128, 128)], [WIDE] * 4 + COARSE_SCRATCH, 1,
        [pos, *blocks, *tables, wm, ws, t0, fm, fs, vm, vs], "last", 24)
    return out


def solution(mesh):
    return jax.shard_map(
        per_device,
        mesh=mesh,
        in_specs=(P(None, "gx", "gy", "gz"), P("gx", "gy", "gz"), P()),
        out_specs=P("gx", "gy", "gz"),
        check_vma=False,
    )
```
